32 devices in a mesh: rows: 4 (over x, core), tp: 8 (over z, y).
Axes of the slice: x: 2, y: 2, z: 4, core: 2. Of those that a mesh axis runs over, the one named last changes fastest.
Arguments:
- tokens: bfloat16 [8192, 1024], P('rows'), may hold values from -6 to 6
- time_embed: bfloat16 [8, 1024], P('rows'), may hold values from -3 to 3
- segment_ids: int32 [8, 1024], P('rows'), may hold values from 0 to 5, never falling along the last dimension, each value on 1 to 512 neighbouring positions
- cotangent: bfloat16 [8192, 1024], P('rows'), may hold values from -6 to 6
- input_weight: float32 [1024, 3072], P('rows', 'tp'), may hold values from -0.1875 to 0.1875
- input_moment: float32 [1024, 3072], P('rows', 'tp'), may hold values from -0.00018310547 to 0.00018310547
- input_square: float32 [1024, 3072], P('rows', 'tp'), may hold values from 1.9888103e-11 to 1.2728386e-09
- output_weight: float32 [1024, 1024], P('rows', 'tp'), may hold values from -1 to 1
- output_moment: float32 [1024, 1024], P('rows', 'tp'), may hold values from -0.00018310547 to 0.00018310547
- output_square: float32 [1024, 1024], P('rows', 'tp'), may hold values from 1.9888103e-11 to 1.2728386e-09
- upward_weight: float32 [1024, 4096], P('rows', 'tp'), may hold values from -0.1875 to 0.1875
- upward_moment: float32 [1024, 4096], P('rows', 'tp'), may hold values from -0.00018310547 to 0.00018310547
- upward_square: float32 [1024, 4096], P('rows', 'tp'), may hold values from 1.9888103e-11 to 1.2728386e-09
- downward_weight: float32 [1024, 4096], P('rows', 'tp'), may hold values from -0.09375 to 0.09375
- downward_moment: float32 [1024, 4096], P('rows', 'tp'), may hold values from -0.00018310547 to 0.00018310547
- downward_square: float32 [1024, 4096], P('rows', 'tp'), may hold values from 1.9888103e-11 to 1.2728386e-09
- head_bias: float32 [128, 16], P('rows', 'tp'), may hold values from -1.75 to 1.75
- head_moment: float32 [128, 16], P('rows', 'tp'), may hold values from -0.00018310547 to 0.00018310547
- head_square: float32 [128, 16], P('rows', 'tp'), may hold values from 1.9888103e-11 to 1.2728386e-09
- hidden_bias: float32 [128, 32], P('rows', 'tp'), may hold values from -1.75 to 1.75
- hidden_moment: float32 [128, 32], P('rows', 'tp'), may hold values from -0.00018310547 to 0.00018310547
- hidden_square: float32 [128, 32], P('rows', 'tp'), may hold values from 1.9888103e-11 to 1.2728386e-09
- norm_gains: float32 [1024, 2], P('rows'), may hold values from 0.5 to 1.5
- gains_moment: float32 [1024, 2], P('rows'), may hold values from -0.00018310547 to 0.00018310547
- gains_square: float32 [1024, 2], P('rows'), may hold values from 1.9888103e-11 to 1.2728386e-09
- branch_biases: float32 [1024, 4], P('rows'), may hold values from -1.75 to 1.75
- biases_moment: float32 [1024, 4], P('rows'), may hold values from -0.00018310547 to 0.00018310547
- biases_square: float32 [1024, 4], P('rows'), may hold values from 1.9888103e-11 to 1.2728386e-09
Outputs:
- block_output: bfloat16 [8192, 1024], P('rows')
- input_grad: float32 [8192, 1024], P('rows')
- grad_norm: float32 [1], replicated
- input_weight_new: float32 [1024, 3072], P('rows', 'tp')
- input_moment_new: float32 [1024, 3072], P('rows', 'tp')
- input_square_new: float32 [1024, 3072], P('rows', 'tp')
- output_weight_new: float32 [1024, 1024], P('rows', 'tp')
- output_moment_new: float32 [1024, 1024], P('rows', 'tp')
- output_square_new: float32 [1024, 1024], P('rows', 'tp')
- upward_weight_new: float32 [1024, 4096], P('rows', 'tp')
- upward_moment_new: float32 [1024, 4096], P('rows', 'tp')
- upward_square_new: float32 [1024, 4096], P('rows', 'tp')
- downward_weight_new: float32 [1024, 4096], P('rows', 'tp')
- downward_moment_new: float32 [1024, 4096], P('rows', 'tp')
- downward_square_new: float32 [1024, 4096], P('rows', 'tp')
- head_bias_new: float32 [128, 16], P('rows', 'tp')
- head_moment_new: float32 [128, 16], P('rows', 'tp')
- head_square_new: float32 [128, 16], P('rows', 'tp')
- hidden_bias_new: float32 [128, 32], P('rows', 'tp')
- hidden_moment_new: float32 [128, 32], P('rows', 'tp')
- hidden_square_new: float32 [128, 32], P('rows', 'tp')
- norm_gains_new: float32 [1024, 2], P('rows')
- gains_moment_new: float32 [1024, 2], P('rows')
- gains_square_new: float32 [1024, 2], P('rows')
- branch_biases_new: float32 [1024, 4], P('rows')
- biases_moment_new: float32 [1024, 4], P('rows')
- biases_square_new: float32 [1024, 4], P('rows')
The draws below stay inside these ranges and needn't reach their ends.
Inputs may be any that keep to these rules, and one draw needn't show every extreme that they name: `segment_ids`: in each sequence the numbers never fall, and each document holds at most 512 tokens.
All inputs are finite; a program needn't handle non-finite values.
Results may differ from the reference program's by a relative error of at most 0.01.
The reference program's roundings to bfloat16 on the way count: a program that leaves them out, or rounds other values in their place, can miss the bound.
Values may be sent and summed in bfloat16 or wider, within the bound.
A program may use at most 192 MiB of HBM per device.

```python
import math
from functools import reduce
import jax
import jax.numpy as jnp
import numpy as np
from jax import lax

D = 1024
HEADS = 16
HD = 64
FF = 4096
LENGTH = 1024
STEP = 10
SEQS = 8
TOKENS = 8192
PARAMS = 12582912


def levels(own_key, dims, cuts, low, largest):
    loudness = 1.0
    for axis_at, blocks in cuts:
        steps = jax.random.uniform(jax.random.fold_in(jax.random.fold_in(own_key, 6), axis_at), (blocks,), jnp.float32, low / len(cuts), largest / len(cuts))
        loudness = loudness * jnp.repeat(jnp.exp(steps), dims[axis_at] // blocks).reshape((-1,) + (1,) * (len(dims) - 1 - axis_at))
    return loudness


def profile(number_of, total, limit, slope):
    loads = [(1 << 20) // math.isqrt(standing ** slope) + 1 for standing in range(2, number_of + 1)]
    spare, counts = total - limit - (number_of - 1), [1] * (number_of - 1)
    while spare > 0:
        movable = [i for i in range(number_of - 1) if counts[i] < limit]
        whole, remaining = sum([loads[i] for i in movable]), spare
        for i in movable:
            more = min(limit - counts[i], max(1, remaining * loads[i] // whole), spare)
            counts[i] = counts[i] + more
            spare = spare - more
    return np.array([limit] + counts)


def uneven_parts(stream_key, amount, total, most, slope):
    if amount == 2:
        one = jax.random.randint(stream_key, (), max(1, total - most), min(most, total - 1) + 1)
        return jnp.stack([one, total - one])
    lengths = jnp.asarray(profile(amount, total, most, slope), jnp.int32)
    couples = (amount - 1) // 2
    source_of, receiver = lengths[1:1 + 2 * couples:2], lengths[2:2 + 2 * couples:2]
    slack = jnp.minimum(source_of - 1, most - receiver)
    shifted = jax.random.randint(jax.random.fold_in(stream_key, 1), (couples,), 0, 1 << 20) % (slack + 1)
    lengths = lengths.at[1:1 + 2 * couples:2].set(source_of - shifted).at[2:2 + 2 * couples:2].set(receiver + shifted)
    return lengths[jax.random.permutation(jax.random.fold_in(stream_key, 2), amount)]


def normal_values(own_key, extent, width, bound, shards=(), kind=jnp.bfloat16):
    values = jax.random.normal(own_key, extent, jnp.float32) * width
    if len(shards) > 0:
        values = levels(own_key, extent, shards, -0.22, 0.18) * values
    return jnp.clip(values, min=-bound, max=bound).astype(kind)


def setup_inputs(seed: int = 0) -> dict:
    splits = jax.random.split(jax.random.key(seed), 29)
    tokens = normal_values(splits[0], (TOKENS, D), 1.0, 6.0, ((0, 4),))
    time_embed = normal_values(splits[1], (SEQS, D), 0.5, 3.0, ((0, 4),))
    segment_ids = jax.vmap(lambda own: jnp.searchsorted(jnp.cumsum(uneven_parts(own, 6, LENGTH, LENGTH // 2, 0)), jnp.arange(LENGTH), side="right"))(jax.random.split(splits[2], SEQS)).reshape((SEQS, LENGTH)).astype(jnp.int32)
    cotangent = normal_values(splits[3], (TOKENS, D), 1.0, 6.0, ((0, 4),))
    input_weight = normal_values(splits[4], (D, 3 * D), D ** -0.5, 0.1875, ((0, 4), (1, 8)), jnp.float32)
    input_moment = normal_values(splits[5], (D, 3 * D), (0.1111 / PARAMS ** 0.5), 0.00018310547, ((0, 4), (1, 8)), jnp.float32)
    input_square = jnp.clip(jnp.exp(math.log(1.2728386122873303e-09) - 4.158883 * jax.random.uniform(splits[6], (D, 3 * D), jnp.float32) ** levels(splits[6], (D, 3 * D), ((0, 4), (1, 8)), -0.2, 0.2)), 1.9888103316989536e-11, 1.2728386122873303e-09)
    output_weight = normal_values(splits[7], (D, D), (D // 32) ** -0.5, 1.0, ((0, 4), (1, 8)), jnp.float32)
    output_moment = normal_values(splits[8], (D, D), (0.1111 / PARAMS ** 0.5), 0.00018310547, ((0, 4), (1, 8)), jnp.float32)
    output_square = jnp.clip(jnp.exp(math.log(1.2728386122873303e-09) - 4.158883 * jax.random.uniform(splits[9], (D, D), jnp.float32) ** levels(splits[9], (D, D), ((0, 4), (1, 8)), -0.2, 0.2)), 1.9888103316989536e-11, 1.2728386122873303e-09)
    upward_weight = normal_values(splits[10], (D, FF), D ** -0.5, 0.1875, ((0, 4), (1, 8)), jnp.float32)
    upward_moment = normal_values(splits[11], (D, FF), (0.1111 / PARAMS ** 0.5), 0.00018310547, ((0, 4), (1, 8)), jnp.float32)
    upward_square = jnp.clip(jnp.exp(math.log(1.2728386122873303e-09) - 4.158883 * jax.random.uniform(splits[12], (D, FF), jnp.float32) ** levels(splits[12], (D, FF), ((0, 4), (1, 8)), -0.2, 0.2)), 1.9888103316989536e-11, 1.2728386122873303e-09)
    downward_weight = normal_values(splits[13], (D, FF), FF ** -0.5, 0.09375, ((0, 4), (1, 8)), jnp.float32)
    downward_moment = normal_values(splits[14], (D, FF), (0.1111 / PARAMS ** 0.5), 0.00018310547, ((0, 4), (1, 8)), jnp.float32)
    downward_square = jnp.clip(jnp.exp(math.log(1.2728386122873303e-09) - 4.158883 * jax.random.uniform(splits[15], (D, FF), jnp.float32) ** levels(splits[15], (D, FF), ((0, 4), (1, 8)), -0.2, 0.2)), 1.9888103316989536e-11, 1.2728386122873303e-09)
    head_bias = normal_values(splits[16], (2 * HD, HEADS), 0.3, 1.75, ((0, 4), (1, 8)), jnp.float32)
    head_moment = normal_values(splits[17], (2 * HD, HEADS), (0.1111 / PARAMS ** 0.5), 0.00018310547, ((0, 4), (1, 8)), jnp.float32)
    head_square = jnp.clip(jnp.exp(math.log(1.2728386122873303e-09) - 4.158883 * jax.random.uniform(splits[18], (2 * HD, HEADS), jnp.float32) ** levels(splits[18], (2 * HD, HEADS), ((0, 4), (1, 8)), -0.2, 0.2)), 1.9888103316989536e-11, 1.2728386122873303e-09)
    hidden_bias = normal_values(splits[19], (2 * HD, FF // (2 * HD)), 0.3, 1.75, ((0, 4), (1, 8)), jnp.float32)
    hidden_moment = normal_values(splits[20], (2 * HD, FF // (2 * HD)), (0.1111 / PARAMS ** 0.5), 0.00018310547, ((0, 4), (1, 8)), jnp.float32)
    hidden_square = jnp.clip(jnp.exp(math.log(1.2728386122873303e-09) - 4.158883 * jax.random.uniform(splits[21], (2 * HD, FF // (2 * HD)), jnp.float32) ** levels(splits[21], (2 * HD, FF // (2 * HD)), ((0, 4), (1, 8)), -0.2, 0.2)), 1.9888103316989536e-11, 1.2728386122873303e-09)
    norm_gains = jnp.clip(1.0 + 0.1 * jax.random.normal(splits[22], (D, 2), jnp.float32), 0.5, 1.5)
    gains_moment = normal_values(splits[23], (D, 2), (0.1111 / PARAMS ** 0.5), 0.00018310547, ((0, 4),), jnp.float32)
    gains_square = jnp.clip(jnp.exp(math.log(1.2728386122873303e-09) - 4.158883 * jax.random.uniform(splits[24], (D, 2), jnp.float32) ** levels(splits[24], (D, 2), ((0, 4),), -0.2, 0.2)), 1.9888103316989536e-11, 1.2728386122873303e-09)
    branch_biases = normal_values(splits[25], (D, 4), 0.3, 1.75, ((0, 4),), jnp.float32)
    biases_moment = normal_values(splits[26], (D, 4), (0.1111 / PARAMS ** 0.5), 0.00018310547, ((0, 4),), jnp.float32)
    biases_square = jnp.clip(jnp.exp(math.log(1.2728386122873303e-09) - 4.158883 * jax.random.uniform(splits[27], (D, 4), jnp.float32) ** levels(splits[27], (D, 4), ((0, 4),), -0.2, 0.2)), 1.9888103316989536e-11, 1.2728386122873303e-09)
    return dict(tokens=tokens, time_embed=time_embed, segment_ids=segment_ids, cotangent=cotangent, input_weight=input_weight, input_moment=input_moment, input_square=input_square, output_weight=output_weight, output_moment=output_moment, output_square=output_square, upward_weight=upward_weight, upward_moment=upward_moment, upward_square=upward_square, downward_weight=downward_weight, downward_moment=downward_moment, downward_square=downward_square, head_bias=head_bias, head_moment=head_moment, head_square=head_square, hidden_bias=hidden_bias, hidden_moment=hidden_moment, hidden_square=hidden_square, norm_gains=norm_gains, gains_moment=gains_moment, gains_square=gains_square, branch_biases=branch_biases, biases_moment=biases_moment, biases_square=biases_square)


@jax.custom_vjp
def low(v):
    return lax.optimization_barrier(v.astype(jnp.bfloat16)).astype(jnp.float32)

@jax.custom_vjp
def low_back(v):
    return v

def low_keep(v):
    return (low(v), None)

def low_pass(kept, grad):
    return (grad,)

def back_keep(v):
    return (v, None)

def back_low(kept, grad):
    return (low(grad),)
low.defvjp(low_keep, low_pass)
low_back.defvjp(back_keep, back_low)
NORM_EPS = 1e-05
BETA_ONE = 0.9
BETA_TWO = 0.999
ADAM_EPS = 1e-08
CLIP = 1.0
RATES = (0.1, 0.4, 0.1, 0.05, 0.5, 0.5, 0.5, 0.5)
DECAYS = (0.01, 0.01, 0.01, 0.01, 0.0, 0.0, 0.0, 0.0)
HIGH = lax.Precision.HIGHEST

def gelu_value(inputs):
    return 0.5 * inputs * (1.0 + jax.scipy.special.erf(inputs * 0.7071067811865476))

def layer_norm(summed, scaling, offset):
    average = lax.optimization_barrier(jnp.mean(summed, axis=-1, keepdims=True))
    centered = summed - average
    inverse = lax.rsqrt(lax.optimization_barrier(jnp.mean(centered * centered, axis=-1, keepdims=True)) + NORM_EPS)
    return centered * inverse * scaling + offset

def attend(pieces):
    queries, key_rows, values, segments = pieces
    scores = low_back(jnp.einsum('qhd,khd->hqk', queries, key_rows, precision=HIGH) * HD ** (-0.5))
    matching = segments[:, None] == segments[None, :]
    scores = jnp.where(matching[None], scores, -1e+30)
    highest = lax.optimization_barrier(jnp.max(scores, axis=-1, keepdims=True))
    exponent = jnp.exp(scores - highest)
    probability = exponent / lax.optimization_barrier(jnp.sum(exponent, axis=-1, keepdims=True))
    return jnp.einsum('hqk,khd->qhd', low(probability), values, precision=HIGH)

def forward(params, flat_tokens, times, segments):
    weights_in, weights_out, weights_up, weights_down, head_shift, unit_shift, gains, shifts = [low(member) for member in params]
    seq_count, length = segments.shape
    embedded = (flat_tokens.reshape(seq_count, length, D) + times[:, None, :]).reshape(seq_count * length, D)
    projected = jnp.dot(low(embedded), weights_in, precision=HIGH).reshape(seq_count * length, HEADS, 3, HD)
    offset = jnp.stack([head_shift[:HD].T, jnp.zeros((HEADS, HD), jnp.float32), head_shift[HD:].T], axis=1)
    projected = low(low_back(projected + offset)).reshape(seq_count, length, HEADS, 3, HD)
    context = lax.map(jax.checkpoint(attend), (projected[:, :, :, 0], projected[:, :, :, 1], projected[:, :, :, 2], segments))
    context = low(low_back(context.reshape(seq_count * length, D)))
    mixed = low_back(jnp.dot(context, weights_out.T, precision=HIGH))
    hidden = layer_norm(embedded + mixed + shifts[:, 0], gains[:, 0], shifts[:, 1])
    pre_act = low_back(jnp.dot(low(hidden), weights_up, precision=HIGH) + unit_shift.T.reshape(FF))
    expanded = low(gelu_value(pre_act))
    reduced = low_back(jnp.dot(expanded, weights_down.T, precision=HIGH))
    return layer_norm(hidden + reduced + shifts[:, 2], gains[:, 1], shifts[:, 3])

def adam_update(weight, moment, square, clipped, rate, decay):
    moment = BETA_ONE * moment + (1.0 - BETA_ONE) * clipped
    square = BETA_TWO * square + (1.0 - BETA_TWO) * clipped * clipped
    corrected = moment / (1.0 - BETA_ONE ** STEP) / (jnp.sqrt(square / (1.0 - BETA_TWO ** STEP)) + ADAM_EPS)
    return (weight - rate * (corrected + decay * weight), moment, square)

def reference(tokens, time_embed, segment_ids, cotangent, input_weight, input_moment, input_square, output_weight, output_moment, output_square, upward_weight, upward_moment, upward_square, downward_weight, downward_moment, downward_square, head_bias, head_moment, head_square, hidden_bias, hidden_moment, hidden_square, norm_gains, gains_moment, gains_square, branch_biases, biases_moment, biases_square):
    params = (input_weight, output_weight, upward_weight, downward_weight, head_bias, hidden_bias, norm_gains, branch_biases)
    moments = (input_moment, output_moment, upward_moment, downward_moment, head_moment, hidden_moment, gains_moment, biases_moment)
    squares = (input_square, output_square, upward_square, downward_square, head_square, hidden_square, gains_square, biases_square)
    seq_total, length = segment_ids.shape
    group_size = math.gcd(seq_total, max(1, 4096 // length))
    turn_count = seq_total // group_size
    token_blocks = tokens.astype(jnp.float32).reshape(turn_count, group_size * length, D)
    time_blocks = time_embed.astype(jnp.float32).reshape(turn_count, group_size, D)
    segment_blocks = segment_ids.reshape(turn_count, group_size, length)
    back_blocks = cotangent.astype(jnp.float32).reshape(turn_count, group_size * length, D)

    def one_turn(totals, pieces):
        token_rows, time_rows, segment_rows, back_rows = pieces

        def local_forward(weights, inputs):
            return forward(weights, inputs, time_rows, segment_rows)
        result, pullback = jax.vjp(local_forward, params, token_rows)
        gradients, token_grad = pullback(back_rows)
        return (jax.tree.map(jnp.add, totals, gradients), (result.astype(jnp.bfloat16), token_grad))
    initial = jax.tree.map(jnp.zeros_like, params)
    gradients, (results, token_grads) = lax.scan(one_turn, initial, (token_blocks, time_blocks, segment_blocks, back_blocks))
    squared = reduce(jnp.add, [jnp.sum(member * member) for member in gradients])
    grad_norm = jnp.sqrt(squared)
    factor = CLIP / jnp.maximum(grad_norm, CLIP)
    updated = [adam_update(params[position], moments[position], squares[position], gradients[position] * factor, RATES[position], DECAYS[position]) for position in range(8)]
    return (results.reshape(seq_total * length, D), token_grads.reshape(seq_total * length, D), grad_norm.reshape(1), updated[0][0], updated[0][1], updated[0][2], updated[1][0], updated[1][1], updated[1][2], updated[2][0], updated[2][1], updated[2][2], updated[3][0], updated[3][1], updated[3][2], updated[4][0], updated[4][1], updated[4][2], updated[5][0], updated[5][1], updated[5][2], updated[6][0], updated[6][1], updated[6][2], updated[7][0], updated[7][1], updated[7][2])
```

```python
from functools import partial, reduce

import jax
import jax.numpy as jnp
from jax import lax
from jax.experimental import pallas as pl
from jax.experimental.pallas import tpu as pltpu
from jax.sharding import Mesh
from jax.sharding import PartitionSpec as P

HD = 64
STEP = 10


NORM_EPS = 1e-05
BETA_ONE = 0.9
BETA_TWO = 0.999
ADAM_EPS = 1e-08
CLIP = 1.0
RATES = (0.1, 0.4, 0.1, 0.05, 0.5, 0.5, 0.5, 0.5)
DECAYS = (0.01, 0.01, 0.01, 0.01, 0.0, 0.0, 0.0, 0.0)
ROW_PAIR = (((1,), (1,)), ((), ()))
COL_PAIR = (((0,), (0,)), ((), ()))


def norm_stats(summed):
    average = jnp.mean(summed, axis=-1, keepdims=True)
    centered = summed - average
    inverse = lax.rsqrt(jnp.mean(centered * centered, axis=-1, keepdims=True) + NORM_EPS)
    return (centered * inverse, inverse)


def norm_back(grad_normed, normed, inverse):
    first_mean = jnp.mean(grad_normed, axis=-1, keepdims=True)
    second_mean = jnp.mean(grad_normed * normed, axis=-1, keepdims=True)
    return inverse * (grad_normed - first_mean - normed * second_mean)


def gelu_value(inputs):
    return 0.5 * inputs * (1.0 + jax.scipy.special.erf(inputs * 0.7071067811865476))


def gelu_slope(inputs):
    cumulative = 0.5 * (1.0 + jax.scipy.special.erf(inputs * 0.7071067811865476))
    return cumulative + inputs * jnp.exp(-0.5 * inputs * inputs) * 0.3989422804014327


def masked_scores(queries, key_rows, segments):
    scores = jnp.einsum(
        "qhd,khd->hqk", queries, key_rows, preferred_element_type=jnp.float32
    ) * HD ** (-0.5)
    matching = segments[:, None] == segments[None, :]
    return jnp.where(matching[None], scores, -1e30)


def attend_forward(pieces):
    queries, key_rows, values, segments = pieces
    scores = masked_scores(queries, key_rows, segments)
    highest = jnp.max(scores, axis=-1, keepdims=True)
    exponent = jnp.exp(scores - highest)
    totals = jnp.sum(exponent, axis=-1, keepdims=True)
    probability = (exponent / totals).astype(jnp.bfloat16)
    context = jnp.einsum("hqk,khd->qhd", probability, values, preferred_element_type=jnp.float32)
    return (context, (highest + jnp.log(totals))[..., 0])


def attend_back(pieces):
    queries, key_rows, values, segments, log_total, grad_context = pieces
    scores = masked_scores(queries, key_rows, segments)
    probability = jnp.exp(scores - log_total[..., None])
    grad_prob = jnp.einsum("qhd,khd->hqk", grad_context, values, preferred_element_type=jnp.float32)
    weighted = jnp.sum(probability * grad_prob, axis=-1, keepdims=True)
    grad_score = (probability * (grad_prob - weighted)).astype(jnp.bfloat16)
    grad_query = jnp.einsum(
        "hqk,khd->qhd", grad_score, key_rows, preferred_element_type=jnp.float32
    ) * HD ** (-0.5)
    grad_key = jnp.einsum(
        "hqk,qhd->khd", grad_score, queries, preferred_element_type=jnp.float32
    ) * HD ** (-0.5)
    grad_value = jnp.einsum(
        "hqk,qhd->khd",
        probability.astype(jnp.bfloat16),
        grad_context,
        preferred_element_type=jnp.float32,
    )
    return jnp.stack([grad_query, grad_key, grad_value], axis=2)


def adam_update(weight, moment, square, clipped, rate, decay):
    moment = BETA_ONE * moment + (1.0 - BETA_ONE) * clipped
    square = BETA_TWO * square + (1.0 - BETA_TWO) * clipped * clipped
    corrected = (
        moment / (1.0 - BETA_ONE**STEP) / (jnp.sqrt(square / (1.0 - BETA_TWO**STEP)) + ADAM_EPS)
    )
    return (weight - rate * (corrected + decay * weight), moment, square)


def add_squares(running, member):
    return running + jnp.sum(member * member)


def on_device(
    tokens,
    time_embed,
    segment_ids,
    cotangent,
    input_weight,
    input_moment,
    input_square,
    output_weight,
    output_moment,
    output_square,
    upward_weight,
    upward_moment,
    upward_square,
    downward_weight,
    downward_moment,
    downward_square,
    head_bias,
    head_moment,
    head_square,
    hidden_bias,
    hidden_moment,
    hidden_square,
    norm_gains,
    gains_moment,
    gains_square,
    branch_biases,
    biases_moment,
    biases_square,
):
    masters = (
        input_weight,
        output_weight,
        upward_weight,
        downward_weight,
        head_bias,
        hidden_bias,
        norm_gains,
        branch_biases,
    )
    moments = (
        input_moment,
        output_moment,
        upward_moment,
        downward_moment,
        head_moment,
        hidden_moment,
        gains_moment,
        biases_moment,
    )
    squares = (
        input_square,
        output_square,
        upward_square,
        downward_square,
        head_square,
        hidden_square,
        gains_square,
        biases_square,
    )
    (
        weights_in,
        weights_out,
        weights_up,
        weights_down,
        head_shift,
        unit_shift,
        gains_low,
        shifts_low,
    ) = (
        lax.all_gather(input_weight.astype(jnp.bfloat16), "rows", axis=0, tiled=True),
        lax.all_gather(output_weight.astype(jnp.bfloat16), "rows", axis=0, tiled=True),
        lax.all_gather(upward_weight.astype(jnp.bfloat16), "rows", axis=0, tiled=True),
        lax.all_gather(downward_weight.astype(jnp.bfloat16), "rows", axis=0, tiled=True),
        lax.all_gather(head_bias.astype(jnp.bfloat16), "rows", axis=0, tiled=True),
        lax.all_gather(hidden_bias.astype(jnp.bfloat16), "rows", axis=0, tiled=True),
        lax.all_gather(norm_gains.astype(jnp.bfloat16), "rows", axis=0, tiled=True),
        lax.all_gather(branch_biases.astype(jnp.bfloat16), "rows", axis=0, tiled=True),
    )
    seq_count, length = segment_ids.shape
    width = tokens.shape[1]
    num_heads = head_shift.shape[1]
    head_size = head_shift.shape[0] // 2
    tok_rows = seq_count * length
    gains = gains_low.astype(jnp.float32)
    shifts = shifts_low.astype(jnp.float32)
    embedded = (
        tokens.astype(jnp.float32).reshape(seq_count, length, width)
        + time_embed.astype(jnp.float32)[:, None, :]
    ).reshape(tok_rows, width)
    embedded_low = embedded.astype(jnp.bfloat16)
    head_float = head_shift.astype(jnp.float32)
    offset = jnp.stack(
        [
            head_float[:head_size].T,
            jnp.zeros((num_heads, head_size), jnp.float32),
            head_float[head_size:].T,
        ],
        axis=1,
    )
    projected = jnp.dot(embedded_low, weights_in, preferred_element_type=jnp.float32).reshape(
        tok_rows, num_heads, 3, head_size
    )
    projected = (
        (projected + offset)
        .astype(jnp.bfloat16)
        .reshape(seq_count, length, num_heads, 3, head_size)
    )
    queries = projected[:, :, :, 0]
    key_rows = projected[:, :, :, 1]
    values = projected[:, :, :, 2]
    context, log_total = lax.map(attend_forward, (queries, key_rows, values, segment_ids))
    context_low = context.reshape(tok_rows, num_heads * head_size).astype(jnp.bfloat16)
    mixed_part = lax.dot_general(
        context_low, weights_out, ROW_PAIR, preferred_element_type=jnp.float32
    )
    mixed = lax.psum(mixed_part, "tp")
    normed_one, inverse_one = norm_stats(embedded + mixed + shifts[:, 0])
    hidden = normed_one * gains[:, 0] + shifts[:, 1]
    hidden_low = hidden.astype(jnp.bfloat16)
    unit_offset = unit_shift.astype(jnp.float32).T.reshape(-1)
    pre_act = jnp.dot(hidden_low, weights_up, preferred_element_type=jnp.float32) + unit_offset
    expanded_low = gelu_value(pre_act).astype(jnp.bfloat16)
    reduced_part = lax.dot_general(
        expanded_low, weights_down, ROW_PAIR, preferred_element_type=jnp.float32
    )
    reduced = lax.psum(reduced_part, "tp")
    normed_two, inverse_two = norm_stats(hidden + reduced + shifts[:, 2])
    block_output = (normed_two * gains[:, 1] + shifts[:, 3]).astype(jnp.bfloat16)
    upstream = cotangent.astype(jnp.float32)
    gain_two = jnp.sum(upstream * normed_two, axis=0)
    shift_three = jnp.sum(upstream, axis=0)
    grad_pre_two = norm_back(upstream * gains[:, 1], normed_two, inverse_two)
    shift_two = jnp.sum(grad_pre_two, axis=0)
    grad_pre_two_low = grad_pre_two.astype(jnp.bfloat16)
    grad_down = lax.dot_general(
        grad_pre_two_low, expanded_low, COL_PAIR, preferred_element_type=jnp.float32
    )
    grad_act = jnp.dot(grad_pre_two_low, weights_down, preferred_element_type=jnp.float32)
    grad_pre_act = (grad_act * gelu_slope(pre_act)).astype(jnp.bfloat16)
    unit_sums = jnp.sum(grad_pre_act, axis=0, dtype=jnp.float32)
    grad_unit = unit_sums.reshape(-1, 2 * head_size).T
    grad_up = lax.dot_general(
        hidden_low, grad_pre_act, COL_PAIR, preferred_element_type=jnp.float32
    )
    back_part = lax.dot_general(
        grad_pre_act, weights_up, ROW_PAIR, preferred_element_type=jnp.float32
    )
    grad_hidden = lax.psum(back_part, "tp") + grad_pre_two
    gain_one = jnp.sum(grad_hidden * normed_one, axis=0)
    shift_one = jnp.sum(grad_hidden, axis=0)
    grad_pre_one = norm_back(grad_hidden * gains[:, 0], normed_one, inverse_one)
    shift_zero = jnp.sum(grad_pre_one, axis=0)
    grad_pre_one_low = grad_pre_one.astype(jnp.bfloat16)
    grad_out = lax.dot_general(
        grad_pre_one_low, context_low, COL_PAIR, preferred_element_type=jnp.float32
    )
    grad_context = jnp.dot(
        grad_pre_one_low, weights_out, preferred_element_type=jnp.float32
    ).astype(jnp.bfloat16)
    grad_context = grad_context.reshape(seq_count, length, num_heads, head_size)
    grad_projected = lax.map(
        attend_back, (queries, key_rows, values, segment_ids, log_total, grad_context)
    )
    grad_projected = grad_projected.reshape(tok_rows, num_heads * 3 * head_size).astype(
        jnp.bfloat16
    )
    head_sums = jnp.sum(grad_projected, axis=0, dtype=jnp.float32).reshape(num_heads, 3, head_size)
    grad_head = jnp.concatenate([head_sums[:, 0].T, head_sums[:, 2].T], axis=0)
    grad_in = lax.dot_general(
        embedded_low, grad_projected, COL_PAIR, preferred_element_type=jnp.float32
    )
    input_part = lax.dot_general(
        grad_projected, weights_in, ROW_PAIR, preferred_element_type=jnp.float32
    )
    input_grad = lax.psum(input_part, "tp") + grad_pre_one
    grad_gains = jnp.stack([gain_one, gain_two], axis=1)
    grad_shifts = jnp.stack([shift_zero, shift_one, shift_two, shift_three], axis=1)
    sent_in, sent_out, sent_up, sent_down, sent_head, sent_unit, sent_gains, sent_shifts = (
        lax.psum_scatter(grad_in, "rows", scatter_dimension=0, tiled=True),
        lax.psum_scatter(grad_out, "rows", scatter_dimension=0, tiled=True),
        lax.psum_scatter(grad_up, "rows", scatter_dimension=0, tiled=True),
        lax.psum_scatter(grad_down, "rows", scatter_dimension=0, tiled=True),
        lax.psum_scatter(grad_head, "rows", scatter_dimension=0, tiled=True),
        lax.psum_scatter(grad_unit, "rows", scatter_dimension=0, tiled=True),
        lax.psum_scatter(grad_gains, "rows", scatter_dimension=0, tiled=True),
        lax.psum_scatter(grad_shifts, "rows", scatter_dimension=0, tiled=True),
    )
    gradients = (
        sent_in,
        sent_out,
        sent_up,
        sent_down,
        sent_head,
        sent_unit,
        sent_gains,
        sent_shifts,
    )
    split_part = reduce(
        add_squares,
        (sent_in, sent_out, sent_up, sent_down, sent_head, sent_unit),
        jnp.zeros((), jnp.float32),
    )
    copied_part = (
        jnp.sum(sent_gains * sent_gains) + jnp.sum(sent_shifts * sent_shifts)
    ) / lax.axis_size("tp")
    grad_norm = jnp.sqrt(lax.psum(split_part + copied_part, ("rows", "tp")))
    factor = CLIP / jnp.maximum(grad_norm, CLIP)
    updated = [
        adam_update(
            masters[position],
            moments[position],
            squares[position],
            gradients[position] * factor,
            RATES[position],
            DECAYS[position],
        )
        for position in range(8)
    ]
    return (
        block_output,
        input_grad,
        grad_norm.reshape(1),
        updated[0][0],
        updated[0][1],
        updated[0][2],
        updated[1][0],
        updated[1][1],
        updated[1][2],
        updated[2][0],
        updated[2][1],
        updated[2][2],
        updated[3][0],
        updated[3][1],
        updated[3][2],
        updated[4][0],
        updated[4][1],
        updated[4][2],
        updated[5][0],
        updated[5][1],
        updated[5][2],
        updated[6][0],
        updated[6][1],
        updated[6][2],
        updated[7][0],
        updated[7][1],
        updated[7][2],
    )


def flip(value, axis):
    return lax.ppermute(value, axis, [(0, 1), (1, 0)])


def turn(value, amount, count):
    return lax.ppermute(value, "z", [(i, (i + amount) % count) for i in range(count)])


def swap_halves(value, swapped):
    half = value.shape[-1] // 2
    return jnp.where(
        swapped, jnp.concatenate([value[..., half:], value[..., :half]], axis=-1), value
    )


def in_order(first, mine, other):
    return jnp.where(
        first, jnp.concatenate([mine, other], axis=0), jnp.concatenate([other, mine], axis=0)
    )


def attend_kernel(length, head_size, block, emb_ref, weight_ref, bias_ref, col_ref, row_ref, proj_ref, ctx_ref):
    width = 3 * head_size
    proj = jnp.dot(emb_ref[...], weight_ref[0], preferred_element_type=jnp.float32)
    proj_ref[0] = (proj[:, :width] + bias_ref[0, 0:1, :width]).astype(jnp.bfloat16)
    keys = proj_ref[0, :, head_size : 2 * head_size]
    values = proj_ref[0, :, 2 * head_size : width]

    def one_block(at, carry):
        rows = pl.ds(pl.multiple_of(at * block, block), block)
        queries = proj_ref[0, rows, 0:head_size] * jnp.bfloat16(head_size**-0.5)
        scores = lax.dot_general(queries, keys, ROW_PAIR, preferred_element_type=jnp.float32)
        scores = jnp.where(col_ref[rows, :] == row_ref[...], scores, -1e30)
        highest = jnp.max(scores, axis=1, keepdims=True)
        exponent = jnp.exp(scores - highest)
        totals = jnp.sum(exponent, axis=1, keepdims=True)
        probability = (exponent * (1.0 / totals)).astype(jnp.bfloat16)
        ctx = jnp.dot(probability, values, preferred_element_type=jnp.float32)
        ctx_ref[0, rows, :] = ctx.astype(jnp.bfloat16)
        return carry

    lax.fori_loop(0, length // block, one_block, 0)


def attend_back_kernel(length, head_size, block, proj_ref, grad_ref, col_ref, row_ref, out_ref, key_sum, value_sum):
    width = 3 * head_size
    keys = proj_ref[0, :, head_size : 2 * head_size]
    values = proj_ref[0, :, 2 * head_size : width]
    key_sum[...] = jnp.zeros_like(key_sum)
    value_sum[...] = jnp.zeros_like(value_sum)
    scale = head_size**-0.5

    def one_block(at, carry):
        rows = pl.ds(pl.multiple_of(at * block, block), block)
        queries = proj_ref[0, rows, 0:head_size] * jnp.bfloat16(scale)
        grads = grad_ref[0, rows, :]
        scores = lax.dot_general(keys, queries, ROW_PAIR, preferred_element_type=jnp.float32)
        scores = jnp.where(col_ref[...] == row_ref[0:1, rows], scores, -1e30)
        highest = jnp.max(scores, axis=0, keepdims=True)
        exponent = jnp.exp(scores - highest)
        probability = exponent * (1.0 / jnp.sum(exponent, axis=0, keepdims=True))
        grad_prob = lax.dot_general(values, grads, ROW_PAIR, preferred_element_type=jnp.float32)
        weighted = jnp.sum(probability * grad_prob, axis=0, keepdims=True)
        grad_score = (probability * (grad_prob - weighted)).astype(jnp.bfloat16)
        value_sum[...] += jnp.dot(
            probability.astype(jnp.bfloat16), grads, preferred_element_type=jnp.float32
        )
        key_sum[...] += jnp.dot(grad_score, queries, preferred_element_type=jnp.float32)
        grad_query = lax.dot_general(grad_score, keys, COL_PAIR, preferred_element_type=jnp.float32)
        out_ref[0, rows, 0:head_size] = (grad_query * scale).astype(jnp.bfloat16)
        return carry

    lax.fori_loop(0, length // block, one_block, 0)
    out_ref[0, :, head_size : 2 * head_size] = key_sum[...].astype(jnp.bfloat16)
    out_ref[0, :, 2 * head_size : width] = value_sum[...].astype(jnp.bfloat16)


def attend_all(emb_low, weights, biases, segments, head_size):
    heads, depth, packed = weights.shape
    length = emb_low.shape[0]
    whole = lambda shape: pl.BlockSpec(shape, lambda h: (0, 0))
    each = lambda shape: pl.BlockSpec((1,) + shape, lambda h: (h, 0, 0))
    return pl.pallas_call(
        partial(attend_kernel, length, head_size, 256),
        grid=(heads,),
        in_specs=[
            whole((length, depth)),
            each((depth, packed)),
            each((8, packed)),
            whole((length, 1)),
            whole((1, length)),
        ],
        out_specs=[each((length, 3 * head_size)), each((length, head_size))],
        out_shape=[
            jax.ShapeDtypeStruct((heads, length, 3 * head_size), jnp.bfloat16),
            jax.ShapeDtypeStruct((heads, length, head_size), jnp.bfloat16),
        ],
        compiler_params=pltpu.CompilerParams(vmem_limit_bytes=48 << 20),
        cost_estimate=pl.CostEstimate(
            flops=2 * heads * length * (depth * packed + 2 * length * 128),
            bytes_accessed=8 << 20,
            transcendentals=heads * length * length,
        ),
        name="attend_all",
    )(emb_low, weights, biases, segments[:, None], segments[None, :])


def attend_all_back(proj, grad_ctx, segments, head_size):
    heads, length, width = proj.shape
    whole = lambda shape: pl.BlockSpec(shape, lambda h: (0, 0))
    each = lambda shape: pl.BlockSpec((1,) + shape, lambda h: (h, 0, 0))
    return pl.pallas_call(
        partial(attend_back_kernel, length, head_size, 256),
        grid=(heads,),
        in_specs=[
            each((length, width)),
            each((length, head_size)),
            whole((length, 1)),
            whole((1, length)),
        ],
        out_specs=each((length, width)),
        out_shape=jax.ShapeDtypeStruct((heads, length, width), jnp.bfloat16),
        scratch_shapes=[
            pltpu.VMEM((length, head_size), jnp.float32),
            pltpu.VMEM((length, head_size), jnp.float32),
        ],
        compiler_params=pltpu.CompilerParams(vmem_limit_bytes=48 << 20),
        cost_estimate=pl.CostEstimate(
            flops=2 * heads * length * length * 128 * 5,
            bytes_accessed=8 << 20,
            transcendentals=heads * length * length,
        ),
        name="attend_all_back",
    )(proj, grad_ctx, segments[:, None], segments[None, :])


def spread_tokens(own):
    near = flip(own, "y")
    pair = jnp.concatenate([own, near], axis=0)
    return jnp.concatenate([pair, flip(pair, "core")], axis=0)


def sum_tokens(left, right, pairing):
    half = left.shape[0] // 2
    far = lax.dot_general(left[half:], right, pairing, preferred_element_type=jnp.float32)
    came = flip(far.astype(jnp.bfloat16), "core")
    near = lax.dot_general(left[:half], right, pairing, preferred_element_type=jnp.float32)
    near = near + came.astype(jnp.float32)
    quarter = half // 2
    return near[:quarter] + flip(near[quarter:].astype(jnp.bfloat16), "y").astype(jnp.float32)


def spread_output(own, zs, dtype):
    count = 4
    at_z, at_y = lax.axis_index("z"), lax.axis_index("y")
    quarter, width = own.shape
    result = jnp.zeros((2 * count * quarter, width), dtype)
    for step in range(count):
        pairs = []
        for core in range(2):
            for place in range(count):
                index = core * 2 + place % 2
                target = (place // 2) * count + (index + step) % count
                pairs.append((core * count + place, target))
        came = lax.ppermute(own, ("core", "z"), pairs)
        crossed = flip(came, "y")
        index = (at_z - step) % count
        start = (index % 2) * count + (index // 2) * 2
        result = lax.dynamic_update_slice(
            result, came.astype(dtype), ((start + at_y) * quarter, 0)
        )
        result = lax.dynamic_update_slice(
            result, crossed.astype(dtype), ((start + 1 - at_y) * quarter, 0)
        )
    return result


def sum_scalar(value):
    value = jnp.broadcast_to(value, (8, 128))
    for axis in ("core", "y", "x"):
        value = value + flip(value, axis)
    value = value + lax.ppermute(value, "z", [(0, 1), (1, 0), (2, 3), (3, 2)])
    value = value + lax.ppermute(value, "z", [(0, 3), (3, 0), (1, 2), (2, 1)])
    return value[0, 0]


def on_grid(*arguments):
    tokens, time_embed, segment_ids, cotangent = arguments[:4]
    masters, moments, squares = arguments[4::3], arguments[5::3], arguments[6::3]
    input_weight, output_weight, upward_weight, downward_weight = masters[:4]
    head_bias, hidden_bias, norm_gains, branch_biases = masters[4:]
    at_x, at_core = lax.axis_index("x"), lax.axis_index("core")
    at_z, at_y = lax.axis_index("z"), lax.axis_index("y")
    first_core, first_x = at_core == 0, at_x == 0
    swapped = at_x == 1
    low = jnp.bfloat16
    f32 = jnp.float32
    length = segment_ids.shape[1]
    head_size = head_bias.shape[0] * 4 // 2
    zs = 4
    place = at_core * 2 + at_y
    quarter = length // 4

    rows = input_weight.shape[0]
    wide = upward_weight.shape[1] // 2
    packed = 4 * head_size
    small_rows = head_bias.shape[0]

    def head_piece(half):
        body = jnp.concatenate(
            [
                input_weight[:, half * 3 * head_size : (half + 1) * 3 * head_size],
                output_weight[:, half * head_size : (half + 1) * head_size],
            ],
            axis=1,
        )
        shifts = jnp.concatenate(
            [head_bias[:, half : half + 1], hidden_bias[:, 2 * half : 2 * half + 2]], axis=1
        ).T
        shifts = jnp.pad(shifts, ((0, 0), (0, packed - small_rows)))
        vectors = jnp.concatenate([norm_gains, branch_biases], axis=1).T
        vectors = jnp.pad(vectors, ((0, 7), (0, packed - rows)))
        return jnp.concatenate([body, shifts, vectors], axis=0).astype(low)

    def column_piece(weight):
        return lambda half: weight[:, half * wide : (half + 1) * wide].astype(low)

    def pair_cores(piece):
        zero, one = piece(0), piece(1)
        mine = jnp.where(first_core, zero, one)
        other = flip(jnp.where(first_core, one, zero), "core")
        return mine, other

    def spread(block):
        came = [block] + [turn(block, step, zs) for step in range(1, zs)]
        return came, [flip(member, "x") for member in came]

    mine, other = pair_cores(head_piece)
    head_block = jnp.concatenate(
        [in_order(first_core, mine[:rows], other[:rows]), in_order(first_core, mine[rows:], other[rows:])],
        axis=0,
    )
    head_own, head_far = spread(head_block)
    up_own, up_far = spread(in_order(first_core, *pair_cores(column_piece(upward_weight))))
    down_own, down_far = spread(in_order(first_core, *pair_cores(column_piece(downward_weight))))

    seat = ("core", "z")
    holds = at_core == at_z // 2
    lend = [((i // 2) * zs + i, (1 - i // 2) * zs + i) for i in range(zs)]

    def borrow(kept, sent):
        return jnp.where(holds, kept, lax.ppermute(sent, seat, lend))

    local = at_z % 2
    own_tokens = lax.dynamic_slice_in_dim(tokens, local * length, length, 0)
    own_tokens = borrow(own_tokens, own_tokens)
    own_time = lax.dynamic_slice_in_dim(time_embed, local, 1, 0)
    own_time = borrow(own_time, own_time)
    own_ids = lax.dynamic_slice_in_dim(segment_ids, local, 1, 0)
    own_ids = borrow(own_ids, own_ids)[0]

    def at_quarter(which):
        return lax.dynamic_slice_in_dim(cotangent, local * length + which * quarter, quarter, 0)

    upstream = borrow(at_quarter(place), at_quarter(place ^ 2))
    upstream = swap_halves(upstream, swapped).astype(f32)

    def relative(values):
        return jnp.concatenate(
            [lax.dynamic_slice_in_dim(values, (place ^ turnover) * quarter, quarter, 0) for turnover in range(4)],
            axis=0,
        )

    embedded_all = swap_halves(
        relative(own_tokens).astype(f32) + own_time.astype(f32), swapped
    )
    embedded = embedded_all[:quarter]
    embedded_low = embedded_all.astype(low)
    segments = relative(own_ids)

    span = 2 * rows
    small_own = [member[span:] for member in head_own]
    small_far = [member[span:] for member in head_far]
    weights_head = jnp.stack(
        [jnp.concatenate([a[:span], b[:span]], axis=0) for a, b in zip(head_own, head_far)]
    )
    vectors = [
        jnp.concatenate([member[3:9], member[19:25]], axis=1).astype(f32)
        for member in (small_own[0], small_far[0])
    ]
    vectors = jnp.concatenate(vectors, axis=1)
    gains, shifts = vectors[0:2], vectors[2:6]

    def shift_rows(member):
        return jnp.concatenate([member[0:3, :small_rows], member[16:19, :small_rows]], axis=1)

    biases, unit_offset = [], []
    for a, b in zip(small_own, small_far):
        near, distant = shift_rows(a).astype(f32), shift_rows(b).astype(f32)
        lower = jnp.where(first_x, near, distant)
        upper = jnp.where(first_x, distant, near)
        biases.append(
            jnp.concatenate(
                [lower[0], jnp.zeros((head_size,), f32), upper[0], jnp.zeros((head_size,), f32)]
            )
        )
        unit_offset.append(jnp.concatenate([lower[1:], upper[1:]], axis=1).reshape(-1))
    biases = jnp.broadcast_to(jnp.stack(biases)[:, None, :], (zs, 8, packed))
    unit_offset = jnp.concatenate(unit_offset)

    projected, context = attend_all(embedded_low, weights_head, biases, segments, head_size)
    context_low = jnp.concatenate([context[i] for i in range(zs)], axis=1)
    weights_in = jnp.concatenate([weights_head[i, :, : 3 * head_size] for i in range(zs)], axis=1)
    weights_out = jnp.concatenate([weights_head[i, :, 3 * head_size :] for i in range(zs)], axis=1)
    mixed = sum_tokens(context_low, weights_out, ROW_PAIR)
    normed_one, inverse_one = norm_stats(embedded + mixed + shifts[0])
    hidden = normed_one * gains[0] + shifts[1]
    hidden_low = spread_tokens(hidden.astype(low))

    def joined(own, far):
        return jnp.concatenate(
            [jnp.concatenate(own, axis=1), jnp.concatenate(far, axis=1)], axis=0
        )

    weights_up, weights_down = joined(up_own, up_far), joined(down_own, down_far)
    pre_act = jnp.dot(hidden_low, weights_up, preferred_element_type=f32) + unit_offset
    expanded_low = gelu_value(pre_act).astype(low)
    reduced = sum_tokens(expanded_low, weights_down, ROW_PAIR)
    normed_two, inverse_two = norm_stats(hidden + reduced + shifts[2])
    out = swap_halves((normed_two * gains[1] + shifts[3]).astype(low), swapped)
    block_output = spread_output(out, zs, low)

    gain_two = jnp.sum(upstream * normed_two, axis=0)
    shift_three = jnp.sum(upstream, axis=0)
    grad_pre_two = norm_back(upstream * gains[1], normed_two, inverse_two)
    shift_two = jnp.sum(grad_pre_two, axis=0)
    grad_two_low = spread_tokens(grad_pre_two.astype(low))
    grad_down = lax.dot_general(grad_two_low, expanded_low, COL_PAIR, preferred_element_type=f32)
    grad_act = jnp.dot(grad_two_low, weights_down, preferred_element_type=f32)
    grad_pre_act = (grad_act * gelu_slope(pre_act)).astype(low)
    unit_sums = jnp.sum(grad_pre_act, axis=0, dtype=f32)
    back = sum_tokens(grad_pre_act, weights_up, ROW_PAIR)
    grad_up = lax.dot_general(hidden_low, grad_pre_act, COL_PAIR, preferred_element_type=f32)
    grad_hidden = back + grad_pre_two
    gain_one = jnp.sum(grad_hidden * normed_one, axis=0)
    shift_one = jnp.sum(grad_hidden, axis=0)
    grad_pre_one = norm_back(grad_hidden * gains[0], normed_one, inverse_one)
    shift_zero = jnp.sum(grad_pre_one, axis=0)
    grad_one_low = spread_tokens(grad_pre_one.astype(low))
    grad_context = jnp.dot(grad_one_low, weights_out, preferred_element_type=f32).astype(low)
    grad_context = jnp.stack(
        [grad_context[:, i * head_size : (i + 1) * head_size] for i in range(zs)]
    )
    grad_out = lax.dot_general(grad_one_low, context_low, COL_PAIR, preferred_element_type=f32)
    grad_heads = attend_all_back(projected, grad_context, segments, head_size)
    grad_projected = jnp.concatenate([grad_heads[i] for i in range(zs)], axis=1)
    input_part = sum_tokens(grad_projected, weights_in, ROW_PAIR)
    input_grad = swap_halves((input_part + grad_pre_one).astype(low), swapped)
    input_grad = spread_output(input_grad, zs, f32)
    grad_in = lax.dot_general(embedded_low, grad_projected, COL_PAIR, preferred_element_type=f32)
    head_sums = jnp.sum(grad_projected, axis=0, dtype=f32).reshape(zs, 3, head_size)

    def collect(own, far):
        near = [
            (a + flip(b.astype(low), "x").astype(f32)) for a, b in zip(own, far)
        ]
        total = near[0]
        for step in range(1, zs):
            total = total + turn(near[step].astype(low), -step, zs).astype(f32)
        return total

    def return_cores(block):
        half = block.shape[0] // 2
        mine = jnp.where(first_core, block[:half], block[half:])
        sent = jnp.where(first_core, block[half:], block[:half])
        came = flip(sent.astype(low), "core").astype(f32)
        return jnp.where(first_core, mine, came), jnp.where(first_core, came, mine)

    def split_blocks(grad):
        parts = [grad[:, i * wide : (i + 1) * wide] for i in range(zs)]
        return [p[:span] for p in parts], [p[span:] for p in parts]

    total_down = collect(*split_blocks(grad_down))
    total_up = collect(*split_blocks(grad_up))
    head_near, head_distant = [], []
    units = unit_sums.reshape(zs, 2, 2, 2 * small_rows)
    for i in range(zs):
        whole = jnp.concatenate(
            [
                grad_in[:, i * 3 * head_size : (i + 1) * 3 * head_size],
                grad_out[:, i * head_size : (i + 1) * head_size],
            ],
            axis=1,
        )
        lower = jnp.concatenate([head_sums[i, 0][None], units[i, :, 0]], axis=0)
        upper = jnp.concatenate([head_sums[i, 2][None], units[i, :, 1]], axis=0)
        kept = jnp.where(first_x, lower, upper)
        sent = jnp.where(first_x, upper, lower)
        pad = ((0, 13), (0, packed - 2 * small_rows))
        head_near.append(jnp.concatenate([whole[:span], jnp.pad(kept, pad)], axis=0))
        head_distant.append(jnp.concatenate([whole[span:], jnp.pad(sent, pad)], axis=0))
    total_head = collect(head_near, head_distant)
    small_total = total_head[span : span + 3]
    small_total = jnp.concatenate(
        [small_total[:, :small_rows], small_total[:, small_rows : 2 * small_rows]], axis=0
    )
    tail = jnp.pad(small_total, ((0, 0), (0, packed - small_rows)))
    head_zero, head_one = return_cores(
        jnp.concatenate(
            [
                total_head[:rows],
                jnp.pad(tail[:3], ((0, 13), (0, 0))),
                total_head[rows:span],
                jnp.pad(tail[3:], ((0, 13), (0, 0))),
            ],
            axis=0,
        )
    )
    up_zero, up_one = return_cores(total_up)
    down_zero, down_one = return_cores(total_down)
    in_size = 3 * head_size
    sent_in = jnp.concatenate([head_zero[:rows, :in_size], head_one[:rows, :in_size]], axis=1)
    sent_out = jnp.concatenate([head_zero[:rows, in_size:], head_one[:rows, in_size:]], axis=1)
    sent_up = jnp.concatenate([up_zero, up_one], axis=1)
    sent_down = jnp.concatenate([down_zero, down_one], axis=1)
    tails = [member[rows : rows + 3, :small_rows].T for member in (head_zero, head_one)]
    sent_head = jnp.concatenate([tails[0][:, :1], tails[1][:, :1]], axis=1)
    sent_unit = jnp.concatenate([tails[0][:, 1:], tails[1][:, 1:]], axis=1)

    feature = jnp.stack([gain_one, gain_two, shift_zero, shift_one, shift_two, shift_three])
    feature = jnp.pad(feature, ((0, 2), (0, 0)))
    for axis in ("core", "y"):
        feature = feature + flip(feature, axis)
    feature = feature + lax.ppermute(feature, "z", [(0, 1), (1, 0), (2, 3), (3, 2)])
    feature = feature + lax.ppermute(feature, "z", [(0, 3), (3, 0), (1, 2), (2, 1)])
    feature = feature[:, :span] + flip(feature[:, span:], "x")
    feature = jnp.where(first_core, feature[:, :rows], feature[:, rows:])
    sent_gains, sent_shifts = feature[0:2].T, feature[2:6].T

    gradients = (sent_in, sent_out, sent_up, sent_down, sent_head, sent_unit, sent_gains, sent_shifts)
    split_part = reduce(add_squares, gradients[:6], jnp.zeros((), f32))
    copied_part = reduce(add_squares, gradients[6:], jnp.zeros((), f32)) / (
        lax.axis_size("z") * lax.axis_size("y")
    )
    grad_norm = jnp.sqrt(sum_scalar(split_part + copied_part))
    factor = CLIP / jnp.maximum(grad_norm, CLIP)
    results = [block_output, input_grad, grad_norm.reshape(1)]
    for position in range(8):
        results += adam_update(
            masters[position],
            moments[position],
            squares[position],
            gradients[position] * factor,
            RATES[position],
            DECAYS[position],
        )
    return tuple(results)


def solution(mesh):
    plain = mesh.shape["rows"] != 4 or mesh.shape["tp"] != 8
    if plain:
        rows, tp = "rows", "tp"
        grid, work = mesh, on_device
    else:
        rows, tp = ("x", "core"), ("z", "y")
        grid = Mesh(mesh.devices.reshape(2, 2, 4, 2), ("x", "core", "z", "y"))
        work = on_grid
    narrow, split = P(rows, None), P(rows, tp)
    return jax.shard_map(
        work,
        mesh=grid,
        in_specs=(narrow,) * 4 + (split,) * 18 + (narrow,) * 6,
        out_specs=(narrow, narrow, P()) + (split,) * 18 + (narrow,) * 6,
        check_vma=False,
    )
```

```python
from functools import partial, reduce

import jax
import jax.numpy as jnp
from jax import lax
from jax.experimental import pallas as pl
from jax.experimental.pallas import tpu as pltpu
from jax.sharding import Mesh
from jax.sharding import PartitionSpec as P

HD = 64
STEP = 10


NORM_EPS = 1e-05
BETA_ONE = 0.9
BETA_TWO = 0.999
ADAM_EPS = 1e-08
CLIP = 1.0
RATES = (0.1, 0.4, 0.1, 0.05, 0.5, 0.5, 0.5, 0.5)
DECAYS = (0.01, 0.01, 0.01, 0.01, 0.0, 0.0, 0.0, 0.0)
ROW_PAIR = (((1,), (1,)), ((), ()))
COL_PAIR = (((0,), (0,)), ((), ()))


def norm_stats(summed):
    average = jnp.mean(summed, axis=-1, keepdims=True)
    centered = summed - average
    inverse = lax.rsqrt(jnp.mean(centered * centered, axis=-1, keepdims=True) + NORM_EPS)
    return (centered * inverse, inverse)


def norm_back(grad_normed, normed, inverse):
    first_mean = jnp.mean(grad_normed, axis=-1, keepdims=True)
    second_mean = jnp.mean(grad_normed * normed, axis=-1, keepdims=True)
    return inverse * (grad_normed - first_mean - normed * second_mean)


def gelu_value(inputs):
    return 0.5 * inputs * (1.0 + jax.scipy.special.erf(inputs * 0.7071067811865476))


def gelu_slope(inputs):
    cumulative = 0.5 * (1.0 + jax.scipy.special.erf(inputs * 0.7071067811865476))
    return cumulative + inputs * jnp.exp(-0.5 * inputs * inputs) * 0.3989422804014327


def masked_scores(queries, key_rows, segments):
    scores = jnp.einsum(
        "qhd,khd->hqk", queries, key_rows, preferred_element_type=jnp.float32
    ) * HD ** (-0.5)
    matching = segments[:, None] == segments[None, :]
    return jnp.where(matching[None], scores, -1e30)


def attend_forward(pieces):
    queries, key_rows, values, segments = pieces
    scores = masked_scores(queries, key_rows, segments)
    highest = jnp.max(scores, axis=-1, keepdims=True)
    exponent = jnp.exp(scores - highest)
    totals = jnp.sum(exponent, axis=-1, keepdims=True)
    probability = (exponent / totals).astype(jnp.bfloat16)
    context = jnp.einsum("hqk,khd->qhd", probability, values, preferred_element_type=jnp.float32)
    return (context, (highest + jnp.log(totals))[..., 0])


def attend_back(pieces):
    queries, key_rows, values, segments, log_total, grad_context = pieces
    scores = masked_scores(queries, key_rows, segments)
    probability = jnp.exp(scores - log_total[..., None])
    grad_prob = jnp.einsum("qhd,khd->hqk", grad_context, values, preferred_element_type=jnp.float32)
    weighted = jnp.sum(probability * grad_prob, axis=-1, keepdims=True)
    grad_score = (probability * (grad_prob - weighted)).astype(jnp.bfloat16)
    grad_query = jnp.einsum(
        "hqk,khd->qhd", grad_score, key_rows, preferred_element_type=jnp.float32
    ) * HD ** (-0.5)
    grad_key = jnp.einsum(
        "hqk,qhd->khd", grad_score, queries, preferred_element_type=jnp.float32
    ) * HD ** (-0.5)
    grad_value = jnp.einsum(
        "hqk,qhd->khd",
        probability.astype(jnp.bfloat16),
        grad_context,
        preferred_element_type=jnp.float32,
    )
    return jnp.stack([grad_query, grad_key, grad_value], axis=2)


def adam_update(weight, moment, square, clipped, rate, decay):
    moment = BETA_ONE * moment + (1.0 - BETA_ONE) * clipped
    square = BETA_TWO * square + (1.0 - BETA_TWO) * clipped * clipped
    corrected = (
        moment / (1.0 - BETA_ONE**STEP) / (jnp.sqrt(square / (1.0 - BETA_TWO**STEP)) + ADAM_EPS)
    )
    return (weight - rate * (corrected + decay * weight), moment, square)


def add_squares(running, member):
    return running + jnp.sum(member * member)


def on_device(
    tokens,
    time_embed,
    segment_ids,
    cotangent,
    input_weight,
    input_moment,
    input_square,
    output_weight,
    output_moment,
    output_square,
    upward_weight,
    upward_moment,
    upward_square,
    downward_weight,
    downward_moment,
    downward_square,
    head_bias,
    head_moment,
    head_square,
    hidden_bias,
    hidden_moment,
    hidden_square,
    norm_gains,
    gains_moment,
    gains_square,
    branch_biases,
    biases_moment,
    biases_square,
):
    masters = (
        input_weight,
        output_weight,
        upward_weight,
        downward_weight,
        head_bias,
        hidden_bias,
        norm_gains,
        branch_biases,
    )
    moments = (
        input_moment,
        output_moment,
        upward_moment,
        downward_moment,
        head_moment,
        hidden_moment,
        gains_moment,
        biases_moment,
    )
    squares = (
        input_square,
        output_square,
        upward_square,
        downward_square,
        head_square,
        hidden_square,
        gains_square,
        biases_square,
    )
    (
        weights_in,
        weights_out,
        weights_up,
        weights_down,
        head_shift,
        unit_shift,
        gains_low,
        shifts_low,
    ) = (
        lax.all_gather(input_weight.astype(jnp.bfloat16), "rows", axis=0, tiled=True),
        lax.all_gather(output_weight.astype(jnp.bfloat16), "rows", axis=0, tiled=True),
        lax.all_gather(upward_weight.astype(jnp.bfloat16), "rows", axis=0, tiled=True),
        lax.all_gather(downward_weight.astype(jnp.bfloat16), "rows", axis=0, tiled=True),
        lax.all_gather(head_bias.astype(jnp.bfloat16), "rows", axis=0, tiled=True),
        lax.all_gather(hidden_bias.astype(jnp.bfloat16), "rows", axis=0, tiled=True),
        lax.all_gather(norm_gains.astype(jnp.bfloat16), "rows", axis=0, tiled=True),
        lax.all_gather(branch_biases.astype(jnp.bfloat16), "rows", axis=0, tiled=True),
    )
    seq_count, length = segment_ids.shape
    width = tokens.shape[1]
    num_heads = head_shift.shape[1]
    head_size = head_shift.shape[0] // 2
    tok_rows = seq_count * length
    gains = gains_low.astype(jnp.float32)
    shifts = shifts_low.astype(jnp.float32)
    embedded = (
        tokens.astype(jnp.float32).reshape(seq_count, length, width)
        + time_embed.astype(jnp.float32)[:, None, :]
    ).reshape(tok_rows, width)
    embedded_low = embedded.astype(jnp.bfloat16)
    head_float = head_shift.astype(jnp.float32)
    offset = jnp.stack(
        [
            head_float[:head_size].T,
            jnp.zeros((num_heads, head_size), jnp.float32),
            head_float[head_size:].T,
        ],
        axis=1,
    )
    projected = jnp.dot(embedded_low, weights_in, preferred_element_type=jnp.float32).reshape(
        tok_rows, num_heads, 3, head_size
    )
    projected = (
        (projected + offset)
        .astype(jnp.bfloat16)
        .reshape(seq_count, length, num_heads, 3, head_size)
    )
    queries = projected[:, :, :, 0]
    key_rows = projected[:, :, :, 1]
    values = projected[:, :, :, 2]
    context, log_total = lax.map(attend_forward, (queries, key_rows, values, segment_ids))
    context_low = context.reshape(tok_rows, num_heads * head_size).astype(jnp.bfloat16)
    mixed_part = lax.dot_general(
        context_low, weights_out, ROW_PAIR, preferred_element_type=jnp.float32
    )
    mixed = lax.psum(mixed_part, "tp")
    normed_one, inverse_one = norm_stats(embedded + mixed + shifts[:, 0])
    hidden = normed_one * gains[:, 0] + shifts[:, 1]
    hidden_low = hidden.astype(jnp.bfloat16)
    unit_offset = unit_shift.astype(jnp.float32).T.reshape(-1)
    pre_act = jnp.dot(hidden_low, weights_up, preferred_element_type=jnp.float32) + unit_offset
    expanded_low = gelu_value(pre_act).astype(jnp.bfloat16)
    reduced_part = lax.dot_general(
        expanded_low, weights_down, ROW_PAIR, preferred_element_type=jnp.float32
    )
    reduced = lax.psum(reduced_part, "tp")
    normed_two, inverse_two = norm_stats(hidden + reduced + shifts[:, 2])
    block_output = (normed_two * gains[:, 1] + shifts[:, 3]).astype(jnp.bfloat16)
    upstream = cotangent.astype(jnp.float32)
    gain_two = jnp.sum(upstream * normed_two, axis=0)
    shift_three = jnp.sum(upstream, axis=0)
    grad_pre_two = norm_back(upstream * gains[:, 1], normed_two, inverse_two)
    shift_two = jnp.sum(grad_pre_two, axis=0)
    grad_pre_two_low = grad_pre_two.astype(jnp.bfloat16)
    grad_down = lax.dot_general(
        grad_pre_two_low, expanded_low, COL_PAIR, preferred_element_type=jnp.float32
    )
    grad_act = jnp.dot(grad_pre_two_low, weights_down, preferred_element_type=jnp.float32)
    grad_pre_act = (grad_act * gelu_slope(pre_act)).astype(jnp.bfloat16)
    unit_sums = jnp.sum(grad_pre_act, axis=0, dtype=jnp.float32)
    grad_unit = unit_sums.reshape(-1, 2 * head_size).T
    grad_up = lax.dot_general(
        hidden_low, grad_pre_act, COL_PAIR, preferred_element_type=jnp.float32
    )
    back_part = lax.dot_general(
        grad_pre_act, weights_up, ROW_PAIR, preferred_element_type=jnp.float32
    )
    grad_hidden = lax.psum(back_part, "tp") + grad_pre_two
    gain_one = jnp.sum(grad_hidden * normed_one, axis=0)
    shift_one = jnp.sum(grad_hidden, axis=0)
    grad_pre_one = norm_back(grad_hidden * gains[:, 0], normed_one, inverse_one)
    shift_zero = jnp.sum(grad_pre_one, axis=0)
    grad_pre_one_low = grad_pre_one.astype(jnp.bfloat16)
    grad_out = lax.dot_general(
        grad_pre_one_low, context_low, COL_PAIR, preferred_element_type=jnp.float32
    )
    grad_context = jnp.dot(
        grad_pre_one_low, weights_out, preferred_element_type=jnp.float32
    ).astype(jnp.bfloat16)
    grad_context = grad_context.reshape(seq_count, length, num_heads, head_size)
    grad_projected = lax.map(
        attend_back, (queries, key_rows, values, segment_ids, log_total, grad_context)
    )
    grad_projected = grad_projected.reshape(tok_rows, num_heads * 3 * head_size).astype(
        jnp.bfloat16
    )
    head_sums = jnp.sum(grad_projected, axis=0, dtype=jnp.float32).reshape(num_heads, 3, head_size)
    grad_head = jnp.concatenate([head_sums[:, 0].T, head_sums[:, 2].T], axis=0)
    grad_in = lax.dot_general(
        embedded_low, grad_projected, COL_PAIR, preferred_element_type=jnp.float32
    )
    input_part = lax.dot_general(
        grad_projected, weights_in, ROW_PAIR, preferred_element_type=jnp.float32
    )
    input_grad = lax.psum(input_part, "tp") + grad_pre_one
    grad_gains = jnp.stack([gain_one, gain_two], axis=1)
    grad_shifts = jnp.stack([shift_zero, shift_one, shift_two, shift_three], axis=1)
    sent_in, sent_out, sent_up, sent_down, sent_head, sent_unit, sent_gains, sent_shifts = (
        lax.psum_scatter(grad_in, "rows", scatter_dimension=0, tiled=True),
        lax.psum_scatter(grad_out, "rows", scatter_dimension=0, tiled=True),
        lax.psum_scatter(grad_up, "rows", scatter_dimension=0, tiled=True),
        lax.psum_scatter(grad_down, "rows", scatter_dimension=0, tiled=True),
        lax.psum_scatter(grad_head, "rows", scatter_dimension=0, tiled=True),
        lax.psum_scatter(grad_unit, "rows", scatter_dimension=0, tiled=True),
        lax.psum_scatter(grad_gains, "rows", scatter_dimension=0, tiled=True),
        lax.psum_scatter(grad_shifts, "rows", scatter_dimension=0, tiled=True),
    )
    gradients = (
        sent_in,
        sent_out,
        sent_up,
        sent_down,
        sent_head,
        sent_unit,
        sent_gains,
        sent_shifts,
    )
    split_part = reduce(
        add_squares,
        (sent_in, sent_out, sent_up, sent_down, sent_head, sent_unit),
        jnp.zeros((), jnp.float32),
    )
    copied_part = (
        jnp.sum(sent_gains * sent_gains) + jnp.sum(sent_shifts * sent_shifts)
    ) / lax.axis_size("tp")
    grad_norm = jnp.sqrt(lax.psum(split_part + copied_part, ("rows", "tp")))
    factor = CLIP / jnp.maximum(grad_norm, CLIP)
    updated = [
        adam_update(
            masters[position],
            moments[position],
            squares[position],
            gradients[position] * factor,
            RATES[position],
            DECAYS[position],
        )
        for position in range(8)
    ]
    return (
        block_output,
        input_grad,
        grad_norm.reshape(1),
        updated[0][0],
        updated[0][1],
        updated[0][2],
        updated[1][0],
        updated[1][1],
        updated[1][2],
        updated[2][0],
        updated[2][1],
        updated[2][2],
        updated[3][0],
        updated[3][1],
        updated[3][2],
        updated[4][0],
        updated[4][1],
        updated[4][2],
        updated[5][0],
        updated[5][1],
        updated[5][2],
        updated[6][0],
        updated[6][1],
        updated[6][2],
        updated[7][0],
        updated[7][1],
        updated[7][2],
    )


def flip(value, axis):
    return lax.ppermute(value, axis, [(0, 1), (1, 0)])


def turn(value, amount, count):
    return lax.ppermute(value, "z", [(i, (i + amount) % count) for i in range(count)])


def swap_halves(value, swapped):
    half = value.shape[-1] // 2
    return jnp.where(
        swapped, jnp.concatenate([value[..., half:], value[..., :half]], axis=-1), value
    )


def in_order(first, mine, other):
    return jnp.where(
        first, jnp.concatenate([mine, other], axis=0), jnp.concatenate([other, mine], axis=0)
    )


def attend_back_kernel(length, head_size, block, proj_ref, grad_ref, col_ref, row_ref, out_ref, key_sum, value_sum):
    width = 3 * head_size
    keys = proj_ref[0, :, head_size : 2 * head_size]
    values = proj_ref[0, :, 2 * head_size : width]
    key_sum[...] = jnp.zeros_like(key_sum)
    value_sum[...] = jnp.zeros_like(value_sum)
    scale = head_size**-0.5

    def one_block(at, carry):
        rows = pl.ds(pl.multiple_of(at * block, block), block)
        queries = proj_ref[0, rows, 0:head_size] * jnp.bfloat16(scale)
        grads = grad_ref[0, rows, :]
        scores = lax.dot_general(keys, queries, ROW_PAIR, preferred_element_type=jnp.float32)
        scores = jnp.where(col_ref[...] == row_ref[0:1, rows], scores, -1e30)
        highest = jnp.max(scores, axis=0, keepdims=True)
        exponent = jnp.exp(scores - highest)
        probability = exponent * (1.0 / jnp.sum(exponent, axis=0, keepdims=True))
        grad_prob = lax.dot_general(values, grads, ROW_PAIR, preferred_element_type=jnp.float32)
        weighted = jnp.sum(probability * grad_prob, axis=0, keepdims=True)
        grad_score = (probability * (grad_prob - weighted)).astype(jnp.bfloat16)
        value_sum[...] += jnp.dot(
            probability.astype(jnp.bfloat16), grads, preferred_element_type=jnp.float32
        )
        key_sum[...] += jnp.dot(grad_score, queries, preferred_element_type=jnp.float32)
        grad_query = lax.dot_general(grad_score, keys, COL_PAIR, preferred_element_type=jnp.float32)
        out_ref[0, rows, 0:head_size] = (grad_query * scale).astype(jnp.bfloat16)
        return carry

    lax.fori_loop(0, length // block, one_block, 0)
    out_ref[0, :, head_size : 2 * head_size] = key_sum[...].astype(jnp.bfloat16)
    out_ref[0, :, 2 * head_size : width] = value_sum[...].astype(jnp.bfloat16)


def attend_all_back(proj, grad_ctx, segments, head_size):
    heads, length, width = proj.shape
    whole = lambda shape: pl.BlockSpec(shape, lambda h: (0, 0))
    each = lambda shape: pl.BlockSpec((1,) + shape, lambda h: (h, 0, 0))
    return pl.pallas_call(
        partial(attend_back_kernel, length, head_size, 256),
        grid=(heads,),
        in_specs=[
            each((length, width)),
            each((length, head_size)),
            whole((length, 1)),
            whole((1, length)),
        ],
        out_specs=each((length, width)),
        out_shape=jax.ShapeDtypeStruct((heads, length, width), jnp.bfloat16),
        scratch_shapes=[
            pltpu.VMEM((length, head_size), jnp.float32),
            pltpu.VMEM((length, head_size), jnp.float32),
        ],
        compiler_params=pltpu.CompilerParams(vmem_limit_bytes=48 << 20),
        cost_estimate=pl.CostEstimate(
            flops=2 * heads * length * length * 128 * 5,
            bytes_accessed=8 << 20,
            transcendentals=heads * length * length,
        ),
        name="attend_all_back",
    )(proj, grad_ctx, segments[:, None], segments[None, :])


MESH_ID = pl.DeviceIdType.MESH
TILE = 16


class Wires:
    def __init__(self, sends, receives):
        self.sends, self.receives, self.used = sends, receives, 0

    def make(self, source, target, **device):
        at = self.used
        self.used += 1
        return pltpu.make_async_remote_copy(
            src_ref=source,
            dst_ref=target,
            send_sem=self.sends.at[at],
            recv_sem=self.receives.at[at],
            device_id=device,
            device_id_type=MESH_ID,
        )


def spots():
    return (lax.axis_index("x"), lax.axis_index("core"), lax.axis_index("z"), lax.axis_index("y"))


def greet(full):
    at_x, at_core, at_z, at_y = spots()
    barrier = pltpu.get_barrier_semaphore()
    count = 0

    def call(**device):
        pl.semaphore_signal(barrier, inc=1, device_id=device, device_id_type=MESH_ID)

    for step in range(4):
        if step:
            call(z=lax.rem(at_z + step, 4))
            count += 1
        if full or step == 0:
            call(core=1 - at_core, z=lax.rem(at_z + step, 4))
            count += 1
    call(x=1 - at_x)
    call(y=1 - at_y)
    pl.semaphore_wait(barrier, count + 2)


def flipped(value, bit):
    return 1 - value if bit else value


def row_loop(count, step, body):
    def inner(at, carry):
        body(pl.ds(pl.multiple_of(at * step, step), step))
        return carry

    lax.fori_loop(0, count // step, inner, 0)


def block_loop(count, body):
    def inner(at, carry):
        body(at)
        return carry

    lax.fori_loop(0, count, inner, 0)


def dot_f32(left, right, pairing=(((1,), (0,)), ((), ()))):
    return lax.dot_general(left, right, pairing, preferred_element_type=jnp.float32)


def spread_rows(wires, ref, quarter):
    _, at_core, _, at_y = spots()
    own, near = ref.at[pl.ds(0, quarter)], ref.at[pl.ds(quarter, quarter)]
    to_y = wires.make(own, near, y=1 - at_y)
    to_core = wires.make(own, ref.at[pl.ds(2 * quarter, quarter)], core=1 - at_core)
    again = wires.make(near, ref.at[pl.ds(3 * quarter, quarter)], core=1 - at_core)
    to_y.start()
    to_core.start()
    return to_y, to_core, again


def add_rows(wires, part, keep, acc, bufs, fill=None):
    _, at_core, _, at_y = spots()
    send_c, recv_c, send_y, recv_y = bufs
    low = jnp.bfloat16
    half = keep.shape[1] // 2
    sides = [pl.ds(0, half), pl.ds(half, half)]
    far = [wires.make(send_c.at[b], recv_c.at[b], core=1 - at_core) for b in range(2)]
    across = wires.make(send_y, recv_y, y=1 - at_y)
    for b, r in ((1, 3), (0, 2)):
        for side in range(2):
            send_c[b, :, sides[side]] = part(r, side).astype(low)
        far[b].start()
    for side in range(2):
        acc[:, sides[side]] = part(1, side)
    far[1].wait_recv()

    def to_send(rows):
        send_y[rows, :] = (acc[rows, :] + recv_c[1, rows, :].astype(jnp.float32)).astype(low)

    row_loop(keep.shape[0], 32, to_send)
    across.start()
    for side in range(2):
        keep[:, sides[side]] = part(0, side)
    far[0].wait_recv()
    if fill is not None:
        fill()
    across.wait_recv()

    def finish(rows):
        keep[rows, :] += recv_c[0, rows, :].astype(jnp.float32) + recv_y[rows, :].astype(jnp.float32)

    row_loop(keep.shape[0], 32, finish)
    far[0].wait_send()
    far[1].wait_send()
    across.wait_send()


def front_kernel(
    head_piece, up_piece, down_piece, tokens, time_row, ids_col, ids_row,
    w_head, w_up, w_down, emb, proj, ctx, w_out, hid, pre, act, normed_one, inverse_one, hidden, summed, vecs,
    tok, send_c, recv_c, send_y, recv_y, keep, acc, send_sem, recv_sem, local_sem,
):
    at_x, at_core, at_z, at_y = spots()
    low, f32 = jnp.bfloat16, jnp.float32
    length, width = emb.shape
    quarter, half = length // 4, width // 2
    zs = w_head.shape[0]
    span = half + 2 * TILE
    head_size = ctx.shape[2]
    in_size = 3 * head_size
    wires = Wires(send_sem, recv_sem)
    greet(False)

    kept, lent = [], []
    for at, (piece, target) in enumerate(((head_piece, w_head), (up_piece, w_up), (down_piece, w_down))):
        size = piece.shape[1]
        place = target.at[0, 0, pl.ds(pl.multiple_of(at_core * size, size), size)]
        local = pltpu.make_async_copy(piece.at[at_core], place, local_sem.at[at])
        local.start()
        remote = wires.make(piece.at[1 - at_core], place, core=1 - at_core)
        remote.start()
        kept.append(local)
        lent.append(remote)
    turns, cross = [], []
    for target in (w_head, w_up, w_down):
        turns.append(
            [None]
            + [wires.make(target.at[0, 0], target.at[s, 0], z=lax.rem(at_z + s, zs)) for s in range(1, zs)]
        )
        cross.append([wires.make(target.at[s, 0], target.at[s, 1], x=1 - at_x) for s in range(zs)])

    holds = at_core == lax.div(at_z, 2)
    start = lax.rem(at_z, 2) * length
    here, there = [], []
    for r in range(4):
        for h in range(2):
            spot = tok.at[pl.ds(r * quarter, quarter), pl.ds(pl.multiple_of(flipped(at_x, h) * half, half), half)]

            def source(core):
                at = flipped(core, r // 2) * 2 + flipped(at_y, r % 2)
                return tokens.at[pl.ds(pl.multiple_of(start + at * quarter, quarter), quarter), pl.ds(h * half, half)]

            here.append(pltpu.make_async_copy(source(at_core), spot, local_sem.at[3 + 2 * r + h]))
            there.append(wires.make(source(1 - at_core), spot, core=1 - at_core))

    @pl.when(holds)
    def _():
        for near, far in zip(here, there):
            near.start()
            far.start()

    for at in range(3):
        kept[at].wait()
        lent[at].wait_recv()
        for s in range(1, zs):
            turns[at][s].start()
        if at == 0:
            cross[0][0].start()

    @pl.when(holds)
    def _():
        for near in here:
            near.wait()

    @pl.when(jnp.logical_not(holds))
    def _():
        for far in there:
            far.wait_recv()

    def embed(rows):
        emb[rows, :] = (tok[rows, :].astype(f32) + time_row[...]).astype(low)

    row_loop(length, 32, embed)

    def forward(at, s):
        turns[at][s].wait_recv()
        cross[at][s].start()

    def small(s, side):
        size = half // 2 + TILE
        return (
            w_head[s, side, half // 2 : size, :].astype(f32)
            + w_head[s, side, size + half // 2 : 2 * size, :].astype(f32)
        )

    for s in range(zs):
        if s + 1 < zs:
            forward(0, s + 1)
        if s == 2:
            cross[1][0].start()
            cross[2][0].start()
        cross[0][s].wait_recv()
        bias = (small(s, 0) + small(s, 1))[0:1, :in_size]
        size = half // 2 + TILE

        def project(rows):
            total = bias
            for side in range(2):
                for core in range(2):
                    at = side * half + core * (half // 2)
                    total = total + dot_f32(
                        emb[rows, at : at + half // 2],
                        w_head[s, side, core * size : core * size + half // 2, :],
                    )[:, :in_size]
            proj[s, rows, :] = total.astype(low)

        row_loop(length, quarter, project)
        for side in range(2):
            for core in range(2):
                w_out[side, core * (half // 2) : (core + 1) * (half // 2), s * head_size : (s + 1) * head_size] = w_head[
                    s, side, core * size : core * size + half // 2, in_size:
                ]
        keys = proj[s, :, head_size : 2 * head_size]
        values = proj[s, :, 2 * head_size : in_size]

        def attend(rows):
            queries = proj[s, rows, 0:head_size] * jnp.bfloat16(head_size**-0.5)
            scores = dot_f32(queries, keys, ROW_PAIR)
            scores = jnp.where(ids_col[rows, :] == ids_row[...], scores, -1e30)
            highest = jnp.max(scores, axis=1, keepdims=True)
            exponent = jnp.exp(scores - highest)
            totals = jnp.sum(exponent, axis=1, keepdims=True)
            probability = (exponent * (1.0 / totals)).astype(low)
            ctx[s, rows, :] = dot_f32(probability, values).astype(low)

        row_loop(length, quarter, attend)

    for side in range(2):
        tile = small(0, side)
        for k in range(6):
            vecs[k : k + 1, side * half : side * half + half // 2] = tile[2 + k : 3 + k, :]
            vecs[k : k + 1, side * half + half // 2 : (side + 1) * half] = tile[8 + k : 9 + k, :]

    for s in range(1, zs):
        forward(1, s)
    bufs = (send_c, recv_c, send_y, recv_y)

    def mixed_part(r, side):
        joined = jnp.concatenate([ctx[s, r * quarter : (r + 1) * quarter, :] for s in range(zs)], axis=1)
        return dot_f32(joined, w_out[side], ROW_PAIR)

    add_rows(wires, mixed_part, keep, acc, bufs)

    def first_norm(rows):
        total = tok[rows, :].astype(f32) + time_row[...] + keep[rows, :] + vecs[2:3, :]
        normed, inverse = norm_stats(total)
        normed_one[rows, :] = normed
        inverse_one[rows, :] = inverse
        value = normed * vecs[0:1, :] + vecs[3:4, :]
        hidden[rows, :] = value
        hid[rows, :] = value.astype(low)

    row_loop(quarter, 32, first_norm)
    to_y, to_core, again = spread_rows(wires, hid, quarter)
    for s in range(1, zs):
        forward(2, s)
    for s in range(zs):
        cross[1][s].wait_recv()

    def up(r):
        rows = pl.ds(r * quarter, quarter)

        def one(s):
            lanes = pl.ds(pl.multiple_of(s * (half // 2), half // 2), half // 2)
            shift = (small(s, 0) + small(s, 1))[1:2, :]
            value = dot_f32(hid[rows, 0:half], w_up[s, 0]) + dot_f32(hid[rows, half:], w_up[s, 1]) + shift
            pre[rows, lanes] = value
            act[rows, lanes] = gelu_value(value).astype(low)

        block_loop(zs, one)

    up(0)
    to_core.wait_recv()
    up(2)
    to_y.wait_recv()
    again.start()
    up(1)
    again.wait_recv()
    up(3)
    for s in range(zs):
        cross[2][s].wait_recv()

    def down_part(r, side):
        rows = pl.ds(r * quarter, quarter)
        total = dot_f32(act[rows, 0 : half // 2], w_down[0, side], ROW_PAIR)
        for s in range(1, zs):
            total = total + dot_f32(act[rows, s * (half // 2) : (s + 1) * (half // 2)], w_down[s, side], ROW_PAIR)
        return total

    add_rows(wires, down_part, keep, acc, bufs)

    def second(rows):
        summed[rows, :] = hidden[rows, :] + keep[rows, :] + vecs[4:5, :]

    row_loop(quarter, 32, second)
    for at in range(3):
        lent[at].wait_send()
        for s in range(zs):
            if s:
                turns[at][s].wait_send()
            cross[at][s].wait_send()

    @pl.when(holds)
    def _():
        for far in there:
            far.wait_send()

    for member in (to_y, to_core, again):
        member.wait_send()


def run_front(pieces, tokens, time_row, ids, head_size):
    low, f32 = jnp.bfloat16, jnp.float32
    length, width = ids.shape[0], tokens.shape[1]
    quarter, half, zs = length // 4, width // 2, 4
    blocks = pieces[1].shape[2]
    vmem = pl.BlockSpec(memory_space=pltpu.VMEM)
    shapes = [
        ((zs, 2, half + 2 * TILE, 4 * head_size), low),
        ((zs, 2, half, blocks), low),
        ((zs, 2, half, blocks), low),
        ((length, width), low),
        ((zs, length, 3 * head_size), low),
        ((zs, length, head_size), low),
        ((2, half, zs * head_size), low),
        ((length, width), low),
        ((length, zs * blocks), f32),
        ((length, zs * blocks), low),
        ((quarter, width), f32),
        ((quarter, 1), f32),
        ((quarter, width), f32),
        ((quarter, width), f32),
        ((8, width), f32),
    ]
    return pl.pallas_call(
        front_kernel,
        out_shape=[jax.ShapeDtypeStruct(*s) for s in shapes],
        in_specs=[vmem] * 3 + [pl.BlockSpec(memory_space=pl.ANY)] + [vmem] * 3,
        out_specs=[vmem] * len(shapes),
        scratch_shapes=[
            pltpu.VMEM((length, width), low),
            pltpu.VMEM((2, quarter, width), low),
            pltpu.VMEM((2, quarter, width), low),
            pltpu.VMEM((quarter, width), low),
            pltpu.VMEM((quarter, width), low),
            pltpu.VMEM((quarter, width), f32),
            pltpu.VMEM((quarter, width), f32),
            pltpu.SemaphoreType.DMA((64,)),
            pltpu.SemaphoreType.DMA((64,)),
            pltpu.SemaphoreType.DMA((16,)),
        ],
        compiler_params=pltpu.CompilerParams(
            collective_id=0, has_side_effects=True, vmem_limit_bytes=60 << 20
        ),
        name="front",
    )(*pieces, tokens, time_row, ids[:, None], ids[None, :])


def spread_tokens(own):
    near = flip(own, "y")
    pair = jnp.concatenate([own, near], axis=0)
    return jnp.concatenate([pair, flip(pair, "core")], axis=0)


def sum_tokens(left, right, pairing):
    half = left.shape[0] // 2
    far = lax.dot_general(left[half:], right, pairing, preferred_element_type=jnp.float32)
    came = flip(far.astype(jnp.bfloat16), "core")
    near = lax.dot_general(left[:half], right, pairing, preferred_element_type=jnp.float32)
    near = near + came.astype(jnp.float32)
    quarter = half // 2
    return near[:quarter] + flip(near[quarter:].astype(jnp.bfloat16), "y").astype(jnp.float32)


def spread_output(own, zs, dtype):
    count = 4
    at_z, at_y = lax.axis_index("z"), lax.axis_index("y")
    quarter, width = own.shape
    result = jnp.zeros((2 * count * quarter, width), dtype)
    for step in range(count):
        pairs = []
        for core in range(2):
            for place in range(count):
                index = core * 2 + place % 2
                target = (place // 2) * count + (index + step) % count
                pairs.append((core * count + place, target))
        came = lax.ppermute(own, ("core", "z"), pairs)
        crossed = flip(came, "y")
        index = (at_z - step) % count
        start = (index % 2) * count + (index // 2) * 2
        result = lax.dynamic_update_slice(
            result, came.astype(dtype), ((start + at_y) * quarter, 0)
        )
        result = lax.dynamic_update_slice(
            result, crossed.astype(dtype), ((start + 1 - at_y) * quarter, 0)
        )
    return result


def sum_scalar(value):
    value = jnp.broadcast_to(value, (8, 128))
    for axis in ("core", "y", "x"):
        value = value + flip(value, axis)
    value = value + lax.ppermute(value, "z", [(0, 1), (1, 0), (2, 3), (3, 2)])
    value = value + lax.ppermute(value, "z", [(0, 3), (3, 0), (1, 2), (2, 1)])
    return value[0, 0]


def on_grid(*arguments):
    tokens, time_embed, segment_ids, cotangent = arguments[:4]
    masters, moments, squares = arguments[4::3], arguments[5::3], arguments[6::3]
    input_weight, output_weight, upward_weight, downward_weight = masters[:4]
    head_bias, hidden_bias, norm_gains, branch_biases = masters[4:]
    at_x, at_core = lax.axis_index("x"), lax.axis_index("core")
    at_z, at_y = lax.axis_index("z"), lax.axis_index("y")
    first_core, first_x = at_core == 0, at_x == 0
    swapped = at_x == 1
    low = jnp.bfloat16
    f32 = jnp.float32
    length = segment_ids.shape[1]
    head_size = head_bias.shape[0] * 4 // 2
    zs = 4
    place = at_core * 2 + at_y
    quarter = length // 4

    rows = input_weight.shape[0]
    wide = upward_weight.shape[1] // 2
    packed = 4 * head_size
    small_rows = head_bias.shape[0]

    position = at_x * 2 + at_core
    vectors = jnp.concatenate([norm_gains, branch_biases], axis=1).T
    vectors = lax.dynamic_update_slice(
        jnp.zeros((TILE, rows), f32), vectors, (2 + 6 * at_core, 0)
    )

    def head_piece(half):
        body = jnp.concatenate(
            [
                input_weight[:, half * 3 * head_size : (half + 1) * 3 * head_size],
                output_weight[:, half * head_size : (half + 1) * head_size],
            ],
            axis=1,
        )
        tile = lax.dynamic_update_slice(
            vectors, head_bias[:, half][None], (0, at_x * 2 * head_size + at_core * small_rows)
        )
        units = lax.dynamic_update_slice(
            jnp.zeros((2, 4 * small_rows), f32),
            hidden_bias[:, 2 * half : 2 * half + 2].T,
            (0, position * small_rows),
        )
        tile = lax.dynamic_update_slice(tile, units.reshape(1, -1), (1, 0))
        return jnp.concatenate([body, tile], axis=0)

    pieces = [
        jnp.stack([head_piece(0), head_piece(1)]).astype(low),
        jnp.stack([upward_weight[:, :wide], upward_weight[:, wide:]]).astype(low),
        jnp.stack([downward_weight[:, :wide], downward_weight[:, wide:]]).astype(low),
    ]

    seat = ("core", "z")
    holds = at_core == at_z // 2
    lend = [((i // 2) * zs + i, (1 - i // 2) * zs + i) for i in range(zs)]

    def borrow(kept, sent):
        return jnp.where(holds, kept, lax.ppermute(sent, seat, lend))

    local = at_z % 2
    own_time = lax.dynamic_slice_in_dim(time_embed, local, 1, 0)
    own_time = borrow(own_time, own_time)
    own_ids = lax.dynamic_slice_in_dim(segment_ids, local, 1, 0)
    own_ids = borrow(own_ids, own_ids)[0]

    def at_quarter(which):
        return lax.dynamic_slice_in_dim(cotangent, local * length + which * quarter, quarter, 0)

    upstream = borrow(at_quarter(place), at_quarter(place ^ 2))
    upstream = swap_halves(upstream, swapped).astype(f32)

    def relative(values):
        return jnp.concatenate(
            [lax.dynamic_slice_in_dim(values, (place ^ turnover) * quarter, quarter, 0) for turnover in range(4)],
            axis=0,
        )

    time_row = swap_halves(own_time.astype(f32), swapped)
    segments = relative(own_ids)

    span = 2 * rows
    (
        weights_head, weights_up, weights_down, embedded_low, projected, context, weights_out, hidden_low,
        pre_act, expanded_low, normed_one, inverse_one, hidden, summed_two, vectors,
    ) = run_front(pieces, tokens, time_row, segments, head_size)
    gains, shifts = vectors[0:2], vectors[2:6]
    body = jnp.concatenate(
        [weights_head[:, :, :rows], weights_head[:, :, rows + TILE : 2 * rows + TILE]], axis=2
    ).reshape(zs, 2 * span, packed)
    weights_in = jnp.concatenate([body[i, :, : 3 * head_size] for i in range(zs)], axis=1)
    weights_out = weights_out.reshape(2 * span, zs * head_size)
    context_low = jnp.concatenate([context[i] for i in range(zs)], axis=1)

    def joined(blocks):
        return jnp.concatenate([blocks[i].reshape(2 * span, wide) for i in range(zs)], axis=1)

    weights_up, weights_down = joined(weights_up), joined(weights_down)
    normed_two, inverse_two = norm_stats(summed_two)
    out = swap_halves((normed_two * gains[1] + shifts[3]).astype(low), swapped)
    block_output = spread_output(out, zs, low)

    gain_two = jnp.sum(upstream * normed_two, axis=0)
    shift_three = jnp.sum(upstream, axis=0)
    grad_pre_two = norm_back(upstream * gains[1], normed_two, inverse_two)
    shift_two = jnp.sum(grad_pre_two, axis=0)
    grad_two_low = spread_tokens(grad_pre_two.astype(low))
    grad_down = lax.dot_general(grad_two_low, expanded_low, COL_PAIR, preferred_element_type=f32)
    grad_act = jnp.dot(grad_two_low, weights_down, preferred_element_type=f32)
    grad_pre_act = (grad_act * gelu_slope(pre_act)).astype(low)
    unit_sums = jnp.sum(grad_pre_act, axis=0, dtype=f32)
    back = sum_tokens(grad_pre_act, weights_up, ROW_PAIR)
    grad_up = lax.dot_general(hidden_low, grad_pre_act, COL_PAIR, preferred_element_type=f32)
    grad_hidden = back + grad_pre_two
    gain_one = jnp.sum(grad_hidden * normed_one, axis=0)
    shift_one = jnp.sum(grad_hidden, axis=0)
    grad_pre_one = norm_back(grad_hidden * gains[0], normed_one, inverse_one)
    shift_zero = jnp.sum(grad_pre_one, axis=0)
    grad_one_low = spread_tokens(grad_pre_one.astype(low))
    grad_context = jnp.dot(grad_one_low, weights_out, preferred_element_type=f32).astype(low)
    grad_context = jnp.stack(
        [grad_context[:, i * head_size : (i + 1) * head_size] for i in range(zs)]
    )
    grad_out = lax.dot_general(grad_one_low, context_low, COL_PAIR, preferred_element_type=f32)
    grad_heads = attend_all_back(projected, grad_context, segments, head_size)
    grad_projected = jnp.concatenate([grad_heads[i] for i in range(zs)], axis=1)
    input_part = sum_tokens(grad_projected, weights_in, ROW_PAIR)
    input_grad = swap_halves((input_part + grad_pre_one).astype(low), swapped)
    input_grad = spread_output(input_grad, zs, f32)
    grad_in = lax.dot_general(embedded_low, grad_projected, COL_PAIR, preferred_element_type=f32)
    head_sums = jnp.sum(grad_projected, axis=0, dtype=f32).reshape(zs, 3, head_size)

    def collect(own, far):
        near = [
            (a + flip(b.astype(low), "x").astype(f32)) for a, b in zip(own, far)
        ]
        total = near[0]
        for step in range(1, zs):
            total = total + turn(near[step].astype(low), -step, zs).astype(f32)
        return total

    def return_cores(block):
        half = block.shape[0] // 2
        mine = jnp.where(first_core, block[:half], block[half:])
        sent = jnp.where(first_core, block[half:], block[:half])
        came = flip(sent.astype(low), "core").astype(f32)
        return jnp.where(first_core, mine, came), jnp.where(first_core, came, mine)

    def split_blocks(grad):
        parts = [grad[:, i * wide : (i + 1) * wide] for i in range(zs)]
        return [p[:span] for p in parts], [p[span:] for p in parts]

    total_down = collect(*split_blocks(grad_down))
    total_up = collect(*split_blocks(grad_up))
    head_near, head_distant = [], []
    units = unit_sums.reshape(zs, 2, 2, 2 * small_rows)
    for i in range(zs):
        whole = jnp.concatenate(
            [
                grad_in[:, i * 3 * head_size : (i + 1) * 3 * head_size],
                grad_out[:, i * head_size : (i + 1) * head_size],
            ],
            axis=1,
        )
        lower = jnp.concatenate([head_sums[i, 0][None], units[i, :, 0]], axis=0)
        upper = jnp.concatenate([head_sums[i, 2][None], units[i, :, 1]], axis=0)
        kept = jnp.where(first_x, lower, upper)
        sent = jnp.where(first_x, upper, lower)
        pad = ((0, 13), (0, packed - 2 * small_rows))
        head_near.append(jnp.concatenate([whole[:span], jnp.pad(kept, pad)], axis=0))
        head_distant.append(jnp.concatenate([whole[span:], jnp.pad(sent, pad)], axis=0))
    total_head = collect(head_near, head_distant)
    small_total = total_head[span : span + 3]
    small_total = jnp.concatenate(
        [small_total[:, :small_rows], small_total[:, small_rows : 2 * small_rows]], axis=0
    )
    tail = jnp.pad(small_total, ((0, 0), (0, packed - small_rows)))
    head_zero, head_one = return_cores(
        jnp.concatenate(
            [
                total_head[:rows],
                jnp.pad(tail[:3], ((0, 13), (0, 0))),
                total_head[rows:span],
                jnp.pad(tail[3:], ((0, 13), (0, 0))),
            ],
            axis=0,
        )
    )
    up_zero, up_one = return_cores(total_up)
    down_zero, down_one = return_cores(total_down)
    in_size = 3 * head_size
    sent_in = jnp.concatenate([head_zero[:rows, :in_size], head_one[:rows, :in_size]], axis=1)
    sent_out = jnp.concatenate([head_zero[:rows, in_size:], head_one[:rows, in_size:]], axis=1)
    sent_up = jnp.concatenate([up_zero, up_one], axis=1)
    sent_down = jnp.concatenate([down_zero, down_one], axis=1)
    tails = [member[rows : rows + 3, :small_rows].T for member in (head_zero, head_one)]
    sent_head = jnp.concatenate([tails[0][:, :1], tails[1][:, :1]], axis=1)
    sent_unit = jnp.concatenate([tails[0][:, 1:], tails[1][:, 1:]], axis=1)

    feature = jnp.stack([gain_one, gain_two, shift_zero, shift_one, shift_two, shift_three])
    feature = jnp.pad(feature, ((0, 2), (0, 0)))
    for axis in ("core", "y"):
        feature = feature + flip(feature, axis)
    feature = feature + lax.ppermute(feature, "z", [(0, 1), (1, 0), (2, 3), (3, 2)])
    feature = feature + lax.ppermute(feature, "z", [(0, 3), (3, 0), (1, 2), (2, 1)])
    feature = feature[:, :span] + flip(feature[:, span:], "x")
    feature = jnp.where(first_core, feature[:, :rows], feature[:, rows:])
    sent_gains, sent_shifts = feature[0:2].T, feature[2:6].T

    gradients = (sent_in, sent_out, sent_up, sent_down, sent_head, sent_unit, sent_gains, sent_shifts)
    split_part = reduce(add_squares, gradients[:6], jnp.zeros((), f32))
    copied_part = reduce(add_squares, gradients[6:], jnp.zeros((), f32)) / (
        lax.axis_size("z") * lax.axis_size("y")
    )
    grad_norm = jnp.sqrt(sum_scalar(split_part + copied_part))
    factor = CLIP / jnp.maximum(grad_norm, CLIP)
    results = [block_output, input_grad, grad_norm.reshape(1)]
    for position in range(8):
        results += adam_update(
            masters[position],
            moments[position],
            squares[position],
            gradients[position] * factor,
            RATES[position],
            DECAYS[position],
        )
    return tuple(results)


def solution(mesh):
    plain = mesh.shape["rows"] != 4 or mesh.shape["tp"] != 8
    if plain:
        rows, tp = "rows", "tp"
        grid, work = mesh, on_device
    else:
        rows, tp = ("x", "core"), ("z", "y")
        grid = Mesh(mesh.devices.reshape(2, 2, 4, 2), ("x", "core", "z", "y"))
        work = on_grid
    narrow, split = P(rows, None), P(rows, tp)
    return jax.shard_map(
        work,
        mesh=grid,
        in_specs=(narrow,) * 4 + (split,) * 18 + (narrow,) * 6,
        out_specs=(narrow, narrow, P()) + (split,) * 18 + (narrow,) * 6,
        check_vma=False,
    )
```

```python
from functools import partial, reduce

import jax
import jax.numpy as jnp
from jax import lax
from jax.experimental import pallas as pl
from jax.experimental.pallas import tpu as pltpu
from jax.sharding import Mesh
from jax.sharding import PartitionSpec as P

HD = 64
STEP = 10


NORM_EPS = 1e-05
BETA_ONE = 0.9
BETA_TWO = 0.999
ADAM_EPS = 1e-08
CLIP = 1.0
RATES = (0.1, 0.4, 0.1, 0.05, 0.5, 0.5, 0.5, 0.5)
DECAYS = (0.01, 0.01, 0.01, 0.01, 0.0, 0.0, 0.0, 0.0)
ROW_PAIR = (((1,), (1,)), ((), ()))
COL_PAIR = (((0,), (0,)), ((), ()))


def norm_stats(summed):
    average = jnp.mean(summed, axis=-1, keepdims=True)
    centered = summed - average
    inverse = lax.rsqrt(jnp.mean(centered * centered, axis=-1, keepdims=True) + NORM_EPS)
    return (centered * inverse, inverse)


def norm_back(grad_normed, normed, inverse):
    first_mean = jnp.mean(grad_normed, axis=-1, keepdims=True)
    second_mean = jnp.mean(grad_normed * normed, axis=-1, keepdims=True)
    return inverse * (grad_normed - first_mean - normed * second_mean)


def gelu_value(inputs):
    return 0.5 * inputs * (1.0 + jax.scipy.special.erf(inputs * 0.7071067811865476))


def gelu_slope(inputs):
    cumulative = 0.5 * (1.0 + jax.scipy.special.erf(inputs * 0.7071067811865476))
    return cumulative + inputs * jnp.exp(-0.5 * inputs * inputs) * 0.3989422804014327


def masked_scores(queries, key_rows, segments):
    scores = jnp.einsum(
        "qhd,khd->hqk", queries, key_rows, preferred_element_type=jnp.float32
    ) * HD ** (-0.5)
    matching = segments[:, None] == segments[None, :]
    return jnp.where(matching[None], scores, -1e30)


def attend_forward(pieces):
    queries, key_rows, values, segments = pieces
    scores = masked_scores(queries, key_rows, segments)
    highest = jnp.max(scores, axis=-1, keepdims=True)
    exponent = jnp.exp(scores - highest)
    totals = jnp.sum(exponent, axis=-1, keepdims=True)
    probability = (exponent / totals).astype(jnp.bfloat16)
    context = jnp.einsum("hqk,khd->qhd", probability, values, preferred_element_type=jnp.float32)
    return (context, (highest + jnp.log(totals))[..., 0])


def attend_back(pieces):
    queries, key_rows, values, segments, log_total, grad_context = pieces
    scores = masked_scores(queries, key_rows, segments)
    probability = jnp.exp(scores - log_total[..., None])
    grad_prob = jnp.einsum("qhd,khd->hqk", grad_context, values, preferred_element_type=jnp.float32)
    weighted = jnp.sum(probability * grad_prob, axis=-1, keepdims=True)
    grad_score = (probability * (grad_prob - weighted)).astype(jnp.bfloat16)
    grad_query = jnp.einsum(
        "hqk,khd->qhd", grad_score, key_rows, preferred_element_type=jnp.float32
    ) * HD ** (-0.5)
    grad_key = jnp.einsum(
        "hqk,qhd->khd", grad_score, queries, preferred_element_type=jnp.float32
    ) * HD ** (-0.5)
    grad_value = jnp.einsum(
        "hqk,qhd->khd",
        probability.astype(jnp.bfloat16),
        grad_context,
        preferred_element_type=jnp.float32,
    )
    return jnp.stack([grad_query, grad_key, grad_value], axis=2)


def adam_update(weight, moment, square, clipped, rate, decay):
    moment = BETA_ONE * moment + (1.0 - BETA_ONE) * clipped
    square = BETA_TWO * square + (1.0 - BETA_TWO) * clipped * clipped
    corrected = (
        moment / (1.0 - BETA_ONE**STEP) / (jnp.sqrt(square / (1.0 - BETA_TWO**STEP)) + ADAM_EPS)
    )
    return (weight - rate * (corrected + decay * weight), moment, square)


def add_squares(running, member):
    return running + jnp.sum(member * member)


def on_device(
    tokens,
    time_embed,
    segment_ids,
    cotangent,
    input_weight,
    input_moment,
    input_square,
    output_weight,
    output_moment,
    output_square,
    upward_weight,
    upward_moment,
    upward_square,
    downward_weight,
    downward_moment,
    downward_square,
    head_bias,
    head_moment,
    head_square,
    hidden_bias,
    hidden_moment,
    hidden_square,
    norm_gains,
    gains_moment,
    gains_square,
    branch_biases,
    biases_moment,
    biases_square,
):
    masters = (
        input_weight,
        output_weight,
        upward_weight,
        downward_weight,
        head_bias,
        hidden_bias,
        norm_gains,
        branch_biases,
    )
    moments = (
        input_moment,
        output_moment,
        upward_moment,
        downward_moment,
        head_moment,
        hidden_moment,
        gains_moment,
        biases_moment,
    )
    squares = (
        input_square,
        output_square,
        upward_square,
        downward_square,
        head_square,
        hidden_square,
        gains_square,
        biases_square,
    )
    (
        weights_in,
        weights_out,
        weights_up,
        weights_down,
        head_shift,
        unit_shift,
        gains_low,
        shifts_low,
    ) = (
        lax.all_gather(input_weight.astype(jnp.bfloat16), "rows", axis=0, tiled=True),
        lax.all_gather(output_weight.astype(jnp.bfloat16), "rows", axis=0, tiled=True),
        lax.all_gather(upward_weight.astype(jnp.bfloat16), "rows", axis=0, tiled=True),
        lax.all_gather(downward_weight.astype(jnp.bfloat16), "rows", axis=0, tiled=True),
        lax.all_gather(head_bias.astype(jnp.bfloat16), "rows", axis=0, tiled=True),
        lax.all_gather(hidden_bias.astype(jnp.bfloat16), "rows", axis=0, tiled=True),
        lax.all_gather(norm_gains.astype(jnp.bfloat16), "rows", axis=0, tiled=True),
        lax.all_gather(branch_biases.astype(jnp.bfloat16), "rows", axis=0, tiled=True),
    )
    seq_count, length = segment_ids.shape
    width = tokens.shape[1]
    num_heads = head_shift.shape[1]
    head_size = head_shift.shape[0] // 2
    tok_rows = seq_count * length
    gains = gains_low.astype(jnp.float32)
    shifts = shifts_low.astype(jnp.float32)
    embedded = (
        tokens.astype(jnp.float32).reshape(seq_count, length, width)
        + time_embed.astype(jnp.float32)[:, None, :]
    ).reshape(tok_rows, width)
    embedded_low = embedded.astype(jnp.bfloat16)
    head_float = head_shift.astype(jnp.float32)
    offset = jnp.stack(
        [
            head_float[:head_size].T,
            jnp.zeros((num_heads, head_size), jnp.float32),
            head_float[head_size:].T,
        ],
        axis=1,
    )
    projected = jnp.dot(embedded_low, weights_in, preferred_element_type=jnp.float32).reshape(
        tok_rows, num_heads, 3, head_size
    )
    projected = (
        (projected + offset)
        .astype(jnp.bfloat16)
        .reshape(seq_count, length, num_heads, 3, head_size)
    )
    queries = projected[:, :, :, 0]
    key_rows = projected[:, :, :, 1]
    values = projected[:, :, :, 2]
    context, log_total = lax.map(attend_forward, (queries, key_rows, values, segment_ids))
    context_low = context.reshape(tok_rows, num_heads * head_size).astype(jnp.bfloat16)
    mixed_part = lax.dot_general(
        context_low, weights_out, ROW_PAIR, preferred_element_type=jnp.float32
    )
    mixed = lax.psum(mixed_part, "tp")
    normed_one, inverse_one = norm_stats(embedded + mixed + shifts[:, 0])
    hidden = normed_one * gains[:, 0] + shifts[:, 1]
    hidden_low = hidden.astype(jnp.bfloat16)
    unit_offset = unit_shift.astype(jnp.float32).T.reshape(-1)
    pre_act = jnp.dot(hidden_low, weights_up, preferred_element_type=jnp.float32) + unit_offset
    expanded_low = gelu_value(pre_act).astype(jnp.bfloat16)
    reduced_part = lax.dot_general(
        expanded_low, weights_down, ROW_PAIR, preferred_element_type=jnp.float32
    )
    reduced = lax.psum(reduced_part, "tp")
    normed_two, inverse_two = norm_stats(hidden + reduced + shifts[:, 2])
    block_output = (normed_two * gains[:, 1] + shifts[:, 3]).astype(jnp.bfloat16)
    upstream = cotangent.astype(jnp.float32)
    gain_two = jnp.sum(upstream * normed_two, axis=0)
    shift_three = jnp.sum(upstream, axis=0)
    grad_pre_two = norm_back(upstream * gains[:, 1], normed_two, inverse_two)
    shift_two = jnp.sum(grad_pre_two, axis=0)
    grad_pre_two_low = grad_pre_two.astype(jnp.bfloat16)
    grad_down = lax.dot_general(
        grad_pre_two_low, expanded_low, COL_PAIR, preferred_element_type=jnp.float32
    )
    grad_act = jnp.dot(grad_pre_two_low, weights_down, preferred_element_type=jnp.float32)
    grad_pre_act = (grad_act * gelu_slope(pre_act)).astype(jnp.bfloat16)
    unit_sums = jnp.sum(grad_pre_act, axis=0, dtype=jnp.float32)
    grad_unit = unit_sums.reshape(-1, 2 * head_size).T
    grad_up = lax.dot_general(
        hidden_low, grad_pre_act, COL_PAIR, preferred_element_type=jnp.float32
    )
    back_part = lax.dot_general(
        grad_pre_act, weights_up, ROW_PAIR, preferred_element_type=jnp.float32
    )
    grad_hidden = lax.psum(back_part, "tp") + grad_pre_two
    gain_one = jnp.sum(grad_hidden * normed_one, axis=0)
    shift_one = jnp.sum(grad_hidden, axis=0)
    grad_pre_one = norm_back(grad_hidden * gains[:, 0], normed_one, inverse_one)
    shift_zero = jnp.sum(grad_pre_one, axis=0)
    grad_pre_one_low = grad_pre_one.astype(jnp.bfloat16)
    grad_out = lax.dot_general(
        grad_pre_one_low, context_low, COL_PAIR, preferred_element_type=jnp.float32
    )
    grad_context = jnp.dot(
        grad_pre_one_low, weights_out, preferred_element_type=jnp.float32
    ).astype(jnp.bfloat16)
    grad_context = grad_context.reshape(seq_count, length, num_heads, head_size)
    grad_projected = lax.map(
        attend_back, (queries, key_rows, values, segment_ids, log_total, grad_context)
    )
    grad_projected = grad_projected.reshape(tok_rows, num_heads * 3 * head_size).astype(
        jnp.bfloat16
    )
    head_sums = jnp.sum(grad_projected, axis=0, dtype=jnp.float32).reshape(num_heads, 3, head_size)
    grad_head = jnp.concatenate([head_sums[:, 0].T, head_sums[:, 2].T], axis=0)
    grad_in = lax.dot_general(
        embedded_low, grad_projected, COL_PAIR, preferred_element_type=jnp.float32
    )
    input_part = lax.dot_general(
        grad_projected, weights_in, ROW_PAIR, preferred_element_type=jnp.float32
    )
    input_grad = lax.psum(input_part, "tp") + grad_pre_one
    grad_gains = jnp.stack([gain_one, gain_two], axis=1)
    grad_shifts = jnp.stack([shift_zero, shift_one, shift_two, shift_three], axis=1)
    sent_in, sent_out, sent_up, sent_down, sent_head, sent_unit, sent_gains, sent_shifts = (
        lax.psum_scatter(grad_in, "rows", scatter_dimension=0, tiled=True),
        lax.psum_scatter(grad_out, "rows", scatter_dimension=0, tiled=True),
        lax.psum_scatter(grad_up, "rows", scatter_dimension=0, tiled=True),
        lax.psum_scatter(grad_down, "rows", scatter_dimension=0, tiled=True),
        lax.psum_scatter(grad_head, "rows", scatter_dimension=0, tiled=True),
        lax.psum_scatter(grad_unit, "rows", scatter_dimension=0, tiled=True),
        lax.psum_scatter(grad_gains, "rows", scatter_dimension=0, tiled=True),
        lax.psum_scatter(grad_shifts, "rows", scatter_dimension=0, tiled=True),
    )
    gradients = (
        sent_in,
        sent_out,
        sent_up,
        sent_down,
        sent_head,
        sent_unit,
        sent_gains,
        sent_shifts,
    )
    split_part = reduce(
        add_squares,
        (sent_in, sent_out, sent_up, sent_down, sent_head, sent_unit),
        jnp.zeros((), jnp.float32),
    )
    copied_part = (
        jnp.sum(sent_gains * sent_gains) + jnp.sum(sent_shifts * sent_shifts)
    ) / lax.axis_size("tp")
    grad_norm = jnp.sqrt(lax.psum(split_part + copied_part, ("rows", "tp")))
    factor = CLIP / jnp.maximum(grad_norm, CLIP)
    updated = [
        adam_update(
            masters[position],
            moments[position],
            squares[position],
            gradients[position] * factor,
            RATES[position],
            DECAYS[position],
        )
        for position in range(8)
    ]
    return (
        block_output,
        input_grad,
        grad_norm.reshape(1),
        updated[0][0],
        updated[0][1],
        updated[0][2],
        updated[1][0],
        updated[1][1],
        updated[1][2],
        updated[2][0],
        updated[2][1],
        updated[2][2],
        updated[3][0],
        updated[3][1],
        updated[3][2],
        updated[4][0],
        updated[4][1],
        updated[4][2],
        updated[5][0],
        updated[5][1],
        updated[5][2],
        updated[6][0],
        updated[6][1],
        updated[6][2],
        updated[7][0],
        updated[7][1],
        updated[7][2],
    )


def flip(value, axis):
    return lax.ppermute(value, axis, [(0, 1), (1, 0)])


def turn(value, amount, count):
    return lax.ppermute(value, "z", [(i, (i + amount) % count) for i in range(count)])


def swap_halves(value, swapped):
    half = value.shape[-1] // 2
    return jnp.where(
        swapped, jnp.concatenate([value[..., half:], value[..., :half]], axis=-1), value
    )


def in_order(first, mine, other):
    return jnp.where(
        first, jnp.concatenate([mine, other], axis=0), jnp.concatenate([other, mine], axis=0)
    )


MESH_ID = pl.DeviceIdType.MESH
TILE = 16


class Wires:
    def __init__(self, sends, receives):
        self.sends, self.receives, self.used = sends, receives, 0

    def make(self, source, target, **device):
        at = self.used
        self.used += 1
        return pltpu.make_async_remote_copy(
            src_ref=source,
            dst_ref=target,
            send_sem=self.sends.at[at],
            recv_sem=self.receives.at[at],
            device_id=device,
            device_id_type=MESH_ID,
        )


def spots():
    return (lax.axis_index("x"), lax.axis_index("core"), lax.axis_index("z"), lax.axis_index("y"))


def greet(full):
    at_x, at_core, at_z, at_y = spots()
    barrier = pltpu.get_barrier_semaphore()
    count = 0

    def call(**device):
        pl.semaphore_signal(barrier, inc=1, device_id=device, device_id_type=MESH_ID)

    for step in range(4):
        if step:
            call(z=lax.rem(at_z + step, 4))
            count += 1
        if full or step == 0:
            call(core=1 - at_core, z=lax.rem(at_z + step, 4))
            count += 1
    call(x=1 - at_x)
    call(y=1 - at_y)
    pl.semaphore_wait(barrier, count + 2)


def flipped(value, bit):
    return 1 - value if bit else value


def row_loop(count, step, body):
    def inner(at, carry):
        body(pl.ds(pl.multiple_of(at * step, step), step))
        return carry

    lax.fori_loop(0, count // step, inner, 0)


def block_loop(count, body):
    def inner(at, carry):
        body(at)
        return carry

    lax.fori_loop(0, count, inner, 0)


def dot_f32(left, right, pairing=(((1,), (0,)), ((), ()))):
    return lax.dot_general(left, right, pairing, preferred_element_type=jnp.float32)


def spread_rows(wires, ref, quarter):
    _, at_core, _, at_y = spots()
    own, near = ref.at[pl.ds(0, quarter)], ref.at[pl.ds(quarter, quarter)]
    to_y = wires.make(own, near, y=1 - at_y)
    to_core = wires.make(own, ref.at[pl.ds(2 * quarter, quarter)], core=1 - at_core)
    again = wires.make(near, ref.at[pl.ds(3 * quarter, quarter)], core=1 - at_core)
    to_y.start()
    to_core.start()
    return to_y, to_core, again


def add_rows(wires, part, keep, acc, bufs, fill=None):
    _, at_core, _, at_y = spots()
    send_c, recv_c, send_y, recv_y = bufs
    low = jnp.bfloat16
    half = keep.shape[1] // 2
    sides = [pl.ds(0, half), pl.ds(half, half)]
    far = [wires.make(send_c.at[b], recv_c.at[b], core=1 - at_core) for b in range(2)]
    across = wires.make(send_y, recv_y, y=1 - at_y)
    for b, r in ((1, 3), (0, 2)):
        for side in range(2):
            send_c[b, :, sides[side]] = part(r, side).astype(low)
        far[b].start()
    for side in range(2):
        acc[:, sides[side]] = part(1, side)
    far[1].wait_recv()

    def to_send(rows):
        send_y[rows, :] = (acc[rows, :] + recv_c[1, rows, :].astype(jnp.float32)).astype(low)

    row_loop(keep.shape[0], 32, to_send)
    across.start()
    for side in range(2):
        keep[:, sides[side]] = part(0, side)
    far[0].wait_recv()
    if fill is not None:
        fill()
    across.wait_recv()

    def finish(rows):
        keep[rows, :] += recv_c[0, rows, :].astype(jnp.float32) + recv_y[rows, :].astype(jnp.float32)

    row_loop(keep.shape[0], 32, finish)
    far[0].wait_send()
    far[1].wait_send()
    across.wait_send()


def front_kernel(
    head_piece, up_piece, down_piece, tokens, time_row, ids_col, ids_row,
    w_head, w_up, w_down, emb, proj, ctx, w_out, hid, pre, act, normed_one, inverse_one, hidden, summed, vecs,
    tok, send_c, recv_c, send_y, recv_y, keep, acc, send_sem, recv_sem, local_sem,
):
    at_x, at_core, at_z, at_y = spots()
    low, f32 = jnp.bfloat16, jnp.float32
    length, width = emb.shape
    quarter, half = length // 4, width // 2
    zs = w_head.shape[0]
    span = half + 2 * TILE
    head_size = ctx.shape[2]
    in_size = 3 * head_size
    wires = Wires(send_sem, recv_sem)
    greet(False)

    kept, lent = [], []
    for at, (piece, target) in enumerate(((head_piece, w_head), (up_piece, w_up), (down_piece, w_down))):
        size = piece.shape[1]
        place = target.at[0, 0, pl.ds(pl.multiple_of(at_core * size, size), size)]
        local = pltpu.make_async_copy(piece.at[at_core], place, local_sem.at[at])
        local.start()
        remote = wires.make(piece.at[1 - at_core], place, core=1 - at_core)
        remote.start()
        kept.append(local)
        lent.append(remote)
    turns, cross = [], []
    for target in (w_head, w_up, w_down):
        turns.append(
            [None]
            + [wires.make(target.at[0, 0], target.at[s, 0], z=lax.rem(at_z + s, zs)) for s in range(1, zs)]
        )
        cross.append([wires.make(target.at[s, 0], target.at[s, 1], x=1 - at_x) for s in range(zs)])

    holds = at_core == lax.div(at_z, 2)
    start = lax.rem(at_z, 2) * length
    here, there = [], []
    for r in range(4):
        for h in range(2):
            spot = tok.at[pl.ds(r * quarter, quarter), pl.ds(pl.multiple_of(flipped(at_x, h) * half, half), half)]

            def source(core):
                at = flipped(core, r // 2) * 2 + flipped(at_y, r % 2)
                return tokens.at[pl.ds(pl.multiple_of(start + at * quarter, quarter), quarter), pl.ds(h * half, half)]

            here.append(pltpu.make_async_copy(source(at_core), spot, local_sem.at[3 + 2 * r + h]))
            there.append(wires.make(source(1 - at_core), spot, core=1 - at_core))

    @pl.when(holds)
    def _():
        for near, far in zip(here, there):
            near.start()
            far.start()

    for at in range(3):
        kept[at].wait()
        lent[at].wait_recv()
        for s in range(1, zs):
            turns[at][s].start()
        if at == 0:
            cross[0][0].start()

    @pl.when(holds)
    def _():
        for near in here:
            near.wait()

    @pl.when(jnp.logical_not(holds))
    def _():
        for far in there:
            far.wait_recv()

    def embed(rows):
        emb[rows, :] = (tok[rows, :].astype(f32) + time_row[...]).astype(low)

    row_loop(length, 32, embed)

    def forward(at, s):
        turns[at][s].wait_recv()
        cross[at][s].start()

    def small(s, side):
        size = half // 2 + TILE
        return (
            w_head[s, side, half // 2 : size, :].astype(f32)
            + w_head[s, side, size + half // 2 : 2 * size, :].astype(f32)
        )

    for s in range(zs):
        if s + 1 < zs:
            forward(0, s + 1)
        if s == 2:
            cross[1][0].start()
            cross[2][0].start()
        cross[0][s].wait_recv()
        bias = (small(s, 0) + small(s, 1))[0:1, :in_size]
        size = half // 2 + TILE

        def project(rows):
            total = bias
            for side in range(2):
                for core in range(2):
                    at = side * half + core * (half // 2)
                    total = total + dot_f32(
                        emb[rows, at : at + half // 2],
                        w_head[s, side, core * size : core * size + half // 2, :],
                    )[:, :in_size]
            proj[s, rows, :] = total.astype(low)

        row_loop(length, quarter, project)
        for side in range(2):
            for core in range(2):
                w_out[side, core * (half // 2) : (core + 1) * (half // 2), s * head_size : (s + 1) * head_size] = w_head[
                    s, side, core * size : core * size + half // 2, in_size:
                ]
        keys = proj[s, :, head_size : 2 * head_size]
        values = proj[s, :, 2 * head_size : in_size]

        def attend(rows):
            queries = proj[s, rows, 0:head_size] * jnp.bfloat16(head_size**-0.5)
            scores = dot_f32(queries, keys, ROW_PAIR)
            scores = jnp.where(ids_col[rows, :] == ids_row[...], scores, -1e30)
            highest = jnp.max(scores, axis=1, keepdims=True)
            exponent = jnp.exp(scores - highest)
            totals = jnp.sum(exponent, axis=1, keepdims=True)
            probability = (exponent * (1.0 / totals)).astype(low)
            ctx[s, rows, :] = dot_f32(probability, values).astype(low)

        row_loop(length, quarter, attend)

    for side in range(2):
        tile = small(0, side)
        for k in range(6):
            vecs[k : k + 1, side * half : side * half + half // 2] = tile[2 + k : 3 + k, :]
            vecs[k : k + 1, side * half + half // 2 : (side + 1) * half] = tile[8 + k : 9 + k, :]

    for s in range(1, zs):
        forward(1, s)
    bufs = (send_c, recv_c, send_y, recv_y)

    def mixed_part(r, side):
        joined = jnp.concatenate([ctx[s, r * quarter : (r + 1) * quarter, :] for s in range(zs)], axis=1)
        return dot_f32(joined, w_out[side], ROW_PAIR)

    add_rows(wires, mixed_part, keep, acc, bufs)

    def first_norm(rows):
        total = tok[rows, :].astype(f32) + time_row[...] + keep[rows, :] + vecs[2:3, :]
        normed, inverse = norm_stats(total)
        normed_one[rows, :] = normed
        inverse_one[rows, :] = inverse
        value = normed * vecs[0:1, :] + vecs[3:4, :]
        hidden[rows, :] = value
        hid[rows, :] = value.astype(low)

    row_loop(quarter, 32, first_norm)
    to_y, to_core, again = spread_rows(wires, hid, quarter)
    for s in range(1, zs):
        forward(2, s)
    for s in range(zs):
        cross[1][s].wait_recv()

    def up(r):
        rows = pl.ds(r * quarter, quarter)

        def one(s):
            lanes = pl.ds(pl.multiple_of(s * (half // 2), half // 2), half // 2)
            shift = (small(s, 0) + small(s, 1))[1:2, :]
            value = dot_f32(hid[rows, 0:half], w_up[s, 0]) + dot_f32(hid[rows, half:], w_up[s, 1]) + shift
            pre[rows, lanes] = value
            act[rows, lanes] = gelu_value(value).astype(low)

        block_loop(zs, one)

    up(0)
    to_core.wait_recv()
    up(2)
    to_y.wait_recv()
    again.start()
    up(1)
    again.wait_recv()
    up(3)
    for s in range(zs):
        cross[2][s].wait_recv()

    def down_part(r, side):
        rows = pl.ds(r * quarter, quarter)
        total = dot_f32(act[rows, 0 : half // 2], w_down[0, side], ROW_PAIR)
        for s in range(1, zs):
            total = total + dot_f32(act[rows, s * (half // 2) : (s + 1) * (half // 2)], w_down[s, side], ROW_PAIR)
        return total

    add_rows(wires, down_part, keep, acc, bufs)

    def second(rows):
        summed[rows, :] = hidden[rows, :] + keep[rows, :] + vecs[4:5, :]

    row_loop(quarter, 32, second)
    for at in range(3):
        lent[at].wait_send()
        for s in range(zs):
            if s:
                turns[at][s].wait_send()
            cross[at][s].wait_send()

    @pl.when(holds)
    def _():
        for far in there:
            far.wait_send()

    for member in (to_y, to_core, again):
        member.wait_send()


def run_front(pieces, tokens, time_row, ids, head_size):
    low, f32 = jnp.bfloat16, jnp.float32
    length, width = ids.shape[0], tokens.shape[1]
    quarter, half, zs = length // 4, width // 2, 4
    blocks = pieces[1].shape[2]
    vmem = pl.BlockSpec(memory_space=pltpu.VMEM)
    shapes = [
        ((zs, 2, half + 2 * TILE, 4 * head_size), low),
        ((zs, 2, half, blocks), low),
        ((zs, 2, half, blocks), low),
        ((length, width), low),
        ((zs, length, 3 * head_size), low),
        ((zs, length, head_size), low),
        ((2, half, zs * head_size), low),
        ((length, width), low),
        ((length, zs * blocks), f32),
        ((length, zs * blocks), low),
        ((quarter, width), f32),
        ((quarter, 1), f32),
        ((quarter, width), f32),
        ((quarter, width), f32),
        ((8, width), f32),
    ]
    return pl.pallas_call(
        front_kernel,
        out_shape=[jax.ShapeDtypeStruct(*s) for s in shapes],
        in_specs=[vmem] * 3 + [pl.BlockSpec(memory_space=pl.ANY)] + [vmem] * 3,
        out_specs=[vmem] * len(shapes),
        scratch_shapes=[
            pltpu.VMEM((length, width), low),
            pltpu.VMEM((2, quarter, width), low),
            pltpu.VMEM((2, quarter, width), low),
            pltpu.VMEM((quarter, width), low),
            pltpu.VMEM((quarter, width), low),
            pltpu.VMEM((quarter, width), f32),
            pltpu.VMEM((quarter, width), f32),
            pltpu.SemaphoreType.DMA((64,)),
            pltpu.SemaphoreType.DMA((64,)),
            pltpu.SemaphoreType.DMA((16,)),
        ],
        compiler_params=pltpu.CompilerParams(
            collective_id=0, has_side_effects=True, vmem_limit_bytes=60 << 20
        ),
        name="front",
    )(*pieces, tokens, time_row, ids[:, None], ids[None, :])


def plane_sum(wires, value, slots):
    at_x, at_core, at_z, at_y = spots()
    own = at_core * 4 + at_z
    sent = []
    for step in range(8):
        core, turned = step // 4, step % 4
        if step == 0:
            slots[own] = value[...]
            continue
        sent.append(
            wires.make(
                value,
                slots.at[own],
                core=flipped(at_core, core),
                z=lax.rem(at_z + turned, 4),
            )
        )
        sent[-1].start()
    return sent


def plane_total(sent, slots):
    for member in sent:
        member.wait_recv()
    total = slots[0]
    for at in range(1, 8):
        total = total + slots[at]
    return total


class Outlet:
    def __init__(self, own, result, sends, receives, y_sends, y_receives, local):
        self.own, self.result, self.local = own, result, local
        self.sends, self.receives = sends, receives
        self.y_sends, self.y_receives = y_sends, y_receives
        self.at_x, self.at_core, self.at_z, self.at_y = spots()
        self.quarter = own.shape[0]

    def spot(self, place, core, at_y):
        row = (place * 4 + core * 2 + at_y) * self.quarter
        return self.result.at[pl.ds(pl.multiple_of(row, self.quarter), self.quarter)]

    def copy(self, step):
        at = 2 * step + self.at_core
        return pltpu.make_async_remote_copy(
            src_ref=self.own,
            dst_ref=self.spot(lax.rem(self.at_z, 2), self.at_core, self.at_y),
            send_sem=self.sends.at[at],
            recv_sem=self.receives.at[at],
            device_id={"core": lax.div(self.at_z, 2), "z": lax.rem(self.at_z + step, 4)},
            device_id_type=MESH_ID,
        )

    def stay(self):
        return pltpu.make_async_copy(
            self.own, self.spot(lax.rem(self.at_z, 2), self.at_core, self.at_y), self.local
        )

    def start(self):
        home = self.at_core == lax.div(self.at_z, 2)

        @pl.when(home)
        def _():
            self.stay().start()

        @pl.when(jnp.logical_not(home))
        def _():
            self.copy(0).start()

        for step in (1, 3, 2):
            self.copy(step).start()

    def across(self, place, core):
        spot = self.spot(place, core, self.at_y)
        at = place * 2 + core
        return pltpu.make_async_remote_copy(
            src_ref=spot,
            dst_ref=spot,
            send_sem=self.y_sends.at[at],
            recv_sem=self.y_receives.at[at],
            device_id={"y": 1 - self.at_y},
            device_id_type=MESH_ID,
        )

    def forward(self, place, core):
        source = 2 * self.at_core + place
        step = lax.rem(self.at_z - source + 4, 4)
        own = jnp.logical_and(step == 0, self.at_core == core)

        @pl.when(own)
        def _():
            self.stay().wait()

        @pl.when(jnp.logical_not(own))
        def _():
            spot = self.spot(place, core, self.at_y)
            at = 2 * step + core
            pltpu.make_async_remote_copy(
                src_ref=spot,
                dst_ref=spot,
                send_sem=self.sends.at[at],
                recv_sem=self.receives.at[at],
                device_id={"y": 1 - self.at_y},
                device_id_type=MESH_ID,
            ).wait_recv()

        self.across(place, core).start()

    def finish(self):
        home = self.at_core == lax.div(self.at_z, 2)
        for place in range(2):
            for core in range(2):
                self.across(place, core).wait()

        @pl.when(jnp.logical_not(home))
        def _():
            self.copy(0).wait_send()

        for step in range(1, 4):
            self.copy(step).wait_send()


def back_kernel(
    w_head, w_up, w_down, emb, proj, ctx, w_out, hid, pre, act, normed_one, inverse_one, summed, vecs, upstream,
    ids_col, ids_row,
    block_out, input_out, res_head, res_up, res_down, res_tile, feature, norm,
    two, slope, one, grad_ctx, grad_proj, two_full, one_full, send_c, recv_c, send_y, recv_y, keep, acc,
    near_head, far_head, got_head, came_head, near_up, far_up, got_up, came_up, near_down, far_down, got_down, came_down,
    out_one, out_two, feat, slots, scalar, scalar_slots, key_sum, value_sum, y_feat, x_feat, y_scalar, x_scalar,
    send_sem, recv_sem, out_sem, local_sem,
):
    at_x, at_core, at_z, at_y = spots()
    low, f32 = jnp.bfloat16, jnp.float32
    length, width = emb.shape
    quarter, half = length // 4, width // 2
    zs = w_head.shape[0]
    block = half // 2
    head_size = ctx.shape[2]
    in_size = 3 * head_size
    wires = Wires(send_sem, recv_sem)
    greet(True)
    feat[...] = jnp.zeros_like(feat)

    def lanes(h):
        return pl.ds(pl.multiple_of(flipped(at_x, h) * half, half), half)

    def second_norm(rows):
        normed, inverse = norm_stats(summed[rows, :])
        gain, shift = vecs[1:2, :], vecs[5:6, :]
        value = (normed * gain + shift).astype(low)
        for h in range(2):
            out_one[rows, lanes(h)] = value[:, h * half : (h + 1) * half]
        above = upstream[rows, :].astype(f32)
        grad = norm_back(above * gain, normed, inverse)
        feat[1:2, :] += jnp.sum(above * normed, axis=0, keepdims=True)
        feat[5:6, :] += jnp.sum(above, axis=0, keepdims=True)
        feat[4:5, :] += jnp.sum(grad, axis=0, keepdims=True)
        two_full[rows, :] = grad
        two[rows, :] = grad.astype(low)

    row_loop(quarter, 32, second_norm)
    to_y, to_core, again = spread_rows(wires, two, quarter)
    outlets = [
        Outlet(own, result, *[out_sem.at[n, k] for k in range(4)], local_sem.at[n])
        for n, (own, result) in enumerate(((out_one, block_out), (out_two, input_out)))
    ]
    outlets[0].start()

    def slopes(r):
        rows = pl.ds(r * quarter, quarter)

        def inner(s):
            units = pl.ds(pl.multiple_of(s * block, block), block)
            value = dot_f32(two[rows, 0:half], w_down[s, 0]) + dot_f32(two[rows, half:], w_down[s, 1])
            slope[rows, units] = (value * gelu_slope(pre[rows, units])).astype(low)

        block_loop(zs, inner)

    slopes(0)
    to_core.wait_recv()
    slopes(2)
    to_y.wait_recv()
    again.start()
    slopes(1)
    again.wait_recv()
    slopes(3)
    ended = [to_y, to_core, again]

    def group(near, far, got, came):
        crossed = [wires.make(far.at[s], got.at[s], x=1 - at_x) for s in range(zs)]
        turned = [
            wires.make(far.at[s], came.at[s - 1], z=lax.rem(at_z + zs - s, zs)) for s in range(1, zs)
        ]
        return near, far, got, crossed, turned, came

    groups = {
        "head": group(near_head, far_head, got_head, came_head),
        "up": group(near_up, far_up, got_up, came_up),
        "down": group(near_down, far_down, got_down, came_down),
    }

    def weight_grads(name, left, right):
        near, far, got, crossed, turned, came = groups[name]

        for s in range(zs):
            far[s] = dot_f32(left[:, half:], right[:, s * block : (s + 1) * block], COL_PAIR).astype(low)
            crossed[s].start()

        def inner(s):
            units = pl.ds(pl.multiple_of(s * block, block), block)
            near[s] = dot_f32(left[:, 0:half], right[:, units], COL_PAIR)

        block_loop(zs, inner)

    def turn_blocks(name):
        near, far, got, crossed, turned, came = groups[name]
        size = near.shape[1]
        for s in range(zs):
            crossed[s].wait()

        def inner(s):
            def add(rows):
                near[s, rows, :] += got[s, rows, :].astype(f32)
                far[s, rows, :] = near[s, rows, :].astype(low)

            row_loop(size, 16, add)

        block_loop(zs, inner)

    def start_turns(name):
        for member in groups[name][4]:
            member.start()

    def settle(name):
        near, far, got, crossed, turned, came = groups[name]
        size = near.shape[1]
        for member in turned:
            member.wait()

        def add(rows):
            total = near[0, rows, :]
            for s in range(1, zs):
                total = total + came[s - 1, rows, :].astype(f32)
            near[0, rows, :] = total

        row_loop(size, 16, add)

    bufs = (send_c, recv_c, send_y, recv_y)

    def back_part(r, side):
        rows = pl.ds(r * quarter, quarter)
        total = dot_f32(slope[rows, 0:block], w_up[0, side], ROW_PAIR)
        for s in range(1, zs):
            total = total + dot_f32(slope[rows, s * block : (s + 1) * block], w_up[s, side], ROW_PAIR)
        return total

    add_rows(wires, back_part, keep, acc, bufs, lambda: weight_grads("down", two, act))

    def first_norm(rows):
        grad_hidden = keep[rows, :] + two_full[rows, :]
        normed = normed_one[rows, :]
        grad = norm_back(grad_hidden * vecs[0:1, :], normed, inverse_one[rows, :])
        feat[0:1, :] += jnp.sum(grad_hidden * normed, axis=0, keepdims=True)
        feat[3:4, :] += jnp.sum(grad_hidden, axis=0, keepdims=True)
        feat[2:3, :] += jnp.sum(grad, axis=0, keepdims=True)
        one_full[rows, :] = grad
        one[rows, :] = grad.astype(low)

    row_loop(quarter, 32, first_norm)
    to_y, to_core, again = spread_rows(wires, one, quarter)
    ended += [to_y, to_core, again]
    feat_sent = plane_sum(wires, feat, slots)
    weight_grads("up", hid, slope)

    def contexts(r):
        rows = pl.ds(r * quarter, quarter)
        value = dot_f32(one[rows, 0:half], w_out[0]) + dot_f32(one[rows, half:], w_out[1])
        value = value.astype(low)
        for s in range(zs):
            grad_ctx[s, rows, :] = value[:, s * head_size : (s + 1) * head_size]

    contexts(0)
    to_core.wait_recv()
    contexts(2)
    to_y.wait_recv()
    again.start()
    contexts(1)
    turn_blocks("down")
    start_turns("down")
    again.wait_recv()
    contexts(3)
    for place in range(2):
        for core in range(2):
            outlets[0].forward(place, core)
    scale = head_size**-0.5

    def attend(s):
        keys = proj[s, :, head_size : 2 * head_size]
        values = proj[s, :, 2 * head_size : in_size]
        key_sum[...] = jnp.zeros_like(key_sum)
        value_sum[...] = jnp.zeros_like(value_sum)

        def inner(rows):
            queries = proj[s, rows, 0:head_size] * low(scale)
            grads = grad_ctx[s, rows, :]
            scores = dot_f32(keys, queries, ROW_PAIR)
            scores = jnp.where(ids_col[...] == ids_row[0:1, rows], scores, -1e30)
            highest = jnp.max(scores, axis=0, keepdims=True)
            exponent = jnp.exp(scores - highest)
            probability = exponent * (1.0 / jnp.sum(exponent, axis=0, keepdims=True))
            grad_prob = dot_f32(values, grads, ROW_PAIR)
            weighted = jnp.sum(probability * grad_prob, axis=0, keepdims=True)
            grad_score = (probability * (grad_prob - weighted)).astype(low)
            value_sum[...] += dot_f32(probability.astype(low), grads)
            key_sum[...] += dot_f32(grad_score, queries)
            grad_query = dot_f32(grad_score, keys, COL_PAIR)
            grad_proj[s, rows, 0:head_size] = (grad_query * scale).astype(low)

        row_loop(length, quarter, inner)
        grad_proj[s, :, head_size : 2 * head_size] = key_sum[...].astype(low)
        grad_proj[s, :, 2 * head_size : in_size] = value_sum[...].astype(low)

    block_loop(2, attend)
    turn_blocks("up")
    start_turns("up")
    block_loop(2, lambda s: attend(s + 2))

    size = block + TILE

    def input_part(r, side):
        rows = pl.ds(r * quarter, quarter)
        parts = []
        for core in range(2):
            total = None
            for s in range(zs):
                value = dot_f32(
                    grad_proj[s, rows, :], w_head[s, side, core * size : core * size + block, 0:in_size], ROW_PAIR
                )
                total = value if total is None else total + value
            parts.append(total)
        return jnp.concatenate(parts, axis=1)

    near, far, got, crossed, turned, came = groups["head"]

    def head_far():
        for s in range(zs):
            far[s, 0:half, 0:in_size] = dot_f32(emb[:, half:], grad_proj[s], COL_PAIR).astype(low)
            far[s, 0:half, in_size:] = dot_f32(one[:, half:], ctx[s], COL_PAIR).astype(low)
            sums = jnp.sum(grad_proj[s].astype(f32), axis=0, keepdims=True)
            near[s, half:, :] = jnp.zeros((TILE, near.shape[2]), f32)
            near[s, half : half + 1, 0:head_size] = sums[:, 0:head_size]
            near[s, half : half + 1, 2 * head_size : in_size] = sums[:, 2 * head_size :]
            near[s, half + 1 : half + 2, :] = jnp.sum(
                slope[:, s * block : (s + 1) * block].astype(f32), axis=0, keepdims=True
            )
            far[s, half:, :] = near[s, half:, :].astype(low)
            crossed[s].start()

    add_rows(wires, input_part, keep, acc, bufs, head_far)

    def leave(rows):
        value = (keep[rows, :] + one_full[rows, :]).astype(low)
        for h in range(2):
            out_two[rows, lanes(h)] = value[:, h * half : (h + 1) * half]

    row_loop(quarter, 32, leave)
    outlets[1].start()

    def head_near(s):
        near[s, 0:half, 0:in_size] = dot_f32(emb[:, 0:half], grad_proj[s], COL_PAIR)
        near[s, 0:half, in_size:] = dot_f32(one[:, 0:half], ctx[s], COL_PAIR)

    block_loop(zs, head_near)
    turn_blocks("head")
    start_turns("head")

    acc[0:8, :] = plane_total(feat_sent, slots)
    y_copy = wires.make(acc.at[pl.ds(0, 8)], y_feat, y=1 - at_y)
    y_copy.start()
    y_copy.wait_recv()
    feat_all = acc[0:8, :] + y_feat[...]
    keep[0:8, :] = feat_all
    x_copy = wires.make(keep.at[pl.ds(0, 8), pl.ds(half, half)], x_feat, x=1 - at_x)
    x_copy.start()
    x_copy.wait_recv()
    feature[...] = feat_all[:, 0:half] + x_feat[...]

    settle("down")
    settle("up")
    for place in range(2):
        for core in range(2):
            outlets[1].forward(place, core)
    settle("head")

    backs = []
    results = (("head", res_head), ("up", res_up), ("down", res_down))
    for at, (name, result) in enumerate(results):
        near = groups[name][0]
        mine = near.at[0, pl.ds(pl.multiple_of(at_core * block, block), block)]
        other = near.at[0, pl.ds(pl.multiple_of((1 - at_core) * block, block), block)]
        local = pltpu.make_async_copy(mine, result.at[at_core], local_sem.at[2 + at])
        local.start()
        remote = wires.make(other, result.at[at_core], core=1 - at_core)
        remote.start()
        backs += [local, remote]
    tile = near_head.at[0, pl.ds(half, TILE)]
    local = pltpu.make_async_copy(tile, res_tile.at[at_core], local_sem.at[5])
    remote = wires.make(tile, res_tile.at[at_core], core=1 - at_core)
    local.start()
    remote.start()
    backs += [local, remote]

    acc[8:16, 0:block] = jnp.zeros((8, block), f32)
    for name, _ in results:
        near = groups[name][0]

        def add(rows):
            value = near[0, rows, :]
            acc[8:16, 0:block] += value * value

        row_loop(half, 8, add)
    value = near_head[0, half : half + 8, :]
    acc[8:16, 0:block] += 0.5 * value * value
    shared = feature[...] * feature[...] * (1.0 / 16.0)
    shared = shared[:, 0:block] + shared[:, block:]
    summed_squares = jnp.sum(acc[8:16, 0:block] + shared)
    scalar[...] = jnp.broadcast_to(summed_squares, scalar.shape)
    scalar_sent = plane_sum(wires, scalar, scalar_slots)
    value = plane_total(scalar_sent, scalar_slots)
    norm[...] = value
    y_two = wires.make(norm, y_scalar, y=1 - at_y)
    y_two.start()
    y_two.wait()
    value = value + y_scalar[...]
    send_scalar = scalar_slots.at[8]
    send_scalar[...] = value
    x_two = wires.make(send_scalar, x_scalar, x=1 - at_x)
    x_two.start()
    x_two.wait()
    norm[...] = value + x_scalar[...]

    for member in ended + feat_sent + scalar_sent + [y_copy, x_copy]:
        member.wait_send()
    for member in backs:
        member.wait()
    for outlet in outlets:
        outlet.finish()


def run_back(front, upstream, ids, tokens_shape):
    low, f32 = jnp.bfloat16, jnp.float32
    (w_head, w_up, w_down, emb, proj, ctx, w_out, hid, pre, act, normed_one, inverse_one, _, summed, vecs) = front
    length, width = emb.shape
    zs, _, span, packed = w_head.shape
    quarter, half, block = length // 4, width // 2, width // 4
    head_size = ctx.shape[2]
    vmem = pl.BlockSpec(memory_space=pltpu.VMEM)
    anywhere = pl.BlockSpec(memory_space=pl.ANY)
    shape = jax.ShapeDtypeStruct
    inputs = (w_head, w_up, w_down, emb, proj, ctx, w_out, hid, pre, act, normed_one, inverse_one, summed, vecs,
              upstream, ids[:, None], ids[None, :])
    head_rows = half + TILE

    def triple(size):
        return [pltpu.VMEM((n, size, block), d) for n, d in ((zs, f32), (zs, low), (zs, low), (zs - 1, low))]

    return pl.pallas_call(
        back_kernel,
        out_shape=[
            shape(tokens_shape, low),
            shape(tokens_shape, low),
            shape((2, block, block), f32),
            shape((2, block, block), f32),
            shape((2, block, block), f32),
            shape((2, TILE, block), f32),
            shape((8, half), f32),
            shape((8, 128), f32),
        ],
        in_specs=[vmem] * len(inputs),
        out_specs=[anywhere] * 2 + [vmem] * 6,
        scratch_shapes=[
            pltpu.VMEM((length, width), low),
            pltpu.VMEM((length, width), low),
            pltpu.VMEM((length, width), low),
            pltpu.VMEM((zs, length, head_size), low),
            pltpu.VMEM((zs, length, 3 * head_size), low),
            pltpu.VMEM((quarter, width), f32),
            pltpu.VMEM((quarter, width), f32),
            pltpu.VMEM((2, quarter, width), low),
            pltpu.VMEM((2, quarter, width), low),
            pltpu.VMEM((quarter, width), low),
            pltpu.VMEM((quarter, width), low),
            pltpu.VMEM((quarter, width), f32),
            pltpu.VMEM((quarter, width), f32),
            *triple(head_rows),
            *triple(half),
            *triple(half),
            pltpu.VMEM((quarter, width), low),
            pltpu.VMEM((quarter, width), low),
            pltpu.VMEM((8, width), f32),
            pltpu.VMEM((8, 8, width), f32),
            pltpu.VMEM((8, 128), f32),
            pltpu.VMEM((9, 8, 128), f32),
            pltpu.VMEM((length, head_size), f32),
            pltpu.VMEM((length, head_size), f32),
            pltpu.VMEM((8, width), f32),
            pltpu.VMEM((8, half), f32),
            pltpu.VMEM((8, 128), f32),
            pltpu.VMEM((8, 128), f32),
            pltpu.SemaphoreType.DMA((72,)),
            pltpu.SemaphoreType.DMA((72,)),
            pltpu.SemaphoreType.DMA((2, 4, 8)),
            pltpu.SemaphoreType.DMA((6,)),
        ],
        compiler_params=pltpu.CompilerParams(
            collective_id=1, has_side_effects=True, vmem_limit_bytes=67000000
        ),
        name="back",
    )(*inputs)


def on_grid(*arguments):
    tokens, time_embed, segment_ids, cotangent = arguments[:4]
    masters, moments, squares = arguments[4::3], arguments[5::3], arguments[6::3]
    input_weight, output_weight, upward_weight, downward_weight = masters[:4]
    head_bias, hidden_bias, norm_gains, branch_biases = masters[4:]
    at_x, at_core = lax.axis_index("x"), lax.axis_index("core")
    at_z, at_y = lax.axis_index("z"), lax.axis_index("y")
    first_core, first_x = at_core == 0, at_x == 0
    swapped = at_x == 1
    low = jnp.bfloat16
    f32 = jnp.float32
    length = segment_ids.shape[1]
    head_size = head_bias.shape[0] * 4 // 2
    zs = 4
    place = at_core * 2 + at_y
    quarter = length // 4

    rows = input_weight.shape[0]
    wide = upward_weight.shape[1] // 2
    packed = 4 * head_size
    small_rows = head_bias.shape[0]

    position = at_x * 2 + at_core
    vectors = jnp.concatenate([norm_gains, branch_biases], axis=1).T
    vectors = lax.dynamic_update_slice(
        jnp.zeros((TILE, rows), f32), vectors, (2 + 6 * at_core, 0)
    )

    def head_piece(half):
        body = jnp.concatenate(
            [
                input_weight[:, half * 3 * head_size : (half + 1) * 3 * head_size],
                output_weight[:, half * head_size : (half + 1) * head_size],
            ],
            axis=1,
        )
        tile = lax.dynamic_update_slice(
            vectors, head_bias[:, half][None], (0, at_x * 2 * head_size + at_core * small_rows)
        )
        units = lax.dynamic_update_slice(
            jnp.zeros((2, 4 * small_rows), f32),
            hidden_bias[:, 2 * half : 2 * half + 2].T,
            (0, position * small_rows),
        )
        tile = lax.dynamic_update_slice(tile, units.reshape(1, -1), (1, 0))
        return jnp.concatenate([body, tile], axis=0)

    pieces = [
        jnp.stack([head_piece(0), head_piece(1)]).astype(low),
        jnp.stack([upward_weight[:, :wide], upward_weight[:, wide:]]).astype(low),
        jnp.stack([downward_weight[:, :wide], downward_weight[:, wide:]]).astype(low),
    ]

    seat = ("core", "z")
    holds = at_core == at_z // 2
    lend = [((i // 2) * zs + i, (1 - i // 2) * zs + i) for i in range(zs)]

    def borrow(kept, sent):
        return jnp.where(holds, kept, lax.ppermute(sent, seat, lend))

    local = at_z % 2
    own_time = lax.dynamic_slice_in_dim(time_embed, local, 1, 0)
    own_time = borrow(own_time, own_time)
    own_ids = lax.dynamic_slice_in_dim(segment_ids, local, 1, 0)
    own_ids = borrow(own_ids, own_ids)[0]

    def at_quarter(which):
        return lax.dynamic_slice_in_dim(cotangent, local * length + which * quarter, quarter, 0)

    upstream = borrow(at_quarter(place), at_quarter(place ^ 2))
    upstream = swap_halves(upstream, swapped)

    def relative(values):
        return jnp.concatenate(
            [lax.dynamic_slice_in_dim(values, (place ^ turnover) * quarter, quarter, 0) for turnover in range(4)],
            axis=0,
        )

    time_row = swap_halves(own_time.astype(f32), swapped)
    segments = relative(own_ids)

    front = run_front(pieces, tokens, time_row, segments, head_size)
    block_output, input_grad, res_head, res_up, res_down, tiles, feature, norm = run_back(
        front, upstream, segments, tokens.shape
    )
    in_size = 3 * head_size
    sent_in = jnp.concatenate([res_head[0, :, :in_size], res_head[1, :, :in_size]], axis=1)
    sent_out = jnp.concatenate([res_head[0, :, in_size:], res_head[1, :, in_size:]], axis=1)
    sent_up = jnp.concatenate([res_up[0], res_up[1]], axis=1)
    sent_down = jnp.concatenate([res_down[0], res_down[1]], axis=1)
    sent_head = lax.dynamic_slice(
        tiles[:, 0], (0, at_x * 2 * head_size + at_core * small_rows), (2, small_rows)
    ).T
    units = lax.dynamic_slice(
        tiles[:, 1].reshape(4, 4 * small_rows), (0, position * small_rows), (4, small_rows)
    )
    sent_unit = units.T
    feature = lax.dynamic_slice(feature, (0, at_core * rows), (8, rows))
    sent_gains, sent_shifts = feature[0:2].T, feature[2:6].T
    grad_norm = jnp.sqrt(norm[0, 0])
    gradients = (sent_in, sent_out, sent_up, sent_down, sent_head, sent_unit, sent_gains, sent_shifts)
    factor = CLIP / jnp.maximum(grad_norm, CLIP)
    results = [block_output, input_grad.astype(f32), grad_norm.reshape(1)]
    for position in range(8):
        results += adam_update(
            masters[position],
            moments[position],
            squares[position],
            gradients[position] * factor,
            RATES[position],
            DECAYS[position],
        )
    return tuple(results)


def solution(mesh):
    plain = mesh.shape["rows"] != 4 or mesh.shape["tp"] != 8
    if plain:
        rows, tp = "rows", "tp"
        grid, work = mesh, on_device
    else:
        rows, tp = ("x", "core"), ("z", "y")
        grid = Mesh(mesh.devices.reshape(2, 2, 4, 2), ("x", "core", "z", "y"))
        work = on_grid
    narrow, split = P(rows, None), P(rows, tp)
    return jax.shard_map(
        work,
        mesh=grid,
        in_specs=(narrow,) * 4 + (split,) * 18 + (narrow,) * 6,
        out_specs=(narrow, narrow, P()) + (split,) * 18 + (narrow,) * 6,
        check_vma=False,
    )
```

```python
from functools import partial, reduce

import jax
import jax.numpy as jnp
from jax import lax
from jax.experimental import pallas as pl
from jax.experimental.pallas import tpu as pltpu
from jax.sharding import Mesh
from jax.sharding import PartitionSpec as P

HD = 64
STEP = 10


NORM_EPS = 1e-05
BETA_ONE = 0.9
BETA_TWO = 0.999
ADAM_EPS = 1e-08
CLIP = 1.0
RATES = (0.1, 0.4, 0.1, 0.05, 0.5, 0.5, 0.5, 0.5)
DECAYS = (0.01, 0.01, 0.01, 0.01, 0.0, 0.0, 0.0, 0.0)
ROW_PAIR = (((1,), (1,)), ((), ()))
COL_PAIR = (((0,), (0,)), ((), ()))


def norm_stats(summed):
    average = jnp.mean(summed, axis=-1, keepdims=True)
    centered = summed - average
    inverse = lax.rsqrt(jnp.mean(centered * centered, axis=-1, keepdims=True) + NORM_EPS)
    return (centered * inverse, inverse)


def norm_back(grad_normed, normed, inverse):
    first_mean = jnp.mean(grad_normed, axis=-1, keepdims=True)
    second_mean = jnp.mean(grad_normed * normed, axis=-1, keepdims=True)
    return inverse * (grad_normed - first_mean - normed * second_mean)


def gelu_value(inputs):
    return 0.5 * inputs * (1.0 + jax.scipy.special.erf(inputs * 0.7071067811865476))


def gelu_slope(inputs):
    cumulative = 0.5 * (1.0 + jax.scipy.special.erf(inputs * 0.7071067811865476))
    return cumulative + inputs * jnp.exp(-0.5 * inputs * inputs) * 0.3989422804014327


def masked_scores(queries, key_rows, segments):
    scores = jnp.einsum(
        "qhd,khd->hqk", queries, key_rows, preferred_element_type=jnp.float32
    ) * HD ** (-0.5)
    matching = segments[:, None] == segments[None, :]
    return jnp.where(matching[None], scores, -1e30)


def attend_forward(pieces):
    queries, key_rows, values, segments = pieces
    scores = masked_scores(queries, key_rows, segments)
    highest = jnp.max(scores, axis=-1, keepdims=True)
    exponent = jnp.exp(scores - highest)
    totals = jnp.sum(exponent, axis=-1, keepdims=True)
    probability = (exponent / totals).astype(jnp.bfloat16)
    context = jnp.einsum("hqk,khd->qhd", probability, values, preferred_element_type=jnp.float32)
    return (context, (highest + jnp.log(totals))[..., 0])


def attend_back(pieces):
    queries, key_rows, values, segments, log_total, grad_context = pieces
    scores = masked_scores(queries, key_rows, segments)
    probability = jnp.exp(scores - log_total[..., None])
    grad_prob = jnp.einsum("qhd,khd->hqk", grad_context, values, preferred_element_type=jnp.float32)
    weighted = jnp.sum(probability * grad_prob, axis=-1, keepdims=True)
    grad_score = (probability * (grad_prob - weighted)).astype(jnp.bfloat16)
    grad_query = jnp.einsum(
        "hqk,khd->qhd", grad_score, key_rows, preferred_element_type=jnp.float32
    ) * HD ** (-0.5)
    grad_key = jnp.einsum(
        "hqk,qhd->khd", grad_score, queries, preferred_element_type=jnp.float32
    ) * HD ** (-0.5)
    grad_value = jnp.einsum(
        "hqk,qhd->khd",
        probability.astype(jnp.bfloat16),
        grad_context,
        preferred_element_type=jnp.float32,
    )
    return jnp.stack([grad_query, grad_key, grad_value], axis=2)


def adam_update(weight, moment, square, clipped, rate, decay):
    moment = BETA_ONE * moment + (1.0 - BETA_ONE) * clipped
    square = BETA_TWO * square + (1.0 - BETA_TWO) * clipped * clipped
    corrected = (
        moment / (1.0 - BETA_ONE**STEP) / (jnp.sqrt(square / (1.0 - BETA_TWO**STEP)) + ADAM_EPS)
    )
    return (weight - rate * (corrected + decay * weight), moment, square)


def add_squares(running, member):
    return running + jnp.sum(member * member)


def on_device(
    tokens,
    time_embed,
    segment_ids,
    cotangent,
    input_weight,
    input_moment,
    input_square,
    output_weight,
    output_moment,
    output_square,
    upward_weight,
    upward_moment,
    upward_square,
    downward_weight,
    downward_moment,
    downward_square,
    head_bias,
    head_moment,
    head_square,
    hidden_bias,
    hidden_moment,
    hidden_square,
    norm_gains,
    gains_moment,
    gains_square,
    branch_biases,
    biases_moment,
    biases_square,
):
    masters = (
        input_weight,
        output_weight,
        upward_weight,
        downward_weight,
        head_bias,
        hidden_bias,
        norm_gains,
        branch_biases,
    )
    moments = (
        input_moment,
        output_moment,
        upward_moment,
        downward_moment,
        head_moment,
        hidden_moment,
        gains_moment,
        biases_moment,
    )
    squares = (
        input_square,
        output_square,
        upward_square,
        downward_square,
        head_square,
        hidden_square,
        gains_square,
        biases_square,
    )
    (
        weights_in,
        weights_out,
        weights_up,
        weights_down,
        head_shift,
        unit_shift,
        gains_low,
        shifts_low,
    ) = (
        lax.all_gather(input_weight.astype(jnp.bfloat16), "rows", axis=0, tiled=True),
        lax.all_gather(output_weight.astype(jnp.bfloat16), "rows", axis=0, tiled=True),
        lax.all_gather(upward_weight.astype(jnp.bfloat16), "rows", axis=0, tiled=True),
        lax.all_gather(downward_weight.astype(jnp.bfloat16), "rows", axis=0, tiled=True),
        lax.all_gather(head_bias.astype(jnp.bfloat16), "rows", axis=0, tiled=True),
        lax.all_gather(hidden_bias.astype(jnp.bfloat16), "rows", axis=0, tiled=True),
        lax.all_gather(norm_gains.astype(jnp.bfloat16), "rows", axis=0, tiled=True),
        lax.all_gather(branch_biases.astype(jnp.bfloat16), "rows", axis=0, tiled=True),
    )
    seq_count, length = segment_ids.shape
    width = tokens.shape[1]
    num_heads = head_shift.shape[1]
    head_size = head_shift.shape[0] // 2
    tok_rows = seq_count * length
    gains = gains_low.astype(jnp.float32)
    shifts = shifts_low.astype(jnp.float32)
    embedded = (
        tokens.astype(jnp.float32).reshape(seq_count, length, width)
        + time_embed.astype(jnp.float32)[:, None, :]
    ).reshape(tok_rows, width)
    embedded_low = embedded.astype(jnp.bfloat16)
    head_float = head_shift.astype(jnp.float32)
    offset = jnp.stack(
        [
            head_float[:head_size].T,
            jnp.zeros((num_heads, head_size), jnp.float32),
            head_float[head_size:].T,
        ],
        axis=1,
    )
    projected = jnp.dot(embedded_low, weights_in, preferred_element_type=jnp.float32).reshape(
        tok_rows, num_heads, 3, head_size
    )
    projected = (
        (projected + offset)
        .astype(jnp.bfloat16)
        .reshape(seq_count, length, num_heads, 3, head_size)
    )
    queries = projected[:, :, :, 0]
    key_rows = projected[:, :, :, 1]
    values = projected[:, :, :, 2]
    context, log_total = lax.map(attend_forward, (queries, key_rows, values, segment_ids))
    context_low = context.reshape(tok_rows, num_heads * head_size).astype(jnp.bfloat16)
    mixed_part = lax.dot_general(
        context_low, weights_out, ROW_PAIR, preferred_element_type=jnp.float32
    )
    mixed = lax.psum(mixed_part, "tp")
    normed_one, inverse_one = norm_stats(embedded + mixed + shifts[:, 0])
    hidden = normed_one * gains[:, 0] + shifts[:, 1]
    hidden_low = hidden.astype(jnp.bfloat16)
    unit_offset = unit_shift.astype(jnp.float32).T.reshape(-1)
    pre_act = jnp.dot(hidden_low, weights_up, preferred_element_type=jnp.float32) + unit_offset
    expanded_low = gelu_value(pre_act).astype(jnp.bfloat16)
    reduced_part = lax.dot_general(
        expanded_low, weights_down, ROW_PAIR, preferred_element_type=jnp.float32
    )
    reduced = lax.psum(reduced_part, "tp")
    normed_two, inverse_two = norm_stats(hidden + reduced + shifts[:, 2])
    block_output = (normed_two * gains[:, 1] + shifts[:, 3]).astype(jnp.bfloat16)
    upstream = cotangent.astype(jnp.float32)
    gain_two = jnp.sum(upstream * normed_two, axis=0)
    shift_three = jnp.sum(upstream, axis=0)
    grad_pre_two = norm_back(upstream * gains[:, 1], normed_two, inverse_two)
    shift_two = jnp.sum(grad_pre_two, axis=0)
    grad_pre_two_low = grad_pre_two.astype(jnp.bfloat16)
    grad_down = lax.dot_general(
        grad_pre_two_low, expanded_low, COL_PAIR, preferred_element_type=jnp.float32
    )
    grad_act = jnp.dot(grad_pre_two_low, weights_down, preferred_element_type=jnp.float32)
    grad_pre_act = (grad_act * gelu_slope(pre_act)).astype(jnp.bfloat16)
    unit_sums = jnp.sum(grad_pre_act, axis=0, dtype=jnp.float32)
    grad_unit = unit_sums.reshape(-1, 2 * head_size).T
    grad_up = lax.dot_general(
        hidden_low, grad_pre_act, COL_PAIR, preferred_element_type=jnp.float32
    )
    back_part = lax.dot_general(
        grad_pre_act, weights_up, ROW_PAIR, preferred_element_type=jnp.float32
    )
    grad_hidden = lax.psum(back_part, "tp") + grad_pre_two
    gain_one = jnp.sum(grad_hidden * normed_one, axis=0)
    shift_one = jnp.sum(grad_hidden, axis=0)
    grad_pre_one = norm_back(grad_hidden * gains[:, 0], normed_one, inverse_one)
    shift_zero = jnp.sum(grad_pre_one, axis=0)
    grad_pre_one_low = grad_pre_one.astype(jnp.bfloat16)
    grad_out = lax.dot_general(
        grad_pre_one_low, context_low, COL_PAIR, preferred_element_type=jnp.float32
    )
    grad_context = jnp.dot(
        grad_pre_one_low, weights_out, preferred_element_type=jnp.float32
    ).astype(jnp.bfloat16)
    grad_context = grad_context.reshape(seq_count, length, num_heads, head_size)
    grad_projected = lax.map(
        attend_back, (queries, key_rows, values, segment_ids, log_total, grad_context)
    )
    grad_projected = grad_projected.reshape(tok_rows, num_heads * 3 * head_size).astype(
        jnp.bfloat16
    )
    head_sums = jnp.sum(grad_projected, axis=0, dtype=jnp.float32).reshape(num_heads, 3, head_size)
    grad_head = jnp.concatenate([head_sums[:, 0].T, head_sums[:, 2].T], axis=0)
    grad_in = lax.dot_general(
        embedded_low, grad_projected, COL_PAIR, preferred_element_type=jnp.float32
    )
    input_part = lax.dot_general(
        grad_projected, weights_in, ROW_PAIR, preferred_element_type=jnp.float32
    )
    input_grad = lax.psum(input_part, "tp") + grad_pre_one
    grad_gains = jnp.stack([gain_one, gain_two], axis=1)
    grad_shifts = jnp.stack([shift_zero, shift_one, shift_two, shift_three], axis=1)
    sent_in, sent_out, sent_up, sent_down, sent_head, sent_unit, sent_gains, sent_shifts = (
        lax.psum_scatter(grad_in, "rows", scatter_dimension=0, tiled=True),
        lax.psum_scatter(grad_out, "rows", scatter_dimension=0, tiled=True),
        lax.psum_scatter(grad_up, "rows", scatter_dimension=0, tiled=True),
        lax.psum_scatter(grad_down, "rows", scatter_dimension=0, tiled=True),
        lax.psum_scatter(grad_head, "rows", scatter_dimension=0, tiled=True),
        lax.psum_scatter(grad_unit, "rows", scatter_dimension=0, tiled=True),
        lax.psum_scatter(grad_gains, "rows", scatter_dimension=0, tiled=True),
        lax.psum_scatter(grad_shifts, "rows", scatter_dimension=0, tiled=True),
    )
    gradients = (
        sent_in,
        sent_out,
        sent_up,
        sent_down,
        sent_head,
        sent_unit,
        sent_gains,
        sent_shifts,
    )
    split_part = reduce(
        add_squares,
        (sent_in, sent_out, sent_up, sent_down, sent_head, sent_unit),
        jnp.zeros((), jnp.float32),
    )
    copied_part = (
        jnp.sum(sent_gains * sent_gains) + jnp.sum(sent_shifts * sent_shifts)
    ) / lax.axis_size("tp")
    grad_norm = jnp.sqrt(lax.psum(split_part + copied_part, ("rows", "tp")))
    factor = CLIP / jnp.maximum(grad_norm, CLIP)
    updated = [
        adam_update(
            masters[position],
            moments[position],
            squares[position],
            gradients[position] * factor,
            RATES[position],
            DECAYS[position],
        )
        for position in range(8)
    ]
    return (
        block_output,
        input_grad,
        grad_norm.reshape(1),
        updated[0][0],
        updated[0][1],
        updated[0][2],
        updated[1][0],
        updated[1][1],
        updated[1][2],
        updated[2][0],
        updated[2][1],
        updated[2][2],
        updated[3][0],
        updated[3][1],
        updated[3][2],
        updated[4][0],
        updated[4][1],
        updated[4][2],
        updated[5][0],
        updated[5][1],
        updated[5][2],
        updated[6][0],
        updated[6][1],
        updated[6][2],
        updated[7][0],
        updated[7][1],
        updated[7][2],
    )


def flip(value, axis):
    return lax.ppermute(value, axis, [(0, 1), (1, 0)])


def turn(value, amount, count):
    return lax.ppermute(value, "z", [(i, (i + amount) % count) for i in range(count)])


def swap_halves(value, swapped):
    half = value.shape[-1] // 2
    return jnp.where(
        swapped, jnp.concatenate([value[..., half:], value[..., :half]], axis=-1), value
    )


def in_order(first, mine, other):
    return jnp.where(
        first, jnp.concatenate([mine, other], axis=0), jnp.concatenate([other, mine], axis=0)
    )


MESH_ID = pl.DeviceIdType.MESH
TILE = 16


class Wires:
    def __init__(self, sends, receives):
        self.sends, self.receives, self.used = sends, receives, 0

    def make(self, source, target, **device):
        at = self.used
        self.used += 1
        return pltpu.make_async_remote_copy(
            src_ref=source,
            dst_ref=target,
            send_sem=self.sends.at[at],
            recv_sem=self.receives.at[at],
            device_id=device,
            device_id_type=MESH_ID,
        )


def spots():
    return (lax.axis_index("x"), lax.axis_index("core"), lax.axis_index("z"), lax.axis_index("y"))


def greet(full):
    at_x, at_core, at_z, at_y = spots()
    barrier = pltpu.get_barrier_semaphore()
    count = 0

    def call(**device):
        pl.semaphore_signal(barrier, inc=1, device_id=device, device_id_type=MESH_ID)

    for step in range(4):
        if step:
            call(z=lax.rem(at_z + step, 4))
            count += 1
        if full or step == 0:
            call(core=1 - at_core, z=lax.rem(at_z + step, 4))
            count += 1
    call(x=1 - at_x)
    call(y=1 - at_y)
    pl.semaphore_wait(barrier, count + 2)


def flipped(value, bit):
    return 1 - value if bit else value


def row_loop(count, step, body):
    def inner(at, carry):
        body(pl.ds(pl.multiple_of(at * step, step), step))
        return carry

    lax.fori_loop(0, count // step, inner, 0)


def block_loop(count, body):
    def inner(at, carry):
        body(at)
        return carry

    lax.fori_loop(0, count, inner, 0)


def dot_f32(left, right, pairing=(((1,), (0,)), ((), ()))):
    return lax.dot_general(left, right, pairing, preferred_element_type=jnp.float32)


def spread_rows(wires, ref, quarter):
    _, at_core, _, at_y = spots()
    own, near = ref.at[pl.ds(0, quarter)], ref.at[pl.ds(quarter, quarter)]
    to_y = wires.make(own, near, y=1 - at_y)
    to_core = wires.make(own, ref.at[pl.ds(2 * quarter, quarter)], core=1 - at_core)
    again = wires.make(near, ref.at[pl.ds(3 * quarter, quarter)], core=1 - at_core)
    to_y.start()
    to_core.start()
    return to_y, to_core, again


def add_rows(wires, part, keep, acc, bufs, fill=None):
    _, at_core, _, at_y = spots()
    send_c, recv_c, send_y, recv_y = bufs
    low = jnp.bfloat16
    half = keep.shape[1] // 2
    sides = [pl.ds(0, half), pl.ds(half, half)]
    far = [wires.make(send_c.at[b], recv_c.at[b], core=1 - at_core) for b in range(2)]
    across = wires.make(send_y, recv_y, y=1 - at_y)
    for b, r in ((1, 3), (0, 2)):
        for side in range(2):
            send_c[b, :, sides[side]] = part(r, side).astype(low)
        far[b].start()
    for side in range(2):
        acc[:, sides[side]] = part(1, side)
    far[1].wait_recv()

    def to_send(rows):
        send_y[rows, :] = (acc[rows, :] + recv_c[1, rows, :].astype(jnp.float32)).astype(low)

    row_loop(keep.shape[0], 32, to_send)
    across.start()
    for side in range(2):
        keep[:, sides[side]] = part(0, side)
    far[0].wait_recv()
    if fill is not None:
        fill()
    across.wait_recv()

    def finish(rows):
        keep[rows, :] += recv_c[0, rows, :].astype(jnp.float32) + recv_y[rows, :].astype(jnp.float32)

    row_loop(keep.shape[0], 32, finish)
    far[0].wait_send()
    far[1].wait_send()
    across.wait_send()


class Relay:
    def __init__(self, targets, z_sends, z_receives, x_sends, x_receives):
        self.targets, self.z_sends, self.z_receives = targets, z_sends, z_receives
        self.x_sends, self.x_receives = x_sends, x_receives
        self.at_x, _, self.at_z, _ = spots()
        middle = lax.rem(lax.div(self.at_z + 1, 2), 2)
        first = 3 - 2 * lax.rem(self.at_z, 2)
        second = 2 * (1 - middle) + middle * (4 - first)
        self.order = [0, first, second, 6 - first - second]

    def hop(self, at, slot, rising, send):
        to = lax.rem(slot + (1 if rising else 3), 4)
        target = self.targets[at]
        return pltpu.make_async_remote_copy(
            src_ref=target.at[slot, 0],
            dst_ref=target.at[to, 0],
            send_sem=self.z_sends.at[at, send],
            recv_sem=self.z_receives.at[at, to],
            device_id={"z": self.at_z + (1 if rising else -1)},
            device_id_type=MESH_ID,
        )

    def cross(self, at, slot):
        target = self.targets[at]
        return pltpu.make_async_remote_copy(
            src_ref=target.at[slot, 0],
            dst_ref=target.at[slot, 1],
            send_sem=self.x_sends.at[at, slot],
            recv_sem=self.x_receives.at[at, slot],
            device_id={"x": 1 - self.at_x},
            device_id_type=MESH_ID,
        )

    def hops(self, at, turn, act):
        slot = self.order[turn]
        for rising in (True, False):
            inside = self.at_z < 3 if rising else self.at_z > 0
            if turn:
                below = slot <= self.at_z
                inside = jnp.logical_and(inside, below if rising else jnp.logical_not(below))
            send = turn + 1 if turn else int(rising)

            @pl.when(inside)
            def _():
                act(self.hop(at, jnp.int32(slot) if not turn else slot, rising, send))

    def begin(self, at):
        self.hops(at, 0, lambda copy: copy.start())

    def arrive(self, at, turn):
        slot = self.order[turn]
        target = self.targets[at]
        pltpu.make_async_remote_copy(
            src_ref=target.at[slot, 0],
            dst_ref=target.at[slot, 0],
            send_sem=self.z_sends.at[at, 0],
            recv_sem=self.z_receives.at[at, slot],
            device_id={"x": 1 - self.at_x},
            device_id_type=MESH_ID,
        ).wait_recv()
        self.hops(at, turn, lambda copy: copy.start())
        self.cross(at, slot).start()

    def finish(self):
        for at in range(3):
            for turn in range(4):
                self.hops(at, turn, lambda copy: copy.wait_send())
                self.cross(at, turn).wait_send()


def front_part(
    wires, head_piece, up_piece, down_piece, tokens, cotangent, time_row, ids_col, ids_row,
    w_head, w_up, w_down, emb, proj, ctx, w_out, hid, pre, act, normed_one, inverse_one, hidden, vecs, upstream,
    tok, send_c, recv_c, send_y, recv_y, keep, acc, local_sem, gather_sems,
):
    at_x, at_core, at_z, at_y = spots()
    low, f32 = jnp.bfloat16, jnp.float32
    length, width = emb.shape
    quarter, half = length // 4, width // 2
    zs = w_head.shape[0]
    span = half + 2 * TILE
    head_size = ctx.shape[2]
    in_size = 3 * head_size

    kept, lent = [], []
    for at, (piece, target) in enumerate(((head_piece, w_head), (up_piece, w_up), (down_piece, w_down))):
        size = piece.shape[1]
        place = target.at[0, 0, pl.ds(pl.multiple_of(at_core * size, size), size)]
        local = pltpu.make_async_copy(piece.at[at_core], place, local_sem.at[at])
        local.start()
        remote = wires.make(piece.at[1 - at_core], place, core=1 - at_core)
        remote.start()
        kept.append(local)
        lent.append(remote)
    relay = Relay((w_head, w_up, w_down), *gather_sems)

    holds = at_core == lax.div(at_z, 2)
    start = lax.rem(at_z, 2) * length
    here, there = [], []
    for r in range(4):
        for h in range(2):
            spot = tok.at[pl.ds(r * quarter, quarter), pl.ds(pl.multiple_of(flipped(at_x, h) * half, half), half)]

            def source(core):
                at = flipped(core, r // 2) * 2 + flipped(at_y, r % 2)
                return tokens.at[pl.ds(pl.multiple_of(start + at * quarter, quarter), quarter), pl.ds(h * half, half)]

            here.append(pltpu.make_async_copy(source(at_core), spot, local_sem.at[3 + 2 * r + h]))
            there.append(wires.make(source(1 - at_core), spot, core=1 - at_core))
    for h in range(2):
        spot = upstream.at[:, pl.ds(pl.multiple_of(flipped(at_x, h) * half, half), half)]

        def above(core):
            at = start + (core * 2 + at_y) * quarter
            return cotangent.at[pl.ds(pl.multiple_of(at, quarter), quarter), pl.ds(h * half, half)]

        here.append(pltpu.make_async_copy(above(at_core), spot, local_sem.at[11 + h]))
        there.append(wires.make(above(1 - at_core), spot, core=1 - at_core))

    @pl.when(holds)
    def _():
        for near, far in zip(here, there):
            near.start()
            far.start()

    for at in range(3):
        kept[at].wait()
        lent[at].wait_recv()
        relay.begin(at)
        if at == 0:
            relay.cross(0, 0).start()

    @pl.when(holds)
    def _():
        for near in here:
            near.wait()

    @pl.when(jnp.logical_not(holds))
    def _():
        for far in there:
            far.wait_recv()

    def embed(rows):
        emb[rows, :] = (tok[rows, :].astype(f32) + time_row[...]).astype(low)

    row_loop(length, 32, embed)

    def small(s, side):
        size = half // 2 + TILE
        return (
            w_head[s, side, half // 2 : size, :].astype(f32)
            + w_head[s, side, size + half // 2 : 2 * size, :].astype(f32)
        )

    for turn in range(zs):
        s = relay.order[turn]
        if turn + 1 < zs:
            relay.arrive(0, turn + 1)
        if turn == 2:
            relay.cross(1, 0).start()
        relay.cross(0, s).wait_recv()
        bias = (small(s, 0) + small(s, 1))[0:1, :in_size]
        size = half // 2 + TILE

        def project(rows):
            total = bias
            for side in range(2):
                for core in range(2):
                    at = side * half + core * (half // 2)
                    total = total + dot_f32(
                        emb[rows, at : at + half // 2],
                        w_head[s, side, core * size : core * size + half // 2, :],
                    )[:, :in_size]
            proj[s, rows, :] = total.astype(low)

        row_loop(length, quarter, project)
        keys = proj[s, :, head_size : 2 * head_size]
        values = proj[s, :, 2 * head_size : in_size]

        def attend(rows):
            queries = proj[s, rows, 0:head_size] * jnp.bfloat16(head_size**-0.5)
            scores = dot_f32(queries, keys, ROW_PAIR)
            scores = jnp.where(ids_col[rows, :] == ids_row[...], scores, -1e30)
            highest = jnp.max(scores, axis=1, keepdims=True)
            exponent = jnp.exp(scores - highest)
            totals = jnp.sum(exponent, axis=1, keepdims=True)
            probability = (exponent * (1.0 / totals)).astype(low)
            ctx[s, rows, :] = dot_f32(probability, values).astype(low)

        row_loop(length, quarter, attend)

    for side in range(2):
        tile = small(0, side)
        for k in range(6):
            vecs[k : k + 1, side * half : side * half + half // 2] = tile[2 + k : 3 + k, :]
            vecs[k : k + 1, side * half + half // 2 : (side + 1) * half] = tile[8 + k : 9 + k, :]

    relay.arrive(1, 1)
    relay.arrive(1, 2)
    size = half // 2 + TILE
    for s in range(zs):
        for side in range(2):
            for core in range(2):
                w_out[side, core * (half // 2) : (core + 1) * (half // 2), s * head_size : (s + 1) * head_size] = w_head[
                    s, side, core * size : core * size + half // 2, in_size:
                ]
    bufs = (send_c, recv_c, send_y, recv_y)

    def mixed_part(r, side):
        joined = jnp.concatenate([ctx[s, r * quarter : (r + 1) * quarter, :] for s in range(zs)], axis=1)
        return dot_f32(joined, w_out[side], ROW_PAIR)

    add_rows(wires, mixed_part, keep, acc, bufs, lambda: relay.arrive(1, 3))
    relay.cross(2, 0).start()
    relay.arrive(2, 1)

    def first_norm(rows):
        total = tok[rows, :].astype(f32) + time_row[...] + keep[rows, :] + vecs[2:3, :]
        normed, inverse = norm_stats(total)
        normed_one[rows, :] = normed
        inverse_one[rows, :] = inverse
        value = normed * vecs[0:1, :] + vecs[3:4, :]
        hidden[rows, :] = value
        hid[rows, :] = value.astype(low)

    row_loop(quarter, 32, first_norm)
    to_y, to_core, again = spread_rows(wires, hid, quarter)
    for s in range(zs):
        relay.cross(1, s).wait_recv()
    relay.arrive(2, 2)

    def up(r):
        rows = pl.ds(r * quarter, quarter)

        def one(s):
            lanes = pl.ds(pl.multiple_of(s * (half // 2), half // 2), half // 2)
            shift = (small(s, 0) + small(s, 1))[1:2, :]
            value = dot_f32(hid[rows, 0:half], w_up[s, 0]) + dot_f32(hid[rows, half:], w_up[s, 1]) + shift
            pre[rows, lanes] = value
            act[rows, lanes] = gelu_value(value).astype(low)

        block_loop(zs, one)

    up(0)
    to_core.wait_recv()
    up(2)
    relay.arrive(2, 3)
    to_y.wait_recv()
    again.start()
    up(1)
    again.wait_recv()
    up(3)
    for s in range(zs):
        relay.cross(2, s).wait_recv()

    def down_part(r, side):
        rows = pl.ds(r * quarter, quarter)
        total = dot_f32(act[rows, 0 : half // 2], w_down[0, side], ROW_PAIR)
        for s in range(1, zs):
            total = total + dot_f32(act[rows, s * (half // 2) : (s + 1) * (half // 2)], w_down[s, side], ROW_PAIR)
        return total

    add_rows(wires, down_part, keep, acc, bufs)

    def second(rows):
        hidden[rows, :] += keep[rows, :] + vecs[4:5, :]

    row_loop(quarter, 32, second)

    def finish():
        for at in range(3):
            lent[at].wait_send()
        relay.finish()

        @pl.when(holds)
        def _():
            for far in there:
                far.wait_send()

        for member in (to_y, to_core, again):
            member.wait_send()

    return finish


def plane_sum(wires, value, slots):
    at_x, at_core, at_z, at_y = spots()
    own = at_core * 4 + at_z
    sent = []
    for step in range(8):
        core, turned = step // 4, step % 4
        if step == 0:
            slots[own] = value[...]
            continue
        sent.append(
            wires.make(
                value,
                slots.at[own],
                core=flipped(at_core, core),
                z=lax.rem(at_z + turned, 4),
            )
        )
        sent[-1].start()
    return sent


def plane_total(sent, slots):
    for member in sent:
        member.wait_recv()
    total = slots[0]
    for at in range(1, 8):
        total = total + slots[at]
    return total


class Outlet:
    def __init__(self, own, result, sends, receives, y_sends, y_receives, local):
        self.own, self.result, self.local = own, result, local
        self.sends, self.receives = sends, receives
        self.y_sends, self.y_receives = y_sends, y_receives
        self.at_x, self.at_core, self.at_z, self.at_y = spots()
        self.quarter = own.shape[0]

    def spot(self, place, core, at_y):
        row = (place * 4 + core * 2 + at_y) * self.quarter
        return self.result.at[pl.ds(pl.multiple_of(row, self.quarter), self.quarter)]

    def copy(self, step):
        at = 2 * step + self.at_core
        return pltpu.make_async_remote_copy(
            src_ref=self.own,
            dst_ref=self.spot(lax.rem(self.at_z, 2), self.at_core, self.at_y),
            send_sem=self.sends.at[at],
            recv_sem=self.receives.at[at],
            device_id={"core": lax.div(self.at_z, 2), "z": lax.rem(self.at_z + step, 4)},
            device_id_type=MESH_ID,
        )

    def stay(self):
        return pltpu.make_async_copy(
            self.own, self.spot(lax.rem(self.at_z, 2), self.at_core, self.at_y), self.local
        )

    def start(self):
        home = self.at_core == lax.div(self.at_z, 2)

        @pl.when(home)
        def _():
            self.stay().start()

        @pl.when(jnp.logical_not(home))
        def _():
            self.copy(0).start()

        for step in (1, 3, 2):
            self.copy(step).start()

    def across(self, place, core):
        spot = self.spot(place, core, self.at_y)
        at = place * 2 + core
        return pltpu.make_async_remote_copy(
            src_ref=spot,
            dst_ref=spot,
            send_sem=self.y_sends.at[at],
            recv_sem=self.y_receives.at[at],
            device_id={"y": 1 - self.at_y},
            device_id_type=MESH_ID,
        )

    def forward(self, place, core):
        source = 2 * self.at_core + place
        step = lax.rem(self.at_z - source + 4, 4)
        own = jnp.logical_and(step == 0, self.at_core == core)

        @pl.when(own)
        def _():
            self.stay().wait()

        @pl.when(jnp.logical_not(own))
        def _():
            spot = self.spot(place, core, self.at_y)
            at = 2 * step + core
            pltpu.make_async_remote_copy(
                src_ref=spot,
                dst_ref=spot,
                send_sem=self.sends.at[at],
                recv_sem=self.receives.at[at],
                device_id={"y": 1 - self.at_y},
                device_id_type=MESH_ID,
            ).wait_recv()

        self.across(place, core).start()

    def finish(self):
        home = self.at_core == lax.div(self.at_z, 2)
        for place in range(2):
            for core in range(2):
                self.across(place, core).wait()

        @pl.when(jnp.logical_not(home))
        def _():
            self.copy(0).wait_send()

        for step in range(1, 4):
            self.copy(step).wait_send()


def back_part_of(
    wires, w_head, w_up, w_down, emb, proj, ctx, w_out, hid, pre, act, normed_one, inverse_one, summed, vecs, upstream,
    ids_col, ids_row,
    block_out, input_out, res_head, res_up, res_down, res_tile, feature, norm,
    two, slope, one, grad_ctx, grad_proj, two_full, one_full, send_c, recv_c, send_y, recv_y, keep, acc,
    near_head, far_head, got_head, came_head, near_up, far_up, got_up, came_up, near_down, far_down, got_down, came_down,
    out_one, out_two, feat, slots, scalar, scalar_slots, key_sum, value_sum, y_feat, x_feat, y_scalar, x_scalar,
    out_sem, local_sem,
):
    at_x, at_core, at_z, at_y = spots()
    low, f32 = jnp.bfloat16, jnp.float32
    length, width = emb.shape
    quarter, half = length // 4, width // 2
    zs = w_head.shape[0]
    block = half // 2
    head_size = ctx.shape[2]
    in_size = 3 * head_size
    feat[...] = jnp.zeros_like(feat)

    def lanes(h):
        return pl.ds(pl.multiple_of(flipped(at_x, h) * half, half), half)

    def second_norm(rows):
        normed, inverse = norm_stats(summed[rows, :])
        gain, shift = vecs[1:2, :], vecs[5:6, :]
        value = (normed * gain + shift).astype(low)
        for h in range(2):
            out_one[rows, lanes(h)] = value[:, h * half : (h + 1) * half]
        above = upstream[rows, :].astype(f32)
        grad = norm_back(above * gain, normed, inverse)
        feat[1:2, :] += jnp.sum(above * normed, axis=0, keepdims=True)
        feat[5:6, :] += jnp.sum(above, axis=0, keepdims=True)
        feat[4:5, :] += jnp.sum(grad, axis=0, keepdims=True)
        two_full[rows, :] = grad
        two[rows, :] = grad.astype(low)

    row_loop(quarter, 32, second_norm)
    to_y, to_core, again = spread_rows(wires, two, quarter)
    outlets = [
        Outlet(own, result, *[out_sem.at[n, k] for k in range(4)], local_sem.at[n])
        for n, (own, result) in enumerate(((out_one, block_out), (out_two, input_out)))
    ]
    outlets[0].start()

    def slopes(r):
        rows = pl.ds(r * quarter, quarter)

        def inner(s):
            units = pl.ds(pl.multiple_of(s * block, block), block)
            value = dot_f32(two[rows, 0:half], w_down[s, 0]) + dot_f32(two[rows, half:], w_down[s, 1])
            slope[rows, units] = (value * gelu_slope(pre[rows, units])).astype(low)

        block_loop(zs, inner)

    slopes(0)
    to_core.wait_recv()
    slopes(2)
    apart = (at_core - lax.div(at_z, 2)) * (at_core - lax.div(at_z, 2))
    close = (1 - apart) * lax.rem(at_z, 2) + apart * (1 - at_core)
    to_y.wait_recv()
    again.start()
    outlets[0].forward(close, 0)
    slopes(1)
    again.wait_recv()
    slopes(3)
    ended = [to_y, to_core, again]

    def group(near, far, got, came):
        crossed = [wires.make(far.at[s], got.at[s], x=1 - at_x) for s in range(zs)]
        turned = [
            wires.make(far.at[s], came.at[s - 1], z=lax.rem(at_z + zs - s, zs)) for s in range(1, zs)
        ]
        return near, far, got, crossed, turned, came

    groups = {
        "head": group(near_head, far_head, got_head, came_head),
        "up": group(near_up, far_up, got_up, came_up),
        "down": group(near_down, far_down, got_down, came_down),
    }

    def weight_grads(name, left, right):
        near, far, got, crossed, turned, came = groups[name]

        for s in range(zs):
            far[s] = dot_f32(left[:, half:], right[:, s * block : (s + 1) * block], COL_PAIR).astype(low)
            crossed[s].start()

        def inner(s):
            units = pl.ds(pl.multiple_of(s * block, block), block)
            near[s] = dot_f32(left[:, 0:half], right[:, units], COL_PAIR)

        block_loop(zs, inner)

    def turn_blocks(name):
        near, far, got, crossed, turned, came = groups[name]
        size = near.shape[1]
        for s in range(zs):
            crossed[s].wait()

        def inner(s):
            def add(rows):
                near[s, rows, :] += got[s, rows, :].astype(f32)
                far[s, rows, :] = near[s, rows, :].astype(low)

            row_loop(size, 16, add)

        block_loop(zs, inner)

    def start_turns(name):
        for member in groups[name][4]:
            member.start()

    def settle(name):
        near, far, got, crossed, turned, came = groups[name]
        size = near.shape[1]
        for member in turned:
            member.wait()

        def add(rows):
            total = near[0, rows, :]
            for s in range(1, zs):
                total = total + came[s - 1, rows, :].astype(f32)
            near[0, rows, :] = total

        row_loop(size, 16, add)

    bufs = (send_c, recv_c, send_y, recv_y)

    def back_part(r, side):
        rows = pl.ds(r * quarter, quarter)
        total = dot_f32(slope[rows, 0:block], w_up[0, side], ROW_PAIR)
        for s in range(1, zs):
            total = total + dot_f32(slope[rows, s * block : (s + 1) * block], w_up[s, side], ROW_PAIR)
        return total

    add_rows(wires, back_part, keep, acc, bufs, lambda: weight_grads("down", two, act))

    def first_norm(rows):
        grad_hidden = keep[rows, :] + two_full[rows, :]
        normed = normed_one[rows, :]
        grad = norm_back(grad_hidden * vecs[0:1, :], normed, inverse_one[rows, :])
        feat[0:1, :] += jnp.sum(grad_hidden * normed, axis=0, keepdims=True)
        feat[3:4, :] += jnp.sum(grad_hidden, axis=0, keepdims=True)
        feat[2:3, :] += jnp.sum(grad, axis=0, keepdims=True)
        one_full[rows, :] = grad
        one[rows, :] = grad.astype(low)

    row_loop(quarter, 32, first_norm)
    to_y, to_core, again = spread_rows(wires, one, quarter)
    ended += [to_y, to_core, again]
    feat_sent = plane_sum(wires, feat, slots)
    weight_grads("up", hid, slope)

    def contexts(r):
        rows = pl.ds(r * quarter, quarter)
        value = dot_f32(one[rows, 0:half], w_out[0]) + dot_f32(one[rows, half:], w_out[1])
        value = value.astype(low)
        for s in range(zs):
            grad_ctx[s, rows, :] = value[:, s * head_size : (s + 1) * head_size]

    contexts(0)
    to_core.wait_recv()
    contexts(2)
    to_y.wait_recv()
    again.start()
    contexts(1)
    turn_blocks("down")
    start_turns("down")
    again.wait_recv()
    contexts(3)
    outlets[0].forward(close, 1)
    outlets[0].forward(1 - close, 0)
    outlets[0].forward(1 - close, 1)
    scale = head_size**-0.5

    def attend(s):
        keys = proj[s, :, head_size : 2 * head_size]
        values = proj[s, :, 2 * head_size : in_size]
        key_sum[...] = jnp.zeros_like(key_sum)
        value_sum[...] = jnp.zeros_like(value_sum)

        def inner(rows):
            queries = proj[s, rows, 0:head_size] * low(scale)
            grads = grad_ctx[s, rows, :]
            scores = dot_f32(keys, queries, ROW_PAIR)
            scores = jnp.where(ids_col[...] == ids_row[0:1, rows], scores, -1e30)
            highest = jnp.max(scores, axis=0, keepdims=True)
            exponent = jnp.exp(scores - highest)
            probability = exponent * (1.0 / jnp.sum(exponent, axis=0, keepdims=True))
            grad_prob = dot_f32(values, grads, ROW_PAIR)
            weighted = jnp.sum(probability * grad_prob, axis=0, keepdims=True)
            grad_score = (probability * (grad_prob - weighted)).astype(low)
            value_sum[...] += dot_f32(probability.astype(low), grads)
            key_sum[...] += dot_f32(grad_score, queries)
            grad_query = dot_f32(grad_score, keys, COL_PAIR)
            grad_proj[s, rows, 0:head_size] = (grad_query * scale).astype(low)

        row_loop(length, quarter, inner)
        grad_proj[s, :, head_size : 2 * head_size] = key_sum[...].astype(low)
        grad_proj[s, :, 2 * head_size : in_size] = value_sum[...].astype(low)

    block_loop(2, attend)
    turn_blocks("up")
    start_turns("up")
    block_loop(2, lambda s: attend(s + 2))

    size = block + TILE

    def input_part(r, side):
        rows = pl.ds(r * quarter, quarter)
        parts = []
        for core in range(2):
            total = None
            for s in range(zs):
                value = dot_f32(
                    grad_proj[s, rows, :], w_head[s, side, core * size : core * size + block, 0:in_size], ROW_PAIR
                )
                total = value if total is None else total + value
            parts.append(total)
        return jnp.concatenate(parts, axis=1)

    near, far, got, crossed, turned, came = groups["head"]

    def head_far():
        for s in range(zs):
            far[s, 0:half, 0:in_size] = dot_f32(emb[:, half:], grad_proj[s], COL_PAIR).astype(low)
            far[s, 0:half, in_size:] = dot_f32(one[:, half:], ctx[s], COL_PAIR).astype(low)
            sums = jnp.sum(grad_proj[s].astype(f32), axis=0, keepdims=True)
            near[s, half:, :] = jnp.zeros((TILE, near.shape[2]), f32)
            near[s, half : half + 1, 0:head_size] = sums[:, 0:head_size]
            near[s, half : half + 1, 2 * head_size : in_size] = sums[:, 2 * head_size :]
            near[s, half + 1 : half + 2, :] = jnp.sum(
                slope[:, s * block : (s + 1) * block].astype(f32), axis=0, keepdims=True
            )
            far[s, half:, :] = near[s, half:, :].astype(low)
            crossed[s].start()

    add_rows(wires, input_part, keep, acc, bufs, head_far)

    def leave(rows):
        value = (keep[rows, :] + one_full[rows, :]).astype(low)
        for h in range(2):
            out_two[rows, lanes(h)] = value[:, h * half : (h + 1) * half]

    row_loop(quarter, 32, leave)
    outlets[1].start()

    def head_near(s):
        near[s, 0:half, 0:in_size] = dot_f32(emb[:, 0:half], grad_proj[s], COL_PAIR)
        near[s, 0:half, in_size:] = dot_f32(one[:, 0:half], ctx[s], COL_PAIR)

    block_loop(zs, head_near)
    turn_blocks("head")
    start_turns("head")

    acc[0:8, :] = plane_total(feat_sent, slots)
    y_copy = wires.make(acc.at[pl.ds(0, 8)], y_feat, y=1 - at_y)
    y_copy.start()
    y_copy.wait_recv()
    feat_all = acc[0:8, :] + y_feat[...]
    keep[0:8, :] = feat_all
    x_copy = wires.make(keep.at[pl.ds(0, 8), pl.ds(half, half)], x_feat, x=1 - at_x)
    x_copy.start()
    x_copy.wait_recv()
    feature[...] = feat_all[:, 0:half] + x_feat[...]

    settle("down")
    settle("up")
    for place in range(2):
        for core in range(2):
            outlets[1].forward(place, core)
    settle("head")

    backs = []
    results = (("head", res_head), ("up", res_up), ("down", res_down))
    for at, (name, result) in enumerate(results):
        near = groups[name][0]
        mine = near.at[0, pl.ds(pl.multiple_of(at_core * block, block), block)]
        other = near.at[0, pl.ds(pl.multiple_of((1 - at_core) * block, block), block)]
        place = result.at[at_core]
        if name != "head":
            place = result.at[:, pl.ds(pl.multiple_of(at_core * block, block), block)]
        local = pltpu.make_async_copy(mine, place, local_sem.at[2 + at])
        local.start()
        remote = wires.make(other, place, core=1 - at_core)
        remote.start()
        backs += [local, remote]
    tile = near_head.at[0, pl.ds(half, TILE)]
    local = pltpu.make_async_copy(tile, res_tile.at[at_core], local_sem.at[5])
    remote = wires.make(tile, res_tile.at[at_core], core=1 - at_core)
    local.start()
    remote.start()
    backs += [local, remote]

    acc[8:16, 0:block] = jnp.zeros((8, block), f32)
    for name, _ in results:
        near = groups[name][0]

        def add(rows):
            value = near[0, rows, :]
            acc[8:16, 0:block] += value * value

        row_loop(half, 8, add)
    value = near_head[0, half : half + 8, :]
    acc[8:16, 0:block] += 0.5 * value * value
    shared = feature[...] * feature[...] * (1.0 / 16.0)
    shared = shared[:, 0:block] + shared[:, block:]
    summed_squares = jnp.sum(acc[8:16, 0:block] + shared)
    scalar[...] = jnp.broadcast_to(summed_squares, scalar.shape)
    scalar_sent = plane_sum(wires, scalar, scalar_slots)
    value = plane_total(scalar_sent, scalar_slots)
    norm[...] = value
    y_two = wires.make(norm, y_scalar, y=1 - at_y)
    y_two.start()
    y_two.wait()
    value = value + y_scalar[...]
    send_scalar = scalar_slots.at[8]
    send_scalar[...] = value
    x_two = wires.make(send_scalar, x_scalar, x=1 - at_x)
    x_two.start()
    x_two.wait()
    norm[...] = value + x_scalar[...]

    for member in ended + feat_sent + scalar_sent + [y_copy, x_copy]:
        member.wait_send()
    for member in backs:
        member.wait()
    for outlet in outlets:
        outlet.finish()


def layer_kernel(
    head_piece, up_piece, down_piece, tokens, cotangent, time_row, ids_col, ids_row,
    block_out, input_out, res_head, res_up, res_down, res_tile, feature, norm,
    w_head, w_up, w_down, emb, proj, ctx, w_out, hid, pre, act, normed_one, inverse_one, hidden, vecs, upstream, tok,
    *rest,
):
    mids, gather_sems = rest[:-9], rest[-4:]
    send_sem, recv_sem, out_sem, local_sem, front_sem = rest[-9:-4]
    shared = mids[7:13]
    wires = Wires(send_sem, recv_sem)
    greet(True)
    finish = front_part(
        wires, head_piece, up_piece, down_piece, tokens, cotangent, time_row, ids_col, ids_row,
        w_head, w_up, w_down, emb, proj, ctx, w_out, hid, pre, act, normed_one, inverse_one, hidden, vecs, upstream,
        tok, *shared, front_sem, gather_sems,
    )
    quarter = hidden.shape[0]
    out_one, out_two = tok.at[pl.ds(2 * quarter, quarter)], tok.at[pl.ds(3 * quarter, quarter)]
    back_part_of(
        wires, w_head, w_up, w_down, emb, proj, ctx, w_out, hid, pre, act, normed_one, inverse_one, hidden, vecs,
        upstream, ids_col, ids_row,
        block_out, input_out, res_head, res_up, res_down, res_tile, feature, norm,
        *mids[:25], out_one, out_two, *mids[25:], out_sem, local_sem,
    )
    finish()


def run_layer(pieces, tokens, cotangent, time_row, ids, head_size):
    low, f32 = jnp.bfloat16, jnp.float32
    length, width = ids.shape[0], tokens.shape[1]
    zs = 4
    quarter, half, block = length // 4, width // 2, width // 4
    units = pieces[1].shape[2]
    vmem = pl.BlockSpec(memory_space=pltpu.VMEM)
    anywhere = pl.BlockSpec(memory_space=pl.ANY)
    shape = jax.ShapeDtypeStruct
    kept = [
        ((zs, 2, half + 2 * TILE, 4 * head_size), low),
        ((zs, 2, half, units), low),
        ((zs, 2, half, units), low),
        ((length, width), low),
        ((zs, length, 3 * head_size), low),
        ((zs, length, head_size), low),
        ((2, half, zs * head_size), low),
        ((length, width), low),
        ((length, zs * units), f32),
        ((length, zs * units), low),
        ((quarter, width), f32),
        ((quarter, 1), f32),
        ((quarter, width), f32),
        ((8, width), f32),
        ((quarter, width), low),
        ((length, width), low),
    ]

    def group(size):
        return [((n, size, block), d) for n, d in ((zs, f32), (zs, low), (zs, low), (zs - 1, low))]

    worked = [
        ((length, width), low),
        ((length, width), low),
        ((length, width), low),
        ((zs, length, head_size), low),
        ((zs, length, 3 * head_size), low),
        ((quarter, width), f32),
        ((quarter, width), f32),
        ((2, quarter, width), low),
        ((2, quarter, width), low),
        ((quarter, width), low),
        ((quarter, width), low),
        ((quarter, width), f32),
        ((quarter, width), f32),
        *group(half + TILE),
        *group(half),
        *group(half),
        ((8, width), f32),
        ((8, 8, width), f32),
        ((8, 128), f32),
        ((9, 8, 128), f32),
        ((length, head_size), f32),
        ((length, head_size), f32),
        ((8, width), f32),
        ((8, half), f32),
        ((8, 128), f32),
        ((8, 128), f32),
    ]
    return pl.pallas_call(
        layer_kernel,
        out_shape=[
            shape(tokens.shape, low),
            shape(tokens.shape, low),
            shape((2, block, block), f32),
            shape((block, 2 * block), f32),
            shape((block, 2 * block), f32),
            shape((2, TILE, block), f32),
            shape((8, half), f32),
            shape((8, 128), f32),
        ],
        in_specs=[vmem] * 3 + [anywhere] * 2 + [vmem] * 3,
        out_specs=[anywhere] * 2 + [vmem] * 6,
        scratch_shapes=[pltpu.VMEM(*member) for member in kept + worked]
        + [
            pltpu.SemaphoreType.DMA((128,)),
            pltpu.SemaphoreType.DMA((128,)),
            pltpu.SemaphoreType.DMA((2, 4, 8)),
            pltpu.SemaphoreType.DMA((6,)),
            pltpu.SemaphoreType.DMA((16,)),
            pltpu.SemaphoreType.DMA((3, 6)),
            pltpu.SemaphoreType.DMA((3, 4)),
            pltpu.SemaphoreType.DMA((3, 4)),
            pltpu.SemaphoreType.DMA((3, 4)),
        ],
        compiler_params=pltpu.CompilerParams(
            collective_id=0, has_side_effects=True, vmem_limit_bytes=67000000
        ),
        name="layer",
    )(*pieces, tokens, cotangent, time_row, ids[:, None], ids[None, :])


def on_grid(*arguments):
    tokens, time_embed, segment_ids, cotangent = arguments[:4]
    masters, moments, squares = arguments[4::3], arguments[5::3], arguments[6::3]
    input_weight, output_weight, upward_weight, downward_weight = masters[:4]
    head_bias, hidden_bias, norm_gains, branch_biases = masters[4:]
    at_x, at_core = lax.axis_index("x"), lax.axis_index("core")
    at_z, at_y = lax.axis_index("z"), lax.axis_index("y")
    first_core, first_x = at_core == 0, at_x == 0
    swapped = at_x == 1
    low = jnp.bfloat16
    f32 = jnp.float32
    length = segment_ids.shape[1]
    head_size = head_bias.shape[0] * 4 // 2
    zs = 4
    place = at_core * 2 + at_y
    quarter = length // 4

    rows = input_weight.shape[0]
    wide = upward_weight.shape[1] // 2
    packed = 4 * head_size
    small_rows = head_bias.shape[0]

    position = at_x * 2 + at_core
    vectors = jnp.concatenate([norm_gains, branch_biases], axis=1).T
    vectors = lax.dynamic_update_slice(
        jnp.zeros((TILE, rows), f32), vectors, (2 + 6 * at_core, 0)
    )

    def head_piece(half):
        body = jnp.concatenate(
            [
                input_weight[:, half * 3 * head_size : (half + 1) * 3 * head_size],
                output_weight[:, half * head_size : (half + 1) * head_size],
            ],
            axis=1,
        )
        tile = lax.dynamic_update_slice(
            vectors, head_bias[:, half][None], (0, at_x * 2 * head_size + at_core * small_rows)
        )
        units = lax.dynamic_update_slice(
            jnp.zeros((2, 4 * small_rows), f32),
            hidden_bias[:, 2 * half : 2 * half + 2].T,
            (0, position * small_rows),
        )
        tile = lax.dynamic_update_slice(tile, units.reshape(1, -1), (1, 0))
        return jnp.concatenate([body, tile], axis=0)

    pieces = [
        jnp.stack([head_piece(0), head_piece(1)]).astype(low),
        jnp.stack([upward_weight[:, :wide], upward_weight[:, wide:]]).astype(low),
        jnp.stack([downward_weight[:, :wide], downward_weight[:, wide:]]).astype(low),
    ]

    seat = ("core", "z")
    holds = at_core == at_z // 2
    lend = [((i // 2) * zs + i, (1 - i // 2) * zs + i) for i in range(zs)]

    def borrow(kept, sent):
        return jnp.where(holds, kept, lax.ppermute(sent, seat, lend))

    local = at_z % 2
    own_time = lax.dynamic_slice_in_dim(time_embed, local, 1, 0)
    own_time = borrow(own_time, own_time)
    own_ids = lax.dynamic_slice_in_dim(segment_ids, local, 1, 0)
    own_ids = borrow(own_ids, own_ids)[0]

    def relative(values):
        return jnp.concatenate(
            [lax.dynamic_slice_in_dim(values, (place ^ turnover) * quarter, quarter, 0) for turnover in range(4)],
            axis=0,
        )

    time_row = swap_halves(own_time.astype(f32), swapped)
    segments = relative(own_ids)

    block_output, input_grad, res_head, sent_up, sent_down, tiles, feature, norm = run_layer(
        pieces, tokens, cotangent, time_row, segments, head_size
    )
    in_size = 3 * head_size
    sent_in = jnp.concatenate([res_head[0, :, :in_size], res_head[1, :, :in_size]], axis=1)
    sent_out = jnp.concatenate([res_head[0, :, in_size:], res_head[1, :, in_size:]], axis=1)
    sent_head = lax.dynamic_slice(
        tiles[:, 0], (0, at_x * 2 * head_size + at_core * small_rows), (2, small_rows)
    ).T
    units = lax.dynamic_slice(
        tiles[:, 1].reshape(4, 4 * small_rows), (0, position * small_rows), (4, small_rows)
    )
    sent_unit = units.T
    feature = lax.dynamic_slice(feature, (0, at_core * rows), (8, rows))
    sent_gains, sent_shifts = feature[0:2].T, feature[2:6].T
    grad_norm = jnp.sqrt(norm[0, 0])
    gradients = (sent_in, sent_out, sent_up, sent_down, sent_head, sent_unit, sent_gains, sent_shifts)
    factor = CLIP / jnp.maximum(grad_norm, CLIP)
    results = [block_output, input_grad.astype(f32), grad_norm.reshape(1)]
    for position in range(8):
        results += adam_update(
            masters[position],
            moments[position],
            squares[position],
            gradients[position] * factor,
            RATES[position],
            DECAYS[position],
        )
    return tuple(results)


def solution(mesh):
    plain = mesh.shape["rows"] != 4 or mesh.shape["tp"] != 8
    if plain:
        rows, tp = "rows", "tp"
        grid, work = mesh, on_device
    else:
        rows, tp = ("x", "core"), ("z", "y")
        grid = Mesh(mesh.devices.reshape(2, 2, 4, 2), ("x", "core", "z", "y"))
        work = on_grid
    narrow, split = P(rows, None), P(rows, tp)
    return jax.shard_map(
        work,
        mesh=grid,
        in_specs=(narrow,) * 4 + (split,) * 18 + (narrow,) * 6,
        out_specs=(narrow, narrow, P()) + (split,) * 18 + (narrow,) * 6,
        check_vma=False,
    )
```

```python
from functools import partial, reduce

import jax
import jax.numpy as jnp
from jax import lax
from jax.experimental import pallas as pl
from jax.experimental.pallas import tpu as pltpu
from jax.sharding import Mesh
from jax.sharding import PartitionSpec as P

HD = 64
STEP = 10


NORM_EPS = 1e-05
BETA_ONE = 0.9
BETA_TWO = 0.999
ADAM_EPS = 1e-08
CLIP = 1.0
RATES = (0.1, 0.4, 0.1, 0.05, 0.5, 0.5, 0.5, 0.5)
DECAYS = (0.01, 0.01, 0.01, 0.01, 0.0, 0.0, 0.0, 0.0)
ROW_PAIR = (((1,), (1,)), ((), ()))
COL_PAIR = (((0,), (0,)), ((), ()))


def norm_stats(summed):
    average = jnp.mean(summed, axis=-1, keepdims=True)
    centered = summed - average
    inverse = lax.rsqrt(jnp.mean(centered * centered, axis=-1, keepdims=True) + NORM_EPS)
    return (centered * inverse, inverse)


def norm_back(grad_normed, normed, inverse):
    first_mean = jnp.mean(grad_normed, axis=-1, keepdims=True)
    second_mean = jnp.mean(grad_normed * normed, axis=-1, keepdims=True)
    return inverse * (grad_normed - first_mean - normed * second_mean)


def gelu_value(inputs):
    return 0.5 * inputs * (1.0 + jax.scipy.special.erf(inputs * 0.7071067811865476))


def gelu_slope(inputs):
    cumulative = 0.5 * (1.0 + jax.scipy.special.erf(inputs * 0.7071067811865476))
    return cumulative + inputs * jnp.exp(-0.5 * inputs * inputs) * 0.3989422804014327


def masked_scores(queries, key_rows, segments):
    scores = jnp.einsum(
        "qhd,khd->hqk", queries, key_rows, preferred_element_type=jnp.float32
    ) * HD ** (-0.5)
    matching = segments[:, None] == segments[None, :]
    return jnp.where(matching[None], scores, -1e30)


def attend_forward(pieces):
    queries, key_rows, values, segments = pieces
    scores = masked_scores(queries, key_rows, segments)
    highest = jnp.max(scores, axis=-1, keepdims=True)
    exponent = jnp.exp(scores - highest)
    totals = jnp.sum(exponent, axis=-1, keepdims=True)
    probability = (exponent / totals).astype(jnp.bfloat16)
    context = jnp.einsum("hqk,khd->qhd", probability, values, preferred_element_type=jnp.float32)
    return (context, (highest + jnp.log(totals))[..., 0])


def attend_back(pieces):
    queries, key_rows, values, segments, log_total, grad_context = pieces
    scores = masked_scores(queries, key_rows, segments)
    probability = jnp.exp(scores - log_total[..., None])
    grad_prob = jnp.einsum("qhd,khd->hqk", grad_context, values, preferred_element_type=jnp.float32)
    weighted = jnp.sum(probability * grad_prob, axis=-1, keepdims=True)
    grad_score = (probability * (grad_prob - weighted)).astype(jnp.bfloat16)
    grad_query = jnp.einsum(
        "hqk,khd->qhd", grad_score, key_rows, preferred_element_type=jnp.float32
    ) * HD ** (-0.5)
    grad_key = jnp.einsum(
        "hqk,qhd->khd", grad_score, queries, preferred_element_type=jnp.float32
    ) * HD ** (-0.5)
    grad_value = jnp.einsum(
        "hqk,qhd->khd",
        probability.astype(jnp.bfloat16),
        grad_context,
        preferred_element_type=jnp.float32,
    )
    return jnp.stack([grad_query, grad_key, grad_value], axis=2)


def adam_update(weight, moment, square, clipped, rate, decay):
    moment = BETA_ONE * moment + (1.0 - BETA_ONE) * clipped
    square = BETA_TWO * square + (1.0 - BETA_TWO) * clipped * clipped
    corrected = (
        moment / (1.0 - BETA_ONE**STEP) / (jnp.sqrt(square / (1.0 - BETA_TWO**STEP)) + ADAM_EPS)
    )
    return (weight - rate * (corrected + decay * weight), moment, square)


def add_squares(running, member):
    return running + jnp.sum(member * member)


def on_device(
    tokens,
    time_embed,
    segment_ids,
    cotangent,
    input_weight,
    input_moment,
    input_square,
    output_weight,
    output_moment,
    output_square,
    upward_weight,
    upward_moment,
    upward_square,
    downward_weight,
    downward_moment,
    downward_square,
    head_bias,
    head_moment,
    head_square,
    hidden_bias,
    hidden_moment,
    hidden_square,
    norm_gains,
    gains_moment,
    gains_square,
    branch_biases,
    biases_moment,
    biases_square,
):
    masters = (
        input_weight,
        output_weight,
        upward_weight,
        downward_weight,
        head_bias,
        hidden_bias,
        norm_gains,
        branch_biases,
    )
    moments = (
        input_moment,
        output_moment,
        upward_moment,
        downward_moment,
        head_moment,
        hidden_moment,
        gains_moment,
        biases_moment,
    )
    squares = (
        input_square,
        output_square,
        upward_square,
        downward_square,
        head_square,
        hidden_square,
        gains_square,
        biases_square,
    )
    (
        weights_in,
        weights_out,
        weights_up,
        weights_down,
        head_shift,
        unit_shift,
        gains_low,
        shifts_low,
    ) = (
        lax.all_gather(input_weight.astype(jnp.bfloat16), "rows", axis=0, tiled=True),
        lax.all_gather(output_weight.astype(jnp.bfloat16), "rows", axis=0, tiled=True),
        lax.all_gather(upward_weight.astype(jnp.bfloat16), "rows", axis=0, tiled=True),
        lax.all_gather(downward_weight.astype(jnp.bfloat16), "rows", axis=0, tiled=True),
        lax.all_gather(head_bias.astype(jnp.bfloat16), "rows", axis=0, tiled=True),
        lax.all_gather(hidden_bias.astype(jnp.bfloat16), "rows", axis=0, tiled=True),
        lax.all_gather(norm_gains.astype(jnp.bfloat16), "rows", axis=0, tiled=True),
        lax.all_gather(branch_biases.astype(jnp.bfloat16), "rows", axis=0, tiled=True),
    )
    seq_count, length = segment_ids.shape
    width = tokens.shape[1]
    num_heads = head_shift.shape[1]
    head_size = head_shift.shape[0] // 2
    tok_rows = seq_count * length
    gains = gains_low.astype(jnp.float32)
    shifts = shifts_low.astype(jnp.float32)
    embedded = (
        tokens.astype(jnp.float32).reshape(seq_count, length, width)
        + time_embed.astype(jnp.float32)[:, None, :]
    ).reshape(tok_rows, width)
    embedded_low = embedded.astype(jnp.bfloat16)
    head_float = head_shift.astype(jnp.float32)
    offset = jnp.stack(
        [
            head_float[:head_size].T,
            jnp.zeros((num_heads, head_size), jnp.float32),
            head_float[head_size:].T,
        ],
        axis=1,
    )
    projected = jnp.dot(embedded_low, weights_in, preferred_element_type=jnp.float32).reshape(
        tok_rows, num_heads, 3, head_size
    )
    projected = (
        (projected + offset)
        .astype(jnp.bfloat16)
        .reshape(seq_count, length, num_heads, 3, head_size)
    )
    queries = projected[:, :, :, 0]
    key_rows = projected[:, :, :, 1]
    values = projected[:, :, :, 2]
    context, log_total = lax.map(attend_forward, (queries, key_rows, values, segment_ids))
    context_low = context.reshape(tok_rows, num_heads * head_size).astype(jnp.bfloat16)
    mixed_part = lax.dot_general(
        context_low, weights_out, ROW_PAIR, preferred_element_type=jnp.float32
    )
    mixed = lax.psum(mixed_part, "tp")
    normed_one, inverse_one = norm_stats(embedded + mixed + shifts[:, 0])
    hidden = normed_one * gains[:, 0] + shifts[:, 1]
    hidden_low = hidden.astype(jnp.bfloat16)
    unit_offset = unit_shift.astype(jnp.float32).T.reshape(-1)
    pre_act = jnp.dot(hidden_low, weights_up, preferred_element_type=jnp.float32) + unit_offset
    expanded_low = gelu_value(pre_act).astype(jnp.bfloat16)
    reduced_part = lax.dot_general(
        expanded_low, weights_down, ROW_PAIR, preferred_element_type=jnp.float32
    )
    reduced = lax.psum(reduced_part, "tp")
    normed_two, inverse_two = norm_stats(hidden + reduced + shifts[:, 2])
    block_output = (normed_two * gains[:, 1] + shifts[:, 3]).astype(jnp.bfloat16)
    upstream = cotangent.astype(jnp.float32)
    gain_two = jnp.sum(upstream * normed_two, axis=0)
    shift_three = jnp.sum(upstream, axis=0)
    grad_pre_two = norm_back(upstream * gains[:, 1], normed_two, inverse_two)
    shift_two = jnp.sum(grad_pre_two, axis=0)
    grad_pre_two_low = grad_pre_two.astype(jnp.bfloat16)
    grad_down = lax.dot_general(
        grad_pre_two_low, expanded_low, COL_PAIR, preferred_element_type=jnp.float32
    )
    grad_act = jnp.dot(grad_pre_two_low, weights_down, preferred_element_type=jnp.float32)
    grad_pre_act = (grad_act * gelu_slope(pre_act)).astype(jnp.bfloat16)
    unit_sums = jnp.sum(grad_pre_act, axis=0, dtype=jnp.float32)
    grad_unit = unit_sums.reshape(-1, 2 * head_size).T
    grad_up = lax.dot_general(
        hidden_low, grad_pre_act, COL_PAIR, preferred_element_type=jnp.float32
    )
    back_part = lax.dot_general(
        grad_pre_act, weights_up, ROW_PAIR, preferred_element_type=jnp.float32
    )
    grad_hidden = lax.psum(back_part, "tp") + grad_pre_two
    gain_one = jnp.sum(grad_hidden * normed_one, axis=0)
    shift_one = jnp.sum(grad_hidden, axis=0)
    grad_pre_one = norm_back(grad_hidden * gains[:, 0], normed_one, inverse_one)
    shift_zero = jnp.sum(grad_pre_one, axis=0)
    grad_pre_one_low = grad_pre_one.astype(jnp.bfloat16)
    grad_out = lax.dot_general(
        grad_pre_one_low, context_low, COL_PAIR, preferred_element_type=jnp.float32
    )
    grad_context = jnp.dot(
        grad_pre_one_low, weights_out, preferred_element_type=jnp.float32
    ).astype(jnp.bfloat16)
    grad_context = grad_context.reshape(seq_count, length, num_heads, head_size)
    grad_projected = lax.map(
        attend_back, (queries, key_rows, values, segment_ids, log_total, grad_context)
    )
    grad_projected = grad_projected.reshape(tok_rows, num_heads * 3 * head_size).astype(
        jnp.bfloat16
    )
    head_sums = jnp.sum(grad_projected, axis=0, dtype=jnp.float32).reshape(num_heads, 3, head_size)
    grad_head = jnp.concatenate([head_sums[:, 0].T, head_sums[:, 2].T], axis=0)
    grad_in = lax.dot_general(
        embedded_low, grad_projected, COL_PAIR, preferred_element_type=jnp.float32
    )
    input_part = lax.dot_general(
        grad_projected, weights_in, ROW_PAIR, preferred_element_type=jnp.float32
    )
    input_grad = lax.psum(input_part, "tp") + grad_pre_one
    grad_gains = jnp.stack([gain_one, gain_two], axis=1)
    grad_shifts = jnp.stack([shift_zero, shift_one, shift_two, shift_three], axis=1)
    sent_in, sent_out, sent_up, sent_down, sent_head, sent_unit, sent_gains, sent_shifts = (
        lax.psum_scatter(grad_in, "rows", scatter_dimension=0, tiled=True),
        lax.psum_scatter(grad_out, "rows", scatter_dimension=0, tiled=True),
        lax.psum_scatter(grad_up, "rows", scatter_dimension=0, tiled=True),
        lax.psum_scatter(grad_down, "rows", scatter_dimension=0, tiled=True),
        lax.psum_scatter(grad_head, "rows", scatter_dimension=0, tiled=True),
        lax.psum_scatter(grad_unit, "rows", scatter_dimension=0, tiled=True),
        lax.psum_scatter(grad_gains, "rows", scatter_dimension=0, tiled=True),
        lax.psum_scatter(grad_shifts, "rows", scatter_dimension=0, tiled=True),
    )
    gradients = (
        sent_in,
        sent_out,
        sent_up,
        sent_down,
        sent_head,
        sent_unit,
        sent_gains,
        sent_shifts,
    )
    split_part = reduce(
        add_squares,
        (sent_in, sent_out, sent_up, sent_down, sent_head, sent_unit),
        jnp.zeros((), jnp.float32),
    )
    copied_part = (
        jnp.sum(sent_gains * sent_gains) + jnp.sum(sent_shifts * sent_shifts)
    ) / lax.axis_size("tp")
    grad_norm = jnp.sqrt(lax.psum(split_part + copied_part, ("rows", "tp")))
    factor = CLIP / jnp.maximum(grad_norm, CLIP)
    updated = [
        adam_update(
            masters[position],
            moments[position],
            squares[position],
            gradients[position] * factor,
            RATES[position],
            DECAYS[position],
        )
        for position in range(8)
    ]
    return (
        block_output,
        input_grad,
        grad_norm.reshape(1),
        updated[0][0],
        updated[0][1],
        updated[0][2],
        updated[1][0],
        updated[1][1],
        updated[1][2],
        updated[2][0],
        updated[2][1],
        updated[2][2],
        updated[3][0],
        updated[3][1],
        updated[3][2],
        updated[4][0],
        updated[4][1],
        updated[4][2],
        updated[5][0],
        updated[5][1],
        updated[5][2],
        updated[6][0],
        updated[6][1],
        updated[6][2],
        updated[7][0],
        updated[7][1],
        updated[7][2],
    )


def flip(value, axis):
    return lax.ppermute(value, axis, [(0, 1), (1, 0)])


def turn(value, amount, count):
    return lax.ppermute(value, "z", [(i, (i + amount) % count) for i in range(count)])


def swap_halves(value, swapped):
    half = value.shape[-1] // 2
    return jnp.where(
        swapped, jnp.concatenate([value[..., half:], value[..., :half]], axis=-1), value
    )


def in_order(first, mine, other):
    return jnp.where(
        first, jnp.concatenate([mine, other], axis=0), jnp.concatenate([other, mine], axis=0)
    )


MESH_ID = pl.DeviceIdType.MESH
TILE = 16


class Wires:
    def __init__(self, sends, receives):
        self.sends, self.receives, self.used = sends, receives, 0

    def make(self, source, target, **device):
        at = self.used
        self.used += 1
        return pltpu.make_async_remote_copy(
            src_ref=source,
            dst_ref=target,
            send_sem=self.sends.at[at],
            recv_sem=self.receives.at[at],
            device_id=device,
            device_id_type=MESH_ID,
        )


def spots():
    return (lax.axis_index("x"), lax.axis_index("core"), lax.axis_index("z"), lax.axis_index("y"))


def greet(full):
    at_x, at_core, at_z, at_y = spots()
    barrier = pltpu.get_barrier_semaphore()
    count = 0

    def call(**device):
        pl.semaphore_signal(barrier, inc=1, device_id=device, device_id_type=MESH_ID)

    for step in range(4):
        if step:
            call(z=lax.rem(at_z + step, 4))
            count += 1
        if full or step == 0:
            call(core=1 - at_core, z=lax.rem(at_z + step, 4))
            count += 1
    call(x=1 - at_x)
    call(y=1 - at_y)
    pl.semaphore_wait(barrier, count + 2)


def flipped(value, bit):
    return 1 - value if bit else value


def row_loop(count, step, body):
    def inner(at, carry):
        body(pl.ds(pl.multiple_of(at * step, step), step))
        return carry

    lax.fori_loop(0, count // step, inner, 0)


def block_loop(count, body):
    def inner(at, carry):
        body(at)
        return carry

    lax.fori_loop(0, count, inner, 0)


def dot_f32(left, right, pairing=(((1,), (0,)), ((), ()))):
    return lax.dot_general(left, right, pairing, preferred_element_type=jnp.float32)


def spread_rows(wires, ref, quarter):
    _, at_core, _, at_y = spots()
    own, near = ref.at[pl.ds(0, quarter)], ref.at[pl.ds(quarter, quarter)]
    to_y = wires.make(own, near, y=1 - at_y)
    to_core = wires.make(own, ref.at[pl.ds(2 * quarter, quarter)], core=1 - at_core)
    again = wires.make(near, ref.at[pl.ds(3 * quarter, quarter)], core=1 - at_core)
    to_y.start()
    to_core.start()
    return to_y, to_core, again


def add_rows(wires, part, keep, acc, bufs, fill=None):
    _, at_core, _, at_y = spots()
    send_c, recv_c, send_y, recv_y = bufs
    low = jnp.bfloat16
    half = keep.shape[1] // 2
    sides = [pl.ds(0, half), pl.ds(half, half)]
    far = [wires.make(send_c.at[b], recv_c.at[b], core=1 - at_core) for b in range(2)]
    across = wires.make(send_y, recv_y, y=1 - at_y)
    for b, r in ((1, 3), (0, 2)):
        for side in range(2):
            send_c[b, :, sides[side]] = part(r, side).astype(low)
        far[b].start()
    for side in range(2):
        acc[:, sides[side]] = part(1, side)
    far[1].wait_recv()

    def to_send(rows):
        send_y[rows, :] = (acc[rows, :] + recv_c[1, rows, :].astype(jnp.float32)).astype(low)

    row_loop(keep.shape[0], 32, to_send)
    across.start()
    for side in range(2):
        keep[:, sides[side]] = part(0, side)
    far[0].wait_recv()
    if fill is not None:
        fill()
    across.wait_recv()

    def finish(rows):
        keep[rows, :] += recv_c[0, rows, :].astype(jnp.float32) + recv_y[rows, :].astype(jnp.float32)

    row_loop(keep.shape[0], 32, finish)
    far[0].wait_send()
    far[1].wait_send()
    across.wait_send()


class Relay:
    def __init__(self, targets, z_sends, z_receives, x_sends, x_receives):
        self.targets, self.z_sends, self.z_receives = targets, z_sends, z_receives
        self.x_sends, self.x_receives = x_sends, x_receives
        self.at_x, _, self.at_z, _ = spots()
        middle = lax.rem(lax.div(self.at_z + 1, 2), 2)
        first = 3 - 2 * lax.rem(self.at_z, 2)
        second = 2 * (1 - middle) + middle * (4 - first)
        self.order = [0, first, second, 6 - first - second]

    def hop(self, at, slot, rising, send):
        to = lax.rem(slot + (1 if rising else 3), 4)
        target = self.targets[at]
        return pltpu.make_async_remote_copy(
            src_ref=target.at[slot, 0],
            dst_ref=target.at[to, 0],
            send_sem=self.z_sends.at[at, send],
            recv_sem=self.z_receives.at[at, to],
            device_id={"z": self.at_z + (1 if rising else -1)},
            device_id_type=MESH_ID,
        )

    def cross(self, at, slot):
        target = self.targets[at]
        return pltpu.make_async_remote_copy(
            src_ref=target.at[slot, 0],
            dst_ref=target.at[slot, 1],
            send_sem=self.x_sends.at[at, slot],
            recv_sem=self.x_receives.at[at, slot],
            device_id={"x": 1 - self.at_x},
            device_id_type=MESH_ID,
        )

    def hops(self, at, turn, act):
        slot = self.order[turn]
        for rising in (True, False):
            inside = self.at_z < 3 if rising else self.at_z > 0
            if turn:
                below = slot <= self.at_z
                inside = jnp.logical_and(inside, below if rising else jnp.logical_not(below))
            send = turn + 1 if turn else int(rising)

            @pl.when(inside)
            def _():
                act(self.hop(at, jnp.int32(slot) if not turn else slot, rising, send))

    def begin(self, at):
        self.hops(at, 0, lambda copy: copy.start())

    def arrive(self, at, turn):
        slot = self.order[turn]
        target = self.targets[at]
        pltpu.make_async_remote_copy(
            src_ref=target.at[slot, 0],
            dst_ref=target.at[slot, 0],
            send_sem=self.z_sends.at[at, 0],
            recv_sem=self.z_receives.at[at, slot],
            device_id={"x": 1 - self.at_x},
            device_id_type=MESH_ID,
        ).wait_recv()
        self.hops(at, turn, lambda copy: copy.start())
        self.cross(at, slot).start()

    def finish(self):
        for at in range(3):
            for turn in range(4):
                self.hops(at, turn, lambda copy: copy.wait_send())
                self.cross(at, turn).wait_send()


def front_part(
    wires, in_full, out_full, up_full, down_full, tiles, tokens, cotangent, times, ids,
    head_piece, up_piece, down_piece, time_row, ids_col, ids_row,
    w_head, w_up, w_down, emb, proj, ctx, w_out, hid, pre, act, normed_one, inverse_one, hidden, vecs, upstream,
    tok, send_c, recv_c, send_y, recv_y, keep, acc, local_sem, gather_sems,
):
    at_x, at_core, at_z, at_y = spots()
    low, f32 = jnp.bfloat16, jnp.float32
    length, width = emb.shape
    quarter, half = length // 4, width // 2
    zs = w_head.shape[0]
    span = half + 2 * TILE
    head_size = ctx.shape[2]
    in_size = 3 * head_size

    split = in_full.shape[1] // 2
    for h in range(2):
        head_piece[h, 0 : half // 2, 0:split] = in_full[:, h * split : (h + 1) * split].astype(low)
        head_piece[h, 0 : half // 2, split:] = out_full[:, h * head_size : (h + 1) * head_size].astype(low)
        head_piece[h, half // 2 :, :] = tiles[h].astype(low)
    for full, piece in ((up_full, up_piece), (down_full, down_piece)):
        for h in range(2):
            piece[h] = full[:, h * piece.shape[2] : (h + 1) * piece.shape[2]].astype(low)

    kept, lent = [], []
    for at, (piece, target) in enumerate(((head_piece, w_head), (up_piece, w_up), (down_piece, w_down))):
        size = piece.shape[1]
        place = target.at[0, 0, pl.ds(pl.multiple_of(at_core * size, size), size)]
        local = pltpu.make_async_copy(piece.at[at_core], place, local_sem.at[at])
        local.start()
        remote = wires.make(piece.at[1 - at_core], place, core=1 - at_core)
        remote.start()
        kept.append(local)
        lent.append(remote)
    relay = Relay((w_head, w_up, w_down), *gather_sems)

    holds = at_core == lax.div(at_z, 2)
    start = lax.rem(at_z, 2) * length
    here, there = [], []
    for r in range(4):
        for h in range(2):
            spot = tok.at[pl.ds(r * quarter, quarter), pl.ds(pl.multiple_of(flipped(at_x, h) * half, half), half)]

            def source(core):
                at = flipped(core, r // 2) * 2 + flipped(at_y, r % 2)
                return tokens.at[pl.ds(pl.multiple_of(start + at * quarter, quarter), quarter), pl.ds(h * half, half)]

            here.append(pltpu.make_async_copy(source(at_core), spot, local_sem.at[3 + 2 * r + h]))
            there.append(wires.make(source(1 - at_core), spot, core=1 - at_core))
    for h in range(2):
        spot = upstream.at[:, pl.ds(pl.multiple_of(flipped(at_x, h) * half, half), half)]

        def above(core):
            at = start + (core * 2 + at_y) * quarter
            return cotangent.at[pl.ds(pl.multiple_of(at, quarter), quarter), pl.ds(h * half, half)]

        here.append(pltpu.make_async_copy(above(at_core), spot, local_sem.at[11 + h]))
        there.append(wires.make(above(1 - at_core), spot, core=1 - at_core))

    local = lax.rem(at_z, 2)
    for h in range(2):
        source = times.at[local, :, pl.ds(h * half, half)]
        spot = time_row.at[:, pl.ds(pl.multiple_of(flipped(at_x, h) * half, half), half)]
        here.append(pltpu.make_async_copy(source, spot, local_sem.at[13 + h]))
        there.append(wires.make(source, spot, core=1 - at_core))
    for r in range(4):
        spot = ids_row.at[:, pl.ds(r * quarter, quarter)]

        def stretch(core):
            at = flipped(core, r // 2) * 2 + flipped(at_y, r % 2)
            return ids.at[local, :, pl.ds(pl.multiple_of(at * quarter, quarter), quarter)]

        here.append(pltpu.make_async_copy(stretch(at_core), spot, local_sem.at[15 + r]))
        there.append(wires.make(stretch(1 - at_core), spot, core=1 - at_core))

    @pl.when(holds)
    def _():
        for near, far in zip(here, there):
            near.start()
            far.start()

    for at in range(3):
        kept[at].wait()
        lent[at].wait_recv()
        relay.begin(at)
        if at == 0:
            relay.cross(0, 0).start()

    @pl.when(holds)
    def _():
        for near in here:
            near.wait()

    @pl.when(jnp.logical_not(holds))
    def _():
        for far in there:
            far.wait_recv()

    ids_col[...] = jnp.transpose(jnp.broadcast_to(ids_row[...], (8, length)))[:, 0:1]

    def embed(rows):
        emb[rows, :] = (tok[rows, :].astype(f32) + time_row[...]).astype(low)

    row_loop(length, 32, embed)

    def small(s, side):
        size = half // 2 + TILE
        return (
            w_head[s, side, half // 2 : size, :].astype(f32)
            + w_head[s, side, size + half // 2 : 2 * size, :].astype(f32)
        )

    for turn in range(zs):
        s = relay.order[turn]
        if turn + 1 < zs:
            relay.arrive(0, turn + 1)
        if turn == 2:
            relay.cross(1, 0).start()
        relay.cross(0, s).wait_recv()
        bias = (small(s, 0) + small(s, 1))[0:1, :in_size]
        size = half // 2 + TILE

        def project(rows):
            total = bias
            for side in range(2):
                for core in range(2):
                    at = side * half + core * (half // 2)
                    total = total + dot_f32(
                        emb[rows, at : at + half // 2],
                        w_head[s, side, core * size : core * size + half // 2, :],
                    )[:, :in_size]
            proj[s, rows, :] = total.astype(low)

        row_loop(length, quarter, project)
        keys = proj[s, :, head_size : 2 * head_size]
        values = proj[s, :, 2 * head_size : in_size]

        def attend(rows):
            queries = proj[s, rows, 0:head_size] * jnp.bfloat16(head_size**-0.5)
            scores = dot_f32(queries, keys, ROW_PAIR)
            scores = jnp.where(ids_col[rows, :] == ids_row[...], scores, -1e30)
            highest = jnp.max(scores, axis=1, keepdims=True)
            exponent = jnp.exp(scores - highest)
            totals = jnp.sum(exponent, axis=1, keepdims=True)
            probability = (exponent * (1.0 / totals)).astype(low)
            ctx[s, rows, :] = dot_f32(probability, values).astype(low)

        row_loop(length, quarter, attend)

    for side in range(2):
        tile = small(0, side)
        for k in range(6):
            vecs[k : k + 1, side * half : side * half + half // 2] = tile[2 + k : 3 + k, :]
            vecs[k : k + 1, side * half + half // 2 : (side + 1) * half] = tile[8 + k : 9 + k, :]

    relay.arrive(1, 1)
    relay.arrive(1, 2)
    size = half // 2 + TILE
    for s in range(zs):
        for side in range(2):
            for core in range(2):
                w_out[side, core * (half // 2) : (core + 1) * (half // 2), s * head_size : (s + 1) * head_size] = w_head[
                    s, side, core * size : core * size + half // 2, in_size:
                ]
    bufs = (send_c, recv_c, send_y, recv_y)

    def mixed_part(r, side):
        joined = jnp.concatenate([ctx[s, r * quarter : (r + 1) * quarter, :] for s in range(zs)], axis=1)
        return dot_f32(joined, w_out[side], ROW_PAIR)

    add_rows(wires, mixed_part, keep, acc, bufs, lambda: relay.arrive(1, 3))
    relay.cross(2, 0).start()
    relay.arrive(2, 1)

    def first_norm(rows):
        total = tok[rows, :].astype(f32) + time_row[...] + keep[rows, :] + vecs[2:3, :]
        normed, inverse = norm_stats(total)
        normed_one[rows, :] = normed
        inverse_one[rows, :] = inverse
        value = normed * vecs[0:1, :] + vecs[3:4, :]
        hidden[rows, :] = value
        hid[rows, :] = value.astype(low)

    row_loop(quarter, 32, first_norm)
    to_y, to_core, again = spread_rows(wires, hid, quarter)
    for s in range(zs):
        relay.cross(1, s).wait_recv()
    relay.arrive(2, 2)

    def up(r):
        rows = pl.ds(r * quarter, quarter)

        def one(s):
            lanes = pl.ds(pl.multiple_of(s * (half // 2), half // 2), half // 2)
            shift = (small(s, 0) + small(s, 1))[1:2, :]
            value = dot_f32(hid[rows, 0:half], w_up[s, 0]) + dot_f32(hid[rows, half:], w_up[s, 1]) + shift
            pre[rows, lanes] = value
            act[rows, lanes] = gelu_value(value).astype(low)

        block_loop(zs, one)

    up(0)
    to_core.wait_recv()
    up(2)
    relay.arrive(2, 3)
    to_y.wait_recv()
    again.start()
    up(1)
    again.wait_recv()
    up(3)
    for s in range(zs):
        relay.cross(2, s).wait_recv()

    def down_part(r, side):
        rows = pl.ds(r * quarter, quarter)
        total = dot_f32(act[rows, 0 : half // 2], w_down[0, side], ROW_PAIR)
        for s in range(1, zs):
            total = total + dot_f32(act[rows, s * (half // 2) : (s + 1) * (half // 2)], w_down[s, side], ROW_PAIR)
        return total

    add_rows(wires, down_part, keep, acc, bufs)

    def second(rows):
        hidden[rows, :] += keep[rows, :] + vecs[4:5, :]

    row_loop(quarter, 32, second)

    def finish():
        for at in range(3):
            lent[at].wait_send()
        relay.finish()

        @pl.when(holds)
        def _():
            for far in there:
                far.wait_send()

        for member in (to_y, to_core, again):
            member.wait_send()

    return finish


def plane_sum(wires, value, slots):
    at_x, at_core, at_z, at_y = spots()
    own = at_core * 4 + at_z
    sent = []
    for step in range(8):
        core, turned = step // 4, step % 4
        if step == 0:
            slots[own] = value[...]
            continue
        sent.append(
            wires.make(
                value,
                slots.at[own],
                core=flipped(at_core, core),
                z=lax.rem(at_z + turned, 4),
            )
        )
        sent[-1].start()
    return sent


def plane_total(sent, slots):
    for member in sent:
        member.wait_recv()
    total = slots[0]
    for at in range(1, 8):
        total = total + slots[at]
    return total


class Outlet:
    def __init__(self, own, result, sends, receives, y_sends, y_receives, local):
        self.own, self.result, self.local = own, result, local
        self.sends, self.receives = sends, receives
        self.y_sends, self.y_receives = y_sends, y_receives
        self.at_x, self.at_core, self.at_z, self.at_y = spots()
        self.quarter = own.shape[0]

    def spot(self, place, core, at_y):
        row = (place * 4 + core * 2 + at_y) * self.quarter
        return self.result.at[pl.ds(pl.multiple_of(row, self.quarter), self.quarter)]

    def copy(self, step):
        at = 2 * step + self.at_core
        return pltpu.make_async_remote_copy(
            src_ref=self.own,
            dst_ref=self.spot(lax.rem(self.at_z, 2), self.at_core, self.at_y),
            send_sem=self.sends.at[at],
            recv_sem=self.receives.at[at],
            device_id={"core": lax.div(self.at_z, 2), "z": lax.rem(self.at_z + step, 4)},
            device_id_type=MESH_ID,
        )

    def stay(self):
        return pltpu.make_async_copy(
            self.own, self.spot(lax.rem(self.at_z, 2), self.at_core, self.at_y), self.local
        )

    def start(self):
        home = self.at_core == lax.div(self.at_z, 2)

        @pl.when(home)
        def _():
            self.stay().start()

        @pl.when(jnp.logical_not(home))
        def _():
            self.copy(0).start()

        for step in (1, 3, 2):
            self.copy(step).start()

    def across(self, place, core):
        spot = self.spot(place, core, self.at_y)
        at = place * 2 + core
        return pltpu.make_async_remote_copy(
            src_ref=spot,
            dst_ref=spot,
            send_sem=self.y_sends.at[at],
            recv_sem=self.y_receives.at[at],
            device_id={"y": 1 - self.at_y},
            device_id_type=MESH_ID,
        )

    def forward(self, place, core):
        source = 2 * self.at_core + place
        step = lax.rem(self.at_z - source + 4, 4)
        own = jnp.logical_and(step == 0, self.at_core == core)

        @pl.when(own)
        def _():
            self.stay().wait()

        @pl.when(jnp.logical_not(own))
        def _():
            spot = self.spot(place, core, self.at_y)
            at = 2 * step + core
            pltpu.make_async_remote_copy(
                src_ref=spot,
                dst_ref=spot,
                send_sem=self.sends.at[at],
                recv_sem=self.receives.at[at],
                device_id={"y": 1 - self.at_y},
                device_id_type=MESH_ID,
            ).wait_recv()

        self.across(place, core).start()

    def finish(self):
        home = self.at_core == lax.div(self.at_z, 2)
        for place in range(2):
            for core in range(2):
                self.across(place, core).wait()

        @pl.when(jnp.logical_not(home))
        def _():
            self.copy(0).wait_send()

        for step in range(1, 4):
            self.copy(step).wait_send()


class Chain(Outlet):
    def leave(self, rise, send):
        return pltpu.make_async_remote_copy(
            src_ref=self.own,
            dst_ref=self.spot(lax.rem(self.at_z, 2), self.at_core, self.at_y),
            send_sem=self.sends.at[send],
            recv_sem=self.receives.at[lax.rem(self.at_z, 2) * 2 + self.at_core],
            device_id={"core": lax.div(self.at_z, 2), "z": self.at_z + rise},
            device_id_type=MESH_ID,
        )

    def leaving(self, act):
        apart = jnp.logical_not(self.at_core == lax.div(self.at_z, 2))
        for rise, send, inside in ((1, 1, self.at_z < 3), (-1, 2, self.at_z > 0), (0, 0, apart)):

            @pl.when(inside)
            def _():
                act(self.leave(rise, send))

    def start(self):
        @pl.when(self.at_core == lax.div(self.at_z, 2))
        def _():
            self.stay().start()

        self.leaving(lambda copy: copy.start())

    def hop(self, place, core, rise):
        spot = self.spot(place, core, self.at_y)
        at = place * 2 + core
        return pltpu.make_async_remote_copy(
            src_ref=spot,
            dst_ref=spot,
            send_sem=self.sends.at[4 + at],
            recv_sem=self.receives.at[at],
            device_id={"z": self.at_z + rise},
            device_id_type=MESH_ID,
        )

    def hops(self, place, core, act):
        source = 2 * self.at_core + place
        for rise, inside in (
            (1, jnp.logical_and(source < self.at_z, self.at_z < 3)),
            (-1, jnp.logical_and(source > self.at_z, self.at_z > 0)),
        ):

            @pl.when(inside)
            def _():
                act(self.hop(place, core, rise))

    def forward(self, place, core):
        own = jnp.logical_and(2 * self.at_core + place == self.at_z, self.at_core == core)

        @pl.when(own)
        def _():
            self.stay().wait()

        @pl.when(jnp.logical_not(own))
        def _():
            self.hop(place, core, 0).wait_recv()

        self.hops(place, core, lambda copy: copy.start())
        self.across(place, core).start()

    def finish(self):
        self.leaving(lambda copy: copy.wait_send())
        for place in range(2):
            for core in range(2):
                self.hops(place, core, lambda copy: copy.wait_send())
                self.across(place, core).wait()


def back_part_of(
    wires, w_head, w_up, w_down, emb, proj, ctx, w_out, hid, pre, act, normed_one, inverse_one, summed, vecs, upstream,
    ids_col, ids_row,
    block_out, input_out, res_head, res_up, res_down, res_tile, feature, norm,
    two, slope, one, grad_ctx, grad_proj, two_full, one_full, send_c, recv_c, send_y, recv_y, keep, acc,
    near_head, far_head, got_head, came_head, near_up, far_up, got_up, came_up, near_down, far_down, got_down, came_down,
    out_one, out_two, feat, slots, scalar, scalar_slots, key_sum, value_sum, y_feat, x_feat, y_scalar, x_scalar,
    out_sem, local_sem,
):
    at_x, at_core, at_z, at_y = spots()
    low, f32 = jnp.bfloat16, jnp.float32
    length, width = emb.shape
    quarter, half = length // 4, width // 2
    zs = w_head.shape[0]
    block = half // 2
    head_size = ctx.shape[2]
    in_size = 3 * head_size
    feat[...] = jnp.zeros_like(feat)

    def lanes(h):
        return pl.ds(pl.multiple_of(flipped(at_x, h) * half, half), half)

    def second_norm(rows):
        normed, inverse = norm_stats(summed[rows, :])
        gain, shift = vecs[1:2, :], vecs[5:6, :]
        value = (normed * gain + shift).astype(low)
        for h in range(2):
            out_one[rows, lanes(h)] = value[:, h * half : (h + 1) * half]
        above = upstream[rows, :].astype(f32)
        grad = norm_back(above * gain, normed, inverse)
        feat[1:2, :] += jnp.sum(above * normed, axis=0, keepdims=True)
        feat[5:6, :] += jnp.sum(above, axis=0, keepdims=True)
        feat[4:5, :] += jnp.sum(grad, axis=0, keepdims=True)
        two_full[rows, :] = grad
        two[rows, :] = grad.astype(low)

    row_loop(quarter, 32, second_norm)
    to_y, to_core, again = spread_rows(wires, two, quarter)
    outlets = [
        kind(own, result, *[out_sem.at[n, k] for k in range(4)], local_sem.at[n])
        for n, (kind, own, result) in enumerate(((Outlet, out_one, block_out), (Chain, out_two, input_out)))
    ]
    outlets[0].start()

    def slopes(r):
        rows = pl.ds(r * quarter, quarter)

        def inner(s):
            units = pl.ds(pl.multiple_of(s * block, block), block)
            value = dot_f32(two[rows, 0:half], w_down[s, 0]) + dot_f32(two[rows, half:], w_down[s, 1])
            slope[rows, units] = (value * gelu_slope(pre[rows, units])).astype(low)

        block_loop(zs, inner)

    slopes(0)
    to_core.wait_recv()
    slopes(2)
    apart = (at_core - lax.div(at_z, 2)) * (at_core - lax.div(at_z, 2))
    close = (1 - apart) * lax.rem(at_z, 2) + apart * (1 - at_core)
    to_y.wait_recv()
    again.start()
    outlets[0].forward(close, 0)
    slopes(1)
    again.wait_recv()
    slopes(3)
    ended = [to_y, to_core, again]

    def group(near, far, got, came):
        crossed = [wires.make(far.at[s], got.at[s], x=1 - at_x) for s in range(zs)]
        turned = [
            wires.make(far.at[s], came.at[s - 1], z=lax.rem(at_z + zs - s, zs)) for s in range(1, zs)
        ]
        return near, far, got, crossed, turned, came

    groups = {
        "head": group(near_head, far_head, got_head, came_head),
        "up": group(near_up, far_up, got_up, came_up),
        "down": group(near_down, far_down, got_down, came_down),
    }

    def weight_grads(name, left, right):
        near, far, got, crossed, turned, came = groups[name]

        for s in range(zs):
            far[s] = dot_f32(left[:, half:], right[:, s * block : (s + 1) * block], COL_PAIR).astype(low)
            crossed[s].start()

        def inner(s):
            units = pl.ds(pl.multiple_of(s * block, block), block)
            near[s] = dot_f32(left[:, 0:half], right[:, units], COL_PAIR)

        block_loop(zs, inner)

    def turn_blocks(name):
        near, far, got, crossed, turned, came = groups[name]
        size = near.shape[1]
        for s in range(zs):
            crossed[s].wait()

        def inner(s):
            def add(rows):
                near[s, rows, :] += got[s, rows, :].astype(f32)
                far[s, rows, :] = near[s, rows, :].astype(low)

            row_loop(size, 16, add)

        block_loop(zs, inner)

    def start_turns(name):
        for member in groups[name][4]:
            member.start()

    def settle(name):
        near, far, got, crossed, turned, came = groups[name]
        size = near.shape[1]
        for member in turned:
            member.wait()

        def add(rows):
            total = near[0, rows, :]
            for s in range(1, zs):
                total = total + came[s - 1, rows, :].astype(f32)
            near[0, rows, :] = total

        row_loop(size, 16, add)

    bufs = (send_c, recv_c, send_y, recv_y)

    def back_part(r, side):
        rows = pl.ds(r * quarter, quarter)
        total = dot_f32(slope[rows, 0:block], w_up[0, side], ROW_PAIR)
        for s in range(1, zs):
            total = total + dot_f32(slope[rows, s * block : (s + 1) * block], w_up[s, side], ROW_PAIR)
        return total

    add_rows(wires, back_part, keep, acc, bufs, lambda: weight_grads("down", two, act))

    def first_norm(rows):
        grad_hidden = keep[rows, :] + two_full[rows, :]
        normed = normed_one[rows, :]
        grad = norm_back(grad_hidden * vecs[0:1, :], normed, inverse_one[rows, :])
        feat[0:1, :] += jnp.sum(grad_hidden * normed, axis=0, keepdims=True)
        feat[3:4, :] += jnp.sum(grad_hidden, axis=0, keepdims=True)
        feat[2:3, :] += jnp.sum(grad, axis=0, keepdims=True)
        one_full[rows, :] = grad
        one[rows, :] = grad.astype(low)

    row_loop(quarter, 32, first_norm)
    to_y, to_core, again = spread_rows(wires, one, quarter)
    ended += [to_y, to_core, again]
    feat_sent = plane_sum(wires, feat, slots)
    weight_grads("up", hid, slope)

    def contexts(r):
        rows = pl.ds(r * quarter, quarter)
        value = dot_f32(one[rows, 0:half], w_out[0]) + dot_f32(one[rows, half:], w_out[1])
        value = value.astype(low)
        for s in range(zs):
            grad_ctx[s, rows, :] = value[:, s * head_size : (s + 1) * head_size]

    contexts(0)
    to_core.wait_recv()
    contexts(2)
    to_y.wait_recv()
    again.start()
    contexts(1)
    turn_blocks("down")
    start_turns("down")
    again.wait_recv()
    contexts(3)
    outlets[0].forward(close, 1)
    outlets[0].forward(1 - close, 0)
    outlets[0].forward(1 - close, 1)
    scale = head_size**-0.5

    def attend(s):
        keys = proj[s, :, head_size : 2 * head_size]
        values = proj[s, :, 2 * head_size : in_size]
        key_sum[...] = jnp.zeros_like(key_sum)
        value_sum[...] = jnp.zeros_like(value_sum)

        def inner(rows):
            queries = proj[s, rows, 0:head_size] * low(scale)
            grads = grad_ctx[s, rows, :]
            scores = dot_f32(keys, queries, ROW_PAIR)
            scores = jnp.where(ids_col[...] == ids_row[0:1, rows], scores, -1e30)
            highest = jnp.max(scores, axis=0, keepdims=True)
            exponent = jnp.exp(scores - highest)
            probability = exponent * (1.0 / jnp.sum(exponent, axis=0, keepdims=True))
            grad_prob = dot_f32(values, grads, ROW_PAIR)
            weighted = jnp.sum(probability * grad_prob, axis=0, keepdims=True)
            grad_score = (probability * (grad_prob - weighted)).astype(low)
            value_sum[...] += dot_f32(probability.astype(low), grads)
            key_sum[...] += dot_f32(grad_score, queries)
            grad_query = dot_f32(grad_score, keys, COL_PAIR)
            grad_proj[s, rows, 0:head_size] = (grad_query * scale).astype(low)

        row_loop(length, quarter, inner)
        grad_proj[s, :, head_size : 2 * head_size] = key_sum[...].astype(low)
        grad_proj[s, :, 2 * head_size : in_size] = value_sum[...].astype(low)

    block_loop(2, attend)
    turn_blocks("up")
    start_turns("up")
    block_loop(2, lambda s: attend(s + 2))

    size = block + TILE

    def input_part(r, side):
        rows = pl.ds(r * quarter, quarter)
        parts = []
        for core in range(2):
            total = None
            for s in range(zs):
                value = dot_f32(
                    grad_proj[s, rows, :], w_head[s, side, core * size : core * size + block, 0:in_size], ROW_PAIR
                )
                total = value if total is None else total + value
            parts.append(total)
        return jnp.concatenate(parts, axis=1)

    near, far, got, crossed, turned, came = groups["head"]

    def head_far():
        for s in range(zs):
            far[s, 0:half, 0:in_size] = dot_f32(emb[:, half:], grad_proj[s], COL_PAIR).astype(low)
            far[s, 0:half, in_size:] = dot_f32(one[:, half:], ctx[s], COL_PAIR).astype(low)
            sums = jnp.sum(grad_proj[s].astype(f32), axis=0, keepdims=True)
            near[s, half:, :] = jnp.zeros((TILE, near.shape[2]), f32)
            near[s, half : half + 1, 0:head_size] = sums[:, 0:head_size]
            near[s, half : half + 1, 2 * head_size : in_size] = sums[:, 2 * head_size :]
            near[s, half + 1 : half + 2, :] = jnp.sum(
                slope[:, s * block : (s + 1) * block].astype(f32), axis=0, keepdims=True
            )
            far[s, half:, :] = near[s, half:, :].astype(low)
            crossed[s].start()

    add_rows(wires, input_part, keep, acc, bufs, head_far)

    def leave(rows):
        value = (keep[rows, :] + one_full[rows, :]).astype(low)
        for h in range(2):
            out_two[rows, lanes(h)] = value[:, h * half : (h + 1) * half]

    row_loop(quarter, 32, leave)
    outlets[1].start()

    def head_near(s):
        near[s, 0:half, 0:in_size] = dot_f32(emb[:, 0:half], grad_proj[s], COL_PAIR)
        near[s, 0:half, in_size:] = dot_f32(one[:, 0:half], ctx[s], COL_PAIR)

    block_loop(zs, head_near)
    turn_blocks("head")
    edge = at_core * lax.div(at_z, 3) + (1 - at_core) * (1 - lax.div(3 - at_z, 3))
    outlets[1].forward(edge, 0)
    outlets[1].forward(edge, 1)
    start_turns("head")

    acc[0:8, :] = plane_total(feat_sent, slots)
    y_copy = wires.make(acc.at[pl.ds(0, 8)], y_feat, y=1 - at_y)
    y_copy.start()
    y_copy.wait_recv()
    feat_all = acc[0:8, :] + y_feat[...]
    keep[0:8, :] = feat_all
    x_copy = wires.make(keep.at[pl.ds(0, 8), pl.ds(half, half)], x_feat, x=1 - at_x)
    x_copy.start()
    x_copy.wait_recv()
    feature[...] = feat_all[:, 0:half] + x_feat[...]

    settle("down")
    settle("up")
    outlets[1].forward(1 - edge, 0)
    outlets[1].forward(1 - edge, 1)
    settle("head")

    backs = []
    results = (("head", res_head), ("up", res_up), ("down", res_down))
    for at, (name, result) in enumerate(results):
        near = groups[name][0]
        mine = near.at[0, pl.ds(pl.multiple_of(at_core * block, block), block)]
        other = near.at[0, pl.ds(pl.multiple_of((1 - at_core) * block, block), block)]
        place = result.at[at_core]
        if name != "head":
            place = result.at[:, pl.ds(pl.multiple_of(at_core * block, block), block)]
        local = pltpu.make_async_copy(mine, place, local_sem.at[2 + at])
        local.start()
        remote = wires.make(other, place, core=1 - at_core)
        remote.start()
        backs += [local, remote]
    tile = near_head.at[0, pl.ds(half, TILE)]
    local = pltpu.make_async_copy(tile, res_tile.at[at_core], local_sem.at[5])
    remote = wires.make(tile, res_tile.at[at_core], core=1 - at_core)
    local.start()
    remote.start()
    backs += [local, remote]

    acc[8:16, 0:block] = jnp.zeros((8, block), f32)
    for name, _ in results:
        near = groups[name][0]

        def add(rows):
            value = near[0, rows, :]
            acc[8:16, 0:block] += value * value

        row_loop(half, 8, add)
    value = near_head[0, half : half + 8, :]
    acc[8:16, 0:block] += 0.5 * value * value
    shared = feature[...] * feature[...] * (1.0 / 16.0)
    shared = shared[:, 0:block] + shared[:, block:]
    summed_squares = jnp.sum(acc[8:16, 0:block] + shared)
    scalar[...] = jnp.broadcast_to(summed_squares, scalar.shape)
    scalar_sent = plane_sum(wires, scalar, scalar_slots)
    value = plane_total(scalar_sent, scalar_slots)
    norm[...] = value
    y_two = wires.make(norm, y_scalar, y=1 - at_y)
    y_two.start()
    y_two.wait()
    value = value + y_scalar[...]
    send_scalar = scalar_slots.at[8]
    send_scalar[...] = value
    x_two = wires.make(send_scalar, x_scalar, x=1 - at_x)
    x_two.start()
    x_two.wait()
    norm[...] = value + x_scalar[...]

    for member in ended + feat_sent + scalar_sent + [y_copy, x_copy]:
        member.wait_send()
    for member in backs:
        member.wait()
    for outlet in outlets:
        outlet.finish()


def layer_kernel(
    in_full, out_full, up_full, down_full, tiles, tokens, cotangent, times, ids,
    block_out, input_out, res_head, res_up, res_down, res_tile, feature, norm,
    head_piece, up_piece, down_piece, time_row, ids_col, ids_row,
    w_head, w_up, w_down, emb, proj, ctx, w_out, hid, pre, act, normed_one, inverse_one, hidden, vecs, upstream, tok,
    *rest,
):
    mids, gather_sems = rest[:-9], rest[-4:]
    send_sem, recv_sem, out_sem, local_sem, front_sem = rest[-9:-4]
    shared = mids[7:13]
    wires = Wires(send_sem, recv_sem)
    greet(True)
    finish = front_part(
        wires, in_full, out_full, up_full, down_full, tiles, tokens, cotangent, times, ids,
        head_piece, up_piece, down_piece, time_row, ids_col, ids_row,
        w_head, w_up, w_down, emb, proj, ctx, w_out, hid, pre, act, normed_one, inverse_one, hidden, vecs, upstream,
        tok, *shared, front_sem, gather_sems,
    )
    quarter = hidden.shape[0]
    out_one, out_two = tok.at[pl.ds(2 * quarter, quarter)], tok.at[pl.ds(3 * quarter, quarter)]
    back_part_of(
        wires, w_head, w_up, w_down, emb, proj, ctx, w_out, hid, pre, act, normed_one, inverse_one, hidden, vecs,
        upstream, ids_col, ids_row,
        block_out, input_out, res_head, res_up, res_down, res_tile, feature, norm,
        *mids[:25], out_one, out_two, *mids[25:], out_sem, local_sem,
    )
    finish()


def run_layer(weights, tiles, tokens, cotangent, times, ids, head_size):
    low, f32 = jnp.bfloat16, jnp.float32
    length, width = ids.shape[2], tokens.shape[1]
    zs = 4
    quarter, half, block = length // 4, width // 2, width // 4
    units = weights[2].shape[1] // 2
    vmem = pl.BlockSpec(memory_space=pltpu.VMEM)
    anywhere = pl.BlockSpec(memory_space=pl.ANY)
    shape = jax.ShapeDtypeStruct
    kept = [
        ((2, block + TILE, 4 * head_size), low),
        ((2, block, units), low),
        ((2, block, units), low),
        ((1, width), f32),
        ((length, 1), f32),
        ((1, length), f32),
        ((zs, 2, half + 2 * TILE, 4 * head_size), low),
        ((zs, 2, half, units), low),
        ((zs, 2, half, units), low),
        ((length, width), low),
        ((zs, length, 3 * head_size), low),
        ((zs, length, head_size), low),
        ((2, half, zs * head_size), low),
        ((length, width), low),
        ((length, zs * units), f32),
        ((length, zs * units), low),
        ((quarter, width), f32),
        ((quarter, 1), f32),
        ((quarter, width), f32),
        ((8, width), f32),
        ((quarter, width), low),
        ((length, width), low),
    ]

    def group(size):
        return [((n, size, block), d) for n, d in ((zs, f32), (zs, low), (zs, low), (zs - 1, low))]

    worked = [
        ((length, width), low),
        ((length, width), low),
        ((length, width), low),
        ((zs, length, head_size), low),
        ((zs, length, 3 * head_size), low),
        ((quarter, width), f32),
        ((quarter, width), f32),
        ((2, quarter, width), low),
        ((2, quarter, width), low),
        ((quarter, width), low),
        ((quarter, width), low),
        ((quarter, width), f32),
        ((quarter, width), f32),
        *group(half + TILE),
        *group(half),
        *group(half),
        ((8, width), f32),
        ((8, 8, width), f32),
        ((8, 128), f32),
        ((9, 8, 128), f32),
        ((length, head_size), f32),
        ((length, head_size), f32),
        ((8, width), f32),
        ((8, half), f32),
        ((8, 128), f32),
        ((8, 128), f32),
    ]
    return pl.pallas_call(
        layer_kernel,
        out_shape=[
            shape(tokens.shape, low),
            shape(tokens.shape, low),
            shape((2, block, block), f32),
            shape((block, 2 * block), f32),
            shape((block, 2 * block), f32),
            shape((2, TILE, block), f32),
            shape((8, half), f32),
            shape((8, 128), f32),
        ],
        in_specs=[vmem] * 5 + [anywhere] * 4,
        out_specs=[anywhere] * 2 + [vmem] * 6,
        scratch_shapes=[pltpu.VMEM(*member) for member in kept + worked]
        + [
            pltpu.SemaphoreType.DMA((128,)),
            pltpu.SemaphoreType.DMA((128,)),
            pltpu.SemaphoreType.DMA((2, 4, 8)),
            pltpu.SemaphoreType.DMA((6,)),
            pltpu.SemaphoreType.DMA((20,)),
            pltpu.SemaphoreType.DMA((3, 6)),
            pltpu.SemaphoreType.DMA((3, 4)),
            pltpu.SemaphoreType.DMA((3, 4)),
            pltpu.SemaphoreType.DMA((3, 4)),
        ],
        compiler_params=pltpu.CompilerParams(
            collective_id=0, has_side_effects=True, vmem_limit_bytes=67000000
        ),
        name="layer",
    )(*weights, tiles, tokens, cotangent, times, ids)


def on_grid(*arguments):
    tokens, time_embed, segment_ids, cotangent = arguments[:4]
    masters, moments, squares = arguments[4::3], arguments[5::3], arguments[6::3]
    input_weight, output_weight, upward_weight, downward_weight = masters[:4]
    head_bias, hidden_bias, norm_gains, branch_biases = masters[4:]
    at_x, at_core = lax.axis_index("x"), lax.axis_index("core")
    at_z, at_y = lax.axis_index("z"), lax.axis_index("y")
    first_core, first_x = at_core == 0, at_x == 0
    swapped = at_x == 1
    low = jnp.bfloat16
    f32 = jnp.float32
    length = segment_ids.shape[1]
    head_size = head_bias.shape[0] * 4 // 2
    zs = 4
    place = at_core * 2 + at_y
    quarter = length // 4

    rows = input_weight.shape[0]
    wide = upward_weight.shape[1] // 2
    packed = 4 * head_size
    small_rows = head_bias.shape[0]

    position = at_x * 2 + at_core
    vectors = jnp.concatenate([norm_gains, branch_biases], axis=1).T
    vectors = lax.dynamic_update_slice(
        jnp.zeros((TILE, rows), f32), vectors, (2 + 6 * at_core, 0)
    )

    def small_tile(half):
        tile = lax.dynamic_update_slice(
            vectors, head_bias[:, half][None], (0, at_x * 2 * head_size + at_core * small_rows)
        )
        units = lax.dynamic_update_slice(
            jnp.zeros((2, 4 * small_rows), f32),
            hidden_bias[:, 2 * half : 2 * half + 2].T,
            (0, position * small_rows),
        )
        return lax.dynamic_update_slice(tile, units.reshape(1, -1), (1, 0))

    seqs = segment_ids.shape[0]
    times = time_embed.astype(f32).reshape(seqs, 1, -1)
    ids = segment_ids.astype(f32).reshape(seqs, 1, length)
    small = jnp.stack([small_tile(0), small_tile(1)])
    block_output, input_grad, res_head, sent_up, sent_down, tiles, feature, norm = run_layer(
        masters[:4], small, tokens, cotangent, times, ids, head_size
    )
    in_size = 3 * head_size
    sent_in = jnp.concatenate([res_head[0, :, :in_size], res_head[1, :, :in_size]], axis=1)
    sent_out = jnp.concatenate([res_head[0, :, in_size:], res_head[1, :, in_size:]], axis=1)
    sent_head = lax.dynamic_slice(
        tiles[:, 0], (0, at_x * 2 * head_size + at_core * small_rows), (2, small_rows)
    ).T
    units = lax.dynamic_slice(
        tiles[:, 1].reshape(4, 4 * small_rows), (0, position * small_rows), (4, small_rows)
    )
    sent_unit = units.T
    feature = lax.dynamic_slice(feature, (0, at_core * rows), (8, rows))
    sent_gains, sent_shifts = feature[0:2].T, feature[2:6].T
    grad_norm = jnp.sqrt(norm[0, 0])
    gradients = (sent_in, sent_out, sent_up, sent_down, sent_head, sent_unit, sent_gains, sent_shifts)
    factor = CLIP / jnp.maximum(grad_norm, CLIP)
    results = [block_output, input_grad.astype(f32), grad_norm.reshape(1)]
    for position in range(8):
        results += adam_update(
            masters[position],
            moments[position],
            squares[position],
            gradients[position] * factor,
            RATES[position],
            DECAYS[position],
        )
    return tuple(results)


def solution(mesh):
    plain = mesh.shape["rows"] != 4 or mesh.shape["tp"] != 8
    if plain:
        rows, tp = "rows", "tp"
        grid, work = mesh, on_device
    else:
        rows, tp = ("x", "core"), ("z", "y")
        grid = Mesh(mesh.devices.reshape(2, 2, 4, 2), ("x", "core", "z", "y"))
        work = on_grid
    narrow, split = P(rows, None), P(rows, tp)
    return jax.shard_map(
        work,
        mesh=grid,
        in_specs=(narrow,) * 4 + (split,) * 18 + (narrow,) * 6,
        out_specs=(narrow, narrow, P()) + (split,) * 18 + (narrow,) * 6,
        check_vma=False,
    )
```

```python
from functools import partial, reduce

import jax
import jax.numpy as jnp
from jax import lax
from jax.experimental import pallas as pl
from jax.experimental.pallas import tpu as pltpu
from jax.sharding import Mesh
from jax.sharding import PartitionSpec as P

HD = 64
STEP = 10


NORM_EPS = 1e-05
BETA_ONE = 0.9
BETA_TWO = 0.999
ADAM_EPS = 1e-08
CLIP = 1.0
RATES = (0.1, 0.4, 0.1, 0.05, 0.5, 0.5, 0.5, 0.5)
DECAYS = (0.01, 0.01, 0.01, 0.01, 0.0, 0.0, 0.0, 0.0)
ROW_PAIR = (((1,), (1,)), ((), ()))
COL_PAIR = (((0,), (0,)), ((), ()))


def norm_stats(summed):
    average = jnp.mean(summed, axis=-1, keepdims=True)
    centered = summed - average
    inverse = lax.rsqrt(jnp.mean(centered * centered, axis=-1, keepdims=True) + NORM_EPS)
    return (centered * inverse, inverse)


def norm_back(grad_normed, normed, inverse):
    first_mean = jnp.mean(grad_normed, axis=-1, keepdims=True)
    second_mean = jnp.mean(grad_normed * normed, axis=-1, keepdims=True)
    return inverse * (grad_normed - first_mean - normed * second_mean)


def gelu_value(inputs):
    return 0.5 * inputs * (1.0 + jax.scipy.special.erf(inputs * 0.7071067811865476))


def gelu_slope(inputs):
    cumulative = 0.5 * (1.0 + jax.scipy.special.erf(inputs * 0.7071067811865476))
    return cumulative + inputs * jnp.exp(-0.5 * inputs * inputs) * 0.3989422804014327


def masked_scores(queries, key_rows, segments):
    scores = jnp.einsum(
        "qhd,khd->hqk", queries, key_rows, preferred_element_type=jnp.float32
    ) * HD ** (-0.5)
    matching = segments[:, None] == segments[None, :]
    return jnp.where(matching[None], scores, -1e30)


def attend_forward(pieces):
    queries, key_rows, values, segments = pieces
    scores = masked_scores(queries, key_rows, segments)
    highest = jnp.max(scores, axis=-1, keepdims=True)
    exponent = jnp.exp(scores - highest)
    totals = jnp.sum(exponent, axis=-1, keepdims=True)
    probability = (exponent / totals).astype(jnp.bfloat16)
    context = jnp.einsum("hqk,khd->qhd", probability, values, preferred_element_type=jnp.float32)
    return (context, (highest + jnp.log(totals))[..., 0])


def attend_back(pieces):
    queries, key_rows, values, segments, log_total, grad_context = pieces
    scores = masked_scores(queries, key_rows, segments)
    probability = jnp.exp(scores - log_total[..., None])
    grad_prob = jnp.einsum("qhd,khd->hqk", grad_context, values, preferred_element_type=jnp.float32)
    weighted = jnp.sum(probability * grad_prob, axis=-1, keepdims=True)
    grad_score = (probability * (grad_prob - weighted)).astype(jnp.bfloat16)
    grad_query = jnp.einsum(
        "hqk,khd->qhd", grad_score, key_rows, preferred_element_type=jnp.float32
    ) * HD ** (-0.5)
    grad_key = jnp.einsum(
        "hqk,qhd->khd", grad_score, queries, preferred_element_type=jnp.float32
    ) * HD ** (-0.5)
    grad_value = jnp.einsum(
        "hqk,qhd->khd",
        probability.astype(jnp.bfloat16),
        grad_context,
        preferred_element_type=jnp.float32,
    )
    return jnp.stack([grad_query, grad_key, grad_value], axis=2)


def adam_update(weight, moment, square, clipped, rate, decay):
    moment = BETA_ONE * moment + (1.0 - BETA_ONE) * clipped
    square = BETA_TWO * square + (1.0 - BETA_TWO) * clipped * clipped
    corrected = (
        moment / (1.0 - BETA_ONE**STEP) / (jnp.sqrt(square / (1.0 - BETA_TWO**STEP)) + ADAM_EPS)
    )
    return (weight - rate * (corrected + decay * weight), moment, square)


def add_squares(running, member):
    return running + jnp.sum(member * member)


def on_device(
    tokens,
    time_embed,
    segment_ids,
    cotangent,
    input_weight,
    input_moment,
    input_square,
    output_weight,
    output_moment,
    output_square,
    upward_weight,
    upward_moment,
    upward_square,
    downward_weight,
    downward_moment,
    downward_square,
    head_bias,
    head_moment,
    head_square,
    hidden_bias,
    hidden_moment,
    hidden_square,
    norm_gains,
    gains_moment,
    gains_square,
    branch_biases,
    biases_moment,
    biases_square,
):
    masters = (
        input_weight,
        output_weight,
        upward_weight,
        downward_weight,
        head_bias,
        hidden_bias,
        norm_gains,
        branch_biases,
    )
    moments = (
        input_moment,
        output_moment,
        upward_moment,
        downward_moment,
        head_moment,
        hidden_moment,
        gains_moment,
        biases_moment,
    )
    squares = (
        input_square,
        output_square,
        upward_square,
        downward_square,
        head_square,
        hidden_square,
        gains_square,
        biases_square,
    )
    (
        weights_in,
        weights_out,
        weights_up,
        weights_down,
        head_shift,
        unit_shift,
        gains_low,
        shifts_low,
    ) = (
        lax.all_gather(input_weight.astype(jnp.bfloat16), "rows", axis=0, tiled=True),
        lax.all_gather(output_weight.astype(jnp.bfloat16), "rows", axis=0, tiled=True),
        lax.all_gather(upward_weight.astype(jnp.bfloat16), "rows", axis=0, tiled=True),
        lax.all_gather(downward_weight.astype(jnp.bfloat16), "rows", axis=0, tiled=True),
        lax.all_gather(head_bias.astype(jnp.bfloat16), "rows", axis=0, tiled=True),
        lax.all_gather(hidden_bias.astype(jnp.bfloat16), "rows", axis=0, tiled=True),
        lax.all_gather(norm_gains.astype(jnp.bfloat16), "rows", axis=0, tiled=True),
        lax.all_gather(branch_biases.astype(jnp.bfloat16), "rows", axis=0, tiled=True),
    )
    seq_count, length = segment_ids.shape
    width = tokens.shape[1]
    num_heads = head_shift.shape[1]
    head_size = head_shift.shape[0] // 2
    tok_rows = seq_count * length
    gains = gains_low.astype(jnp.float32)
    shifts = shifts_low.astype(jnp.float32)
    embedded = (
        tokens.astype(jnp.float32).reshape(seq_count, length, width)
        + time_embed.astype(jnp.float32)[:, None, :]
    ).reshape(tok_rows, width)
    embedded_low = embedded.astype(jnp.bfloat16)
    head_float = head_shift.astype(jnp.float32)
    offset = jnp.stack(
        [
            head_float[:head_size].T,
            jnp.zeros((num_heads, head_size), jnp.float32),
            head_float[head_size:].T,
        ],
        axis=1,
    )
    projected = jnp.dot(embedded_low, weights_in, preferred_element_type=jnp.float32).reshape(
        tok_rows, num_heads, 3, head_size
    )
    projected = (
        (projected + offset)
        .astype(jnp.bfloat16)
        .reshape(seq_count, length, num_heads, 3, head_size)
    )
    queries = projected[:, :, :, 0]
    key_rows = projected[:, :, :, 1]
    values = projected[:, :, :, 2]
    context, log_total = lax.map(attend_forward, (queries, key_rows, values, segment_ids))
    context_low = context.reshape(tok_rows, num_heads * head_size).astype(jnp.bfloat16)
    mixed_part = lax.dot_general(
        context_low, weights_out, ROW_PAIR, preferred_element_type=jnp.float32
    )
    mixed = lax.psum(mixed_part, "tp")
    normed_one, inverse_one = norm_stats(embedded + mixed + shifts[:, 0])
    hidden = normed_one * gains[:, 0] + shifts[:, 1]
    hidden_low = hidden.astype(jnp.bfloat16)
    unit_offset = unit_shift.astype(jnp.float32).T.reshape(-1)
    pre_act = jnp.dot(hidden_low, weights_up, preferred_element_type=jnp.float32) + unit_offset
    expanded_low = gelu_value(pre_act).astype(jnp.bfloat16)
    reduced_part = lax.dot_general(
        expanded_low, weights_down, ROW_PAIR, preferred_element_type=jnp.float32
    )
    reduced = lax.psum(reduced_part, "tp")
    normed_two, inverse_two = norm_stats(hidden + reduced + shifts[:, 2])
    block_output = (normed_two * gains[:, 1] + shifts[:, 3]).astype(jnp.bfloat16)
    upstream = cotangent.astype(jnp.float32)
    gain_two = jnp.sum(upstream * normed_two, axis=0)
    shift_three = jnp.sum(upstream, axis=0)
    grad_pre_two = norm_back(upstream * gains[:, 1], normed_two, inverse_two)
    shift_two = jnp.sum(grad_pre_two, axis=0)
    grad_pre_two_low = grad_pre_two.astype(jnp.bfloat16)
    grad_down = lax.dot_general(
        grad_pre_two_low, expanded_low, COL_PAIR, preferred_element_type=jnp.float32
    )
    grad_act = jnp.dot(grad_pre_two_low, weights_down, preferred_element_type=jnp.float32)
    grad_pre_act = (grad_act * gelu_slope(pre_act)).astype(jnp.bfloat16)
    unit_sums = jnp.sum(grad_pre_act, axis=0, dtype=jnp.float32)
    grad_unit = unit_sums.reshape(-1, 2 * head_size).T
    grad_up = lax.dot_general(
        hidden_low, grad_pre_act, COL_PAIR, preferred_element_type=jnp.float32
    )
    back_part = lax.dot_general(
        grad_pre_act, weights_up, ROW_PAIR, preferred_element_type=jnp.float32
    )
    grad_hidden = lax.psum(back_part, "tp") + grad_pre_two
    gain_one = jnp.sum(grad_hidden * normed_one, axis=0)
    shift_one = jnp.sum(grad_hidden, axis=0)
    grad_pre_one = norm_back(grad_hidden * gains[:, 0], normed_one, inverse_one)
    shift_zero = jnp.sum(grad_pre_one, axis=0)
    grad_pre_one_low = grad_pre_one.astype(jnp.bfloat16)
    grad_out = lax.dot_general(
        grad_pre_one_low, context_low, COL_PAIR, preferred_element_type=jnp.float32
    )
    grad_context = jnp.dot(
        grad_pre_one_low, weights_out, preferred_element_type=jnp.float32
    ).astype(jnp.bfloat16)
    grad_context = grad_context.reshape(seq_count, length, num_heads, head_size)
    grad_projected = lax.map(
        attend_back, (queries, key_rows, values, segment_ids, log_total, grad_context)
    )
    grad_projected = grad_projected.reshape(tok_rows, num_heads * 3 * head_size).astype(
        jnp.bfloat16
    )
    head_sums = jnp.sum(grad_projected, axis=0, dtype=jnp.float32).reshape(num_heads, 3, head_size)
    grad_head = jnp.concatenate([head_sums[:, 0].T, head_sums[:, 2].T], axis=0)
    grad_in = lax.dot_general(
        embedded_low, grad_projected, COL_PAIR, preferred_element_type=jnp.float32
    )
    input_part = lax.dot_general(
        grad_projected, weights_in, ROW_PAIR, preferred_element_type=jnp.float32
    )
    input_grad = lax.psum(input_part, "tp") + grad_pre_one
    grad_gains = jnp.stack([gain_one, gain_two], axis=1)
    grad_shifts = jnp.stack([shift_zero, shift_one, shift_two, shift_three], axis=1)
    sent_in, sent_out, sent_up, sent_down, sent_head, sent_unit, sent_gains, sent_shifts = (
        lax.psum_scatter(grad_in, "rows", scatter_dimension=0, tiled=True),
        lax.psum_scatter(grad_out, "rows", scatter_dimension=0, tiled=True),
        lax.psum_scatter(grad_up, "rows", scatter_dimension=0, tiled=True),
        lax.psum_scatter(grad_down, "rows", scatter_dimension=0, tiled=True),
        lax.psum_scatter(grad_head, "rows", scatter_dimension=0, tiled=True),
        lax.psum_scatter(grad_unit, "rows", scatter_dimension=0, tiled=True),
        lax.psum_scatter(grad_gains, "rows", scatter_dimension=0, tiled=True),
        lax.psum_scatter(grad_shifts, "rows", scatter_dimension=0, tiled=True),
    )
    gradients = (
        sent_in,
        sent_out,
        sent_up,
        sent_down,
        sent_head,
        sent_unit,
        sent_gains,
        sent_shifts,
    )
    split_part = reduce(
        add_squares,
        (sent_in, sent_out, sent_up, sent_down, sent_head, sent_unit),
        jnp.zeros((), jnp.float32),
    )
    copied_part = (
        jnp.sum(sent_gains * sent_gains) + jnp.sum(sent_shifts * sent_shifts)
    ) / lax.axis_size("tp")
    grad_norm = jnp.sqrt(lax.psum(split_part + copied_part, ("rows", "tp")))
    factor = CLIP / jnp.maximum(grad_norm, CLIP)
    updated = [
        adam_update(
            masters[position],
            moments[position],
            squares[position],
            gradients[position] * factor,
            RATES[position],
            DECAYS[position],
        )
        for position in range(8)
    ]
    return (
        block_output,
        input_grad,
        grad_norm.reshape(1),
        updated[0][0],
        updated[0][1],
        updated[0][2],
        updated[1][0],
        updated[1][1],
        updated[1][2],
        updated[2][0],
        updated[2][1],
        updated[2][2],
        updated[3][0],
        updated[3][1],
        updated[3][2],
        updated[4][0],
        updated[4][1],
        updated[4][2],
        updated[5][0],
        updated[5][1],
        updated[5][2],
        updated[6][0],
        updated[6][1],
        updated[6][2],
        updated[7][0],
        updated[7][1],
        updated[7][2],
    )


def flip(value, axis):
    return lax.ppermute(value, axis, [(0, 1), (1, 0)])


def turn(value, amount, count):
    return lax.ppermute(value, "z", [(i, (i + amount) % count) for i in range(count)])


def swap_halves(value, swapped):
    half = value.shape[-1] // 2
    return jnp.where(
        swapped, jnp.concatenate([value[..., half:], value[..., :half]], axis=-1), value
    )


def in_order(first, mine, other):
    return jnp.where(
        first, jnp.concatenate([mine, other], axis=0), jnp.concatenate([other, mine], axis=0)
    )


MESH_ID = pl.DeviceIdType.MESH
TILE = 16


class Wires:
    def __init__(self, sends, receives):
        self.sends, self.receives, self.used = sends, receives, 0

    def make(self, source, target, **device):
        at = self.used
        self.used += 1
        return pltpu.make_async_remote_copy(
            src_ref=source,
            dst_ref=target,
            send_sem=self.sends.at[at],
            recv_sem=self.receives.at[at],
            device_id=device,
            device_id_type=MESH_ID,
        )


def spots():
    return (lax.axis_index("x"), lax.axis_index("core"), lax.axis_index("z"), lax.axis_index("y"))


def greet(full):
    at_x, at_core, at_z, at_y = spots()
    barrier = pltpu.get_barrier_semaphore()
    count = 0

    def call(**device):
        pl.semaphore_signal(barrier, inc=1, device_id=device, device_id_type=MESH_ID)

    for step in range(4):
        if step:
            call(z=lax.rem(at_z + step, 4))
            count += 1
        if full or step == 0:
            call(core=1 - at_core, z=lax.rem(at_z + step, 4))
            count += 1
    call(x=1 - at_x)
    call(y=1 - at_y)
    pl.semaphore_wait(barrier, count + 2)


def flipped(value, bit):
    return 1 - value if bit else value


def row_loop(count, step, body):
    def inner(at, carry):
        body(pl.ds(pl.multiple_of(at * step, step), step))
        return carry

    lax.fori_loop(0, count // step, inner, 0)


def block_loop(count, body):
    def inner(at, carry):
        body(at)
        return carry

    lax.fori_loop(0, count, inner, 0)


def dot_f32(left, right, pairing=(((1,), (0,)), ((), ()))):
    return lax.dot_general(left, right, pairing, preferred_element_type=jnp.float32)


def spread_rows(wires, ref, quarter):
    _, at_core, _, at_y = spots()
    own, near = ref.at[pl.ds(0, quarter)], ref.at[pl.ds(quarter, quarter)]
    to_y = wires.make(own, near, y=1 - at_y)
    to_core = wires.make(own, ref.at[pl.ds(2 * quarter, quarter)], core=1 - at_core)
    again = wires.make(near, ref.at[pl.ds(3 * quarter, quarter)], core=1 - at_core)
    to_y.start()
    to_core.start()
    return to_y, to_core, again


def add_rows(wires, part, keep, acc, bufs, fill=None):
    _, at_core, _, at_y = spots()
    send_c, recv_c, send_y, recv_y = bufs
    low = jnp.bfloat16
    half = keep.shape[1] // 2
    sides = [pl.ds(0, half), pl.ds(half, half)]
    far = [wires.make(send_c.at[b], recv_c.at[b], core=1 - at_core) for b in range(2)]
    across = wires.make(send_y, recv_y, y=1 - at_y)
    for b, r in ((1, 3), (0, 2)):
        for side in range(2):
            send_c[b, :, sides[side]] = part(r, side).astype(low)
        far[b].start()
    for side in range(2):
        acc[:, sides[side]] = part(1, side)
    far[1].wait_recv()

    def to_send(rows):
        send_y[rows, :] = (acc[rows, :] + recv_c[1, rows, :].astype(jnp.float32)).astype(low)

    row_loop(keep.shape[0], 32, to_send)
    across.start()
    for side in range(2):
        keep[:, sides[side]] = part(0, side)
    far[0].wait_recv()
    if fill is not None:
        fill()
    across.wait_recv()

    def finish(rows):
        keep[rows, :] += recv_c[0, rows, :].astype(jnp.float32) + recv_y[rows, :].astype(jnp.float32)

    row_loop(keep.shape[0], 32, finish)
    far[0].wait_send()
    far[1].wait_send()
    across.wait_send()


class Relay:
    def __init__(self, targets, z_sends, z_receives, x_sends, x_receives):
        self.targets, self.z_sends, self.z_receives = targets, z_sends, z_receives
        self.x_sends, self.x_receives = x_sends, x_receives
        self.at_x, _, self.at_z, _ = spots()
        middle = lax.rem(lax.div(self.at_z + 1, 2), 2)
        first = 3 - 2 * lax.rem(self.at_z, 2)
        second = 2 * (1 - middle) + middle * (4 - first)
        self.order = [0, first, second, 6 - first - second]

    def hop(self, at, slot, rising, send):
        to = lax.rem(slot + (1 if rising else 3), 4)
        target = self.targets[at]
        return pltpu.make_async_remote_copy(
            src_ref=target.at[slot, 0],
            dst_ref=target.at[to, 0],
            send_sem=self.z_sends.at[at, send],
            recv_sem=self.z_receives.at[at, to],
            device_id={"z": self.at_z + (1 if rising else -1)},
            device_id_type=MESH_ID,
        )

    def cross(self, at, slot):
        target = self.targets[at]
        return pltpu.make_async_remote_copy(
            src_ref=target.at[slot, 0],
            dst_ref=target.at[slot, 1],
            send_sem=self.x_sends.at[at, slot],
            recv_sem=self.x_receives.at[at, slot],
            device_id={"x": 1 - self.at_x},
            device_id_type=MESH_ID,
        )

    def hops(self, at, turn, act):
        slot = self.order[turn]
        for rising in (True, False):
            inside = self.at_z < 3 if rising else self.at_z > 0
            if turn:
                below = slot <= self.at_z
                inside = jnp.logical_and(inside, below if rising else jnp.logical_not(below))
            send = turn + 1 if turn else int(rising)

            @pl.when(inside)
            def _():
                act(self.hop(at, jnp.int32(slot) if not turn else slot, rising, send))

    def begin(self, at):
        self.hops(at, 0, lambda copy: copy.start())

    def arrive(self, at, turn):
        slot = self.order[turn]
        target = self.targets[at]
        pltpu.make_async_remote_copy(
            src_ref=target.at[slot, 0],
            dst_ref=target.at[slot, 0],
            send_sem=self.z_sends.at[at, 0],
            recv_sem=self.z_receives.at[at, slot],
            device_id={"x": 1 - self.at_x},
            device_id_type=MESH_ID,
        ).wait_recv()
        self.hops(at, turn, lambda copy: copy.start())
        self.cross(at, slot).start()

    def finish(self):
        for at in range(3):
            for turn in range(4):
                self.hops(at, turn, lambda copy: copy.wait_send())
                self.cross(at, turn).wait_send()


def front_part(
    wires, in_full, out_full, up_full, down_full, tiles, tokens, cotangent, times, ids,
    head_piece, up_piece, down_piece, time_row, ids_col, ids_row,
    w_head, w_up, w_down, emb, proj, ctx, w_out, hid, pre, act, normed_one, inverse_one, hidden, vecs, upstream,
    tok, send_c, recv_c, send_y, recv_y, keep, acc, local_sem, gather_sems,
):
    at_x, at_core, at_z, at_y = spots()
    low, f32 = jnp.bfloat16, jnp.float32
    length, width = emb.shape
    quarter, half = length // 4, width // 2
    zs = w_head.shape[0]
    span = half + 2 * TILE
    head_size = ctx.shape[2]
    in_size = 3 * head_size

    split = in_full.shape[1] // 2
    for h in range(2):
        head_piece[h, 0 : half // 2, 0:split] = in_full[:, h * split : (h + 1) * split].astype(low)
        head_piece[h, 0 : half // 2, split:] = out_full[:, h * head_size : (h + 1) * head_size].astype(low)
        head_piece[h, half // 2 :, :] = tiles[h].astype(low)
    for full, piece in ((up_full, up_piece), (down_full, down_piece)):
        for h in range(2):
            piece[h] = full[:, h * piece.shape[2] : (h + 1) * piece.shape[2]].astype(low)

    kept, lent = [], []
    for at, (piece, target) in enumerate(((head_piece, w_head), (up_piece, w_up), (down_piece, w_down))):
        size = piece.shape[1]
        place = target.at[0, 0, pl.ds(pl.multiple_of(at_core * size, size), size)]
        local = pltpu.make_async_copy(piece.at[at_core], place, local_sem.at[at])
        local.start()
        remote = wires.make(piece.at[1 - at_core], place, core=1 - at_core)
        remote.start()
        kept.append(local)
        lent.append(remote)
    relay = Relay((w_head, w_up, w_down), *gather_sems)

    holds = at_core == lax.div(at_z, 2)
    start = lax.rem(at_z, 2) * length
    here, there = [], []
    for r in range(4):
        for h in range(2):
            spot = tok.at[pl.ds(r * quarter, quarter), pl.ds(pl.multiple_of(flipped(at_x, h) * half, half), half)]

            def source(core):
                at = flipped(core, r // 2) * 2 + flipped(at_y, r % 2)
                return tokens.at[pl.ds(pl.multiple_of(start + at * quarter, quarter), quarter), pl.ds(h * half, half)]

            here.append(pltpu.make_async_copy(source(at_core), spot, local_sem.at[3 + 2 * r + h]))
            there.append(wires.make(source(1 - at_core), spot, core=1 - at_core))
    for h in range(2):
        spot = upstream.at[:, pl.ds(pl.multiple_of(flipped(at_x, h) * half, half), half)]

        def above(core):
            at = start + (core * 2 + at_y) * quarter
            return cotangent.at[pl.ds(pl.multiple_of(at, quarter), quarter), pl.ds(h * half, half)]

        here.append(pltpu.make_async_copy(above(at_core), spot, local_sem.at[11 + h]))
        there.append(wires.make(above(1 - at_core), spot, core=1 - at_core))

    local = lax.rem(at_z, 2)
    for h in range(2):
        source = times.at[local, :, pl.ds(h * half, half)]
        spot = time_row.at[:, pl.ds(pl.multiple_of(flipped(at_x, h) * half, half), half)]
        here.append(pltpu.make_async_copy(source, spot, local_sem.at[13 + h]))
        there.append(wires.make(source, spot, core=1 - at_core))
    for r in range(4):
        spot = ids_row.at[:, pl.ds(r * quarter, quarter)]

        def stretch(core):
            at = flipped(core, r // 2) * 2 + flipped(at_y, r % 2)
            return ids.at[local, :, pl.ds(pl.multiple_of(at * quarter, quarter), quarter)]

        here.append(pltpu.make_async_copy(stretch(at_core), spot, local_sem.at[15 + r]))
        there.append(wires.make(stretch(1 - at_core), spot, core=1 - at_core))

    @pl.when(holds)
    def _():
        for near, far in zip(here, there):
            near.start()
            far.start()

    for at in range(3):
        kept[at].wait()
        lent[at].wait_recv()
        relay.begin(at)
        if at == 0:
            relay.cross(0, 0).start()

    @pl.when(holds)
    def _():
        for near in here:
            near.wait()

    @pl.when(jnp.logical_not(holds))
    def _():
        for far in there:
            far.wait_recv()

    ids_col[...] = jnp.transpose(jnp.broadcast_to(ids_row[...], (8, length)))[:, 0:1]

    def embed(rows):
        emb[rows, :] = (tok[rows, :].astype(f32) + time_row[...]).astype(low)

    row_loop(length, 32, embed)

    def small(s, side):
        size = half // 2 + TILE
        return (
            w_head[s, side, half // 2 : size, :].astype(f32)
            + w_head[s, side, size + half // 2 : 2 * size, :].astype(f32)
        )

    for turn in range(zs):
        s = relay.order[turn]
        if turn + 1 < zs:
            relay.arrive(0, turn + 1)
        if turn == 2:
            relay.cross(1, 0).start()
        relay.cross(0, s).wait_recv()
        bias = (small(s, 0) + small(s, 1))[0:1, :in_size]
        size = half // 2 + TILE

        def project(rows):
            total = bias
            for side in range(2):
                for core in range(2):
                    at = side * half + core * (half // 2)
                    total = total + dot_f32(
                        emb[rows, at : at + half // 2],
                        w_head[s, side, core * size : core * size + half // 2, :],
                    )[:, :in_size]
            proj[s, rows, :] = total.astype(low)

        row_loop(length, quarter, project)
        keys = proj[s, :, head_size : 2 * head_size]
        values = proj[s, :, 2 * head_size : in_size]

        def attend(rows):
            queries = proj[s, rows, 0:head_size] * jnp.bfloat16(head_size**-0.5)
            scores = dot_f32(queries, keys, ROW_PAIR)
            scores = jnp.where(ids_col[rows, :] == ids_row[...], scores, -1e30)
            highest = jnp.max(scores, axis=1, keepdims=True)
            exponent = jnp.exp(scores - highest)
            totals = jnp.sum(exponent, axis=1, keepdims=True)
            probability = (exponent * (1.0 / totals)).astype(low)
            ctx[s, rows, :] = dot_f32(probability, values).astype(low)

        row_loop(length, quarter, attend)

    for side in range(2):
        tile = small(0, side)
        for k in range(6):
            vecs[k : k + 1, side * half : side * half + half // 2] = tile[2 + k : 3 + k, :]
            vecs[k : k + 1, side * half + half // 2 : (side + 1) * half] = tile[8 + k : 9 + k, :]

    relay.arrive(1, 1)
    relay.arrive(1, 2)
    size = half // 2 + TILE
    for s in range(zs):
        for side in range(2):
            for core in range(2):
                w_out[side, core * (half // 2) : (core + 1) * (half // 2), s * head_size : (s + 1) * head_size] = w_head[
                    s, side, core * size : core * size + half // 2, in_size:
                ]
    bufs = (send_c, recv_c, send_y, recv_y)

    def mixed_part(r, side):
        joined = jnp.concatenate([ctx[s, r * quarter : (r + 1) * quarter, :] for s in range(zs)], axis=1)
        return dot_f32(joined, w_out[side], ROW_PAIR)

    add_rows(wires, mixed_part, keep, acc, bufs, lambda: relay.arrive(1, 3))
    relay.cross(2, 0).start()
    relay.arrive(2, 1)

    def first_norm(rows):
        total = tok[rows, :].astype(f32) + time_row[...] + keep[rows, :] + vecs[2:3, :]
        normed, inverse = norm_stats(total)
        normed_one[rows, :] = normed
        inverse_one[rows, :] = inverse
        value = normed * vecs[0:1, :] + vecs[3:4, :]
        hidden[rows, :] = value
        hid[rows, :] = value.astype(low)

    row_loop(quarter, 32, first_norm)
    to_y, to_core, again = spread_rows(wires, hid, quarter)
    for s in range(zs):
        relay.cross(1, s).wait_recv()
    relay.arrive(2, 2)

    def up(r):
        rows = pl.ds(r * quarter, quarter)

        def one(s):
            lanes = pl.ds(pl.multiple_of(s * (half // 2), half // 2), half // 2)
            shift = (small(s, 0) + small(s, 1))[1:2, :]
            value = dot_f32(hid[rows, 0:half], w_up[s, 0]) + dot_f32(hid[rows, half:], w_up[s, 1]) + shift
            pre[rows, lanes] = value
            act[rows, lanes] = gelu_value(value).astype(low)

        block_loop(zs, one)

    up(0)
    to_core.wait_recv()
    up(2)
    relay.arrive(2, 3)
    to_y.wait_recv()
    again.start()
    up(1)
    again.wait_recv()
    up(3)
    for s in range(zs):
        relay.cross(2, s).wait_recv()

    def down_part(r, side):
        rows = pl.ds(r * quarter, quarter)
        total = dot_f32(act[rows, 0 : half // 2], w_down[0, side], ROW_PAIR)
        for s in range(1, zs):
            total = total + dot_f32(act[rows, s * (half // 2) : (s + 1) * (half // 2)], w_down[s, side], ROW_PAIR)
        return total

    add_rows(wires, down_part, keep, acc, bufs)

    def second(rows):
        hidden[rows, :] += keep[rows, :] + vecs[4:5, :]

    row_loop(quarter, 32, second)

    def finish():
        for at in range(3):
            lent[at].wait_send()
        relay.finish()

        @pl.when(holds)
        def _():
            for far in there:
                far.wait_send()

        for member in (to_y, to_core, again):
            member.wait_send()

    return finish


def plane_sum(wires, value, slots):
    at_x, at_core, at_z, at_y = spots()
    own = at_core * 4 + at_z
    sent = []
    for step in range(8):
        core, turned = step // 4, step % 4
        if step == 0:
            slots[own] = value[...]
            continue
        sent.append(
            wires.make(
                value,
                slots.at[own],
                core=flipped(at_core, core),
                z=lax.rem(at_z + turned, 4),
            )
        )
        sent[-1].start()
    return sent


def plane_total(sent, slots):
    for member in sent:
        member.wait_recv()
    total = slots[0]
    for at in range(1, 8):
        total = total + slots[at]
    return total


class Outlet:
    def __init__(self, own, result, sends, receives, y_sends, y_receives, local):
        self.own, self.result, self.local = own, result, local
        self.sends, self.receives = sends, receives
        self.y_sends, self.y_receives = y_sends, y_receives
        self.at_x, self.at_core, self.at_z, self.at_y = spots()
        self.quarter = own.shape[0]

    def spot(self, place, core, at_y):
        row = (place * 4 + core * 2 + at_y) * self.quarter
        return self.result.at[pl.ds(pl.multiple_of(row, self.quarter), self.quarter)]

    def copy(self, step):
        at = 2 * step + self.at_core
        return pltpu.make_async_remote_copy(
            src_ref=self.own,
            dst_ref=self.spot(lax.rem(self.at_z, 2), self.at_core, self.at_y),
            send_sem=self.sends.at[at],
            recv_sem=self.receives.at[at],
            device_id={"core": lax.div(self.at_z, 2), "z": lax.rem(self.at_z + step, 4)},
            device_id_type=MESH_ID,
        )

    def stay(self):
        return pltpu.make_async_copy(
            self.own, self.spot(lax.rem(self.at_z, 2), self.at_core, self.at_y), self.local
        )

    def start(self):
        home = self.at_core == lax.div(self.at_z, 2)

        @pl.when(home)
        def _():
            self.stay().start()

        @pl.when(jnp.logical_not(home))
        def _():
            self.copy(0).start()

        for step in (1, 3, 2):
            self.copy(step).start()

    def across(self, place, core):
        spot = self.spot(place, core, self.at_y)
        at = place * 2 + core
        return pltpu.make_async_remote_copy(
            src_ref=spot,
            dst_ref=spot,
            send_sem=self.y_sends.at[at],
            recv_sem=self.y_receives.at[at],
            device_id={"y": 1 - self.at_y},
            device_id_type=MESH_ID,
        )

    def forward(self, place, core):
        source = 2 * self.at_core + place
        step = lax.rem(self.at_z - source + 4, 4)
        own = jnp.logical_and(step == 0, self.at_core == core)

        @pl.when(own)
        def _():
            self.stay().wait()

        @pl.when(jnp.logical_not(own))
        def _():
            spot = self.spot(place, core, self.at_y)
            at = 2 * step + core
            pltpu.make_async_remote_copy(
                src_ref=spot,
                dst_ref=spot,
                send_sem=self.sends.at[at],
                recv_sem=self.receives.at[at],
                device_id={"y": 1 - self.at_y},
                device_id_type=MESH_ID,
            ).wait_recv()

        self.across(place, core).start()

    def finish(self):
        home = self.at_core == lax.div(self.at_z, 2)
        for place in range(2):
            for core in range(2):
                self.across(place, core).wait()

        @pl.when(jnp.logical_not(home))
        def _():
            self.copy(0).wait_send()

        for step in range(1, 4):
            self.copy(step).wait_send()


class Chain(Outlet):
    def leave(self, rise, send):
        return pltpu.make_async_remote_copy(
            src_ref=self.own,
            dst_ref=self.spot(lax.rem(self.at_z, 2), self.at_core, self.at_y),
            send_sem=self.sends.at[send],
            recv_sem=self.receives.at[lax.rem(self.at_z, 2) * 2 + self.at_core],
            device_id={"core": lax.div(self.at_z, 2), "z": self.at_z + rise},
            device_id_type=MESH_ID,
        )

    def leaving(self, act):
        apart = jnp.logical_not(self.at_core == lax.div(self.at_z, 2))
        for rise, send, inside in ((1, 1, self.at_z < 3), (-1, 2, self.at_z > 0), (0, 0, apart)):

            @pl.when(inside)
            def _():
                act(self.leave(rise, send))

    def start(self):
        @pl.when(self.at_core == lax.div(self.at_z, 2))
        def _():
            self.stay().start()

        self.leaving(lambda copy: copy.start())

    def hop(self, place, core, rise):
        spot = self.spot(place, core, self.at_y)
        at = place * 2 + core
        return pltpu.make_async_remote_copy(
            src_ref=spot,
            dst_ref=spot,
            send_sem=self.sends.at[4 + at],
            recv_sem=self.receives.at[at],
            device_id={"z": self.at_z + rise},
            device_id_type=MESH_ID,
        )

    def hops(self, place, core, act):
        source = 2 * self.at_core + place
        for rise, inside in (
            (1, jnp.logical_and(source < self.at_z, self.at_z < 3)),
            (-1, jnp.logical_and(source > self.at_z, self.at_z > 0)),
        ):

            @pl.when(inside)
            def _():
                act(self.hop(place, core, rise))

    def forward(self, place, core):
        own = jnp.logical_and(2 * self.at_core + place == self.at_z, self.at_core == core)

        @pl.when(own)
        def _():
            self.stay().wait()

        @pl.when(jnp.logical_not(own))
        def _():
            self.hop(place, core, 0).wait_recv()

        self.hops(place, core, lambda copy: copy.start())
        self.across(place, core).start()

    def finish(self):
        self.leaving(lambda copy: copy.wait_send())
        for place in range(2):
            for core in range(2):
                self.hops(place, core, lambda copy: copy.wait_send())
                self.across(place, core).wait()


def back_part_of(
    wires, w_head, w_up, w_down, emb, proj, ctx, w_out, hid, pre, act, normed_one, inverse_one, summed, vecs, upstream,
    ids_col, ids_row,
    block_out, input_out, res_head, res_up, res_down, res_tile, feature, norm,
    two, slope, one, grad_ctx, grad_proj, two_full, one_full, send_c, recv_c, send_y, recv_y, keep, acc,
    near_head, far_head, got_head, came_head, near_up, far_up, got_up, came_up, near_down, far_down, got_down, came_down,
    out_one, out_two, feat, slots, scalar, scalar_slots, key_sum, value_sum, y_feat, x_feat, y_scalar, x_scalar,
    out_sem, local_sem,
):
    at_x, at_core, at_z, at_y = spots()
    low, f32 = jnp.bfloat16, jnp.float32
    length, width = emb.shape
    quarter, half = length // 4, width // 2
    zs = w_head.shape[0]
    block = half // 2
    head_size = ctx.shape[2]
    in_size = 3 * head_size
    feat[...] = jnp.zeros_like(feat)

    def lanes(h):
        return pl.ds(pl.multiple_of(flipped(at_x, h) * half, half), half)

    def second_norm(rows):
        normed, inverse = norm_stats(summed[rows, :])
        gain, shift = vecs[1:2, :], vecs[5:6, :]
        value = (normed * gain + shift).astype(low)
        for h in range(2):
            out_one[rows, lanes(h)] = value[:, h * half : (h + 1) * half]
        above = upstream[rows, :].astype(f32)
        grad = norm_back(above * gain, normed, inverse)
        feat[1:2, :] += jnp.sum(above * normed, axis=0, keepdims=True)
        feat[5:6, :] += jnp.sum(above, axis=0, keepdims=True)
        feat[4:5, :] += jnp.sum(grad, axis=0, keepdims=True)
        two_full[rows, :] = grad
        two[rows, :] = grad.astype(low)

    row_loop(quarter, 32, second_norm)
    to_y, to_core, again = spread_rows(wires, two, quarter)
    outlets = [
        kind(own, result, *[out_sem.at[n, k] for k in range(4)], local_sem.at[n])
        for n, (kind, own, result) in enumerate(((Outlet, out_one, block_out), (Chain, out_two, input_out)))
    ]
    outlets[0].start()

    def slopes(r):
        rows = pl.ds(r * quarter, quarter)

        def inner(s):
            units = pl.ds(pl.multiple_of(s * block, block), block)
            value = dot_f32(two[rows, 0:half], w_down[s, 0]) + dot_f32(two[rows, half:], w_down[s, 1])
            slope[rows, units] = (value * gelu_slope(pre[rows, units])).astype(low)

        block_loop(zs, inner)

    slopes(0)
    to_core.wait_recv()
    slopes(2)
    apart = (at_core - lax.div(at_z, 2)) * (at_core - lax.div(at_z, 2))
    close = (1 - apart) * lax.rem(at_z, 2) + apart * (1 - at_core)
    to_y.wait_recv()
    again.start()
    slopes(1)
    again.wait_recv()
    slopes(3)
    ended = [to_y, to_core, again]

    def group(near, far, got, came):
        crossed = [wires.make(far.at[s], got.at[s], x=1 - at_x) for s in range(zs)]
        turned = [
            wires.make(far.at[s], came.at[s - 1], z=lax.rem(at_z + zs - s, zs)) for s in range(1, zs)
        ]
        return near, far, got, crossed, turned, came

    groups = {
        "head": group(near_head, far_head, got_head, came_head),
        "up": group(near_up, far_up, got_up, came_up),
        "down": group(near_down, far_down, got_down, came_down),
    }

    def weight_grads(name, left, right):
        near, far, got, crossed, turned, came = groups[name]

        for s in range(zs):
            far[s] = dot_f32(left[:, half:], right[:, s * block : (s + 1) * block], COL_PAIR).astype(low)
            crossed[s].start()

        def inner(s):
            units = pl.ds(pl.multiple_of(s * block, block), block)
            near[s] = dot_f32(left[:, 0:half], right[:, units], COL_PAIR)

        block_loop(zs, inner)

    def turn_blocks(name):
        near, far, got, crossed, turned, came = groups[name]
        size = near.shape[1]
        for s in range(zs):
            crossed[s].wait()

        def inner(s):
            def add(rows):
                near[s, rows, :] += got[s, rows, :].astype(f32)
                far[s, rows, :] = near[s, rows, :].astype(low)

            row_loop(size, 16, add)

        block_loop(zs, inner)

    def start_turns(name):
        for member in groups[name][4]:
            member.start()

    def settle(name):
        near, far, got, crossed, turned, came = groups[name]
        size = near.shape[1]
        for member in turned:
            member.wait()

        def add(rows):
            total = near[0, rows, :]
            for s in range(1, zs):
                total = total + came[s - 1, rows, :].astype(f32)
            near[0, rows, :] = total

        row_loop(size, 16, add)

    bufs = (send_c, recv_c, send_y, recv_y)

    def back_part(r, side):
        rows = pl.ds(r * quarter, quarter)
        total = dot_f32(slope[rows, 0:block], w_up[0, side], ROW_PAIR)
        for s in range(1, zs):
            total = total + dot_f32(slope[rows, s * block : (s + 1) * block], w_up[s, side], ROW_PAIR)
        return total

    add_rows(wires, back_part, keep, acc, bufs, lambda: weight_grads("down", two, act))

    def first_norm(rows):
        grad_hidden = keep[rows, :] + two_full[rows, :]
        normed = normed_one[rows, :]
        grad = norm_back(grad_hidden * vecs[0:1, :], normed, inverse_one[rows, :])
        feat[0:1, :] += jnp.sum(grad_hidden * normed, axis=0, keepdims=True)
        feat[3:4, :] += jnp.sum(grad_hidden, axis=0, keepdims=True)
        feat[2:3, :] += jnp.sum(grad, axis=0, keepdims=True)
        one_full[rows, :] = grad
        one[rows, :] = grad.astype(low)

    row_loop(quarter, 32, first_norm)
    to_y, to_core, again = spread_rows(wires, one, quarter)
    ended += [to_y, to_core, again]
    feat_sent = plane_sum(wires, feat, slots)
    weight_grads("up", hid, slope)

    def contexts(r):
        rows = pl.ds(r * quarter, quarter)
        value = dot_f32(one[rows, 0:half], w_out[0]) + dot_f32(one[rows, half:], w_out[1])
        value = value.astype(low)
        for s in range(zs):
            grad_ctx[s, rows, :] = value[:, s * head_size : (s + 1) * head_size]

    contexts(0)
    to_core.wait_recv()
    contexts(2)
    to_y.wait_recv()
    again.start()
    contexts(1)
    turn_blocks("down")
    start_turns("down")
    again.wait_recv()
    contexts(3)
    outlets[0].forward(close, 0)
    outlets[0].forward(close, 1)
    outlets[0].forward(1 - close, 0)
    outlets[0].forward(1 - close, 1)
    scale = head_size**-0.5

    def attend(s):
        keys = proj[s, :, head_size : 2 * head_size]
        values = proj[s, :, 2 * head_size : in_size]
        key_sum[...] = jnp.zeros_like(key_sum)
        value_sum[...] = jnp.zeros_like(value_sum)

        def inner(rows):
            queries = proj[s, rows, 0:head_size] * low(scale)
            grads = grad_ctx[s, rows, :]
            scores = dot_f32(keys, queries, ROW_PAIR)
            scores = jnp.where(ids_col[...] == ids_row[0:1, rows], scores, -1e30)
            highest = jnp.max(scores, axis=0, keepdims=True)
            exponent = jnp.exp(scores - highest)
            probability = exponent * (1.0 / jnp.sum(exponent, axis=0, keepdims=True))
            grad_prob = dot_f32(values, grads, ROW_PAIR)
            weighted = jnp.sum(probability * grad_prob, axis=0, keepdims=True)
            grad_score = (probability * (grad_prob - weighted)).astype(low)
            value_sum[...] += dot_f32(probability.astype(low), grads)
            key_sum[...] += dot_f32(grad_score, queries)
            grad_query = dot_f32(grad_score, keys, COL_PAIR)
            grad_proj[s, rows, 0:head_size] = (grad_query * scale).astype(low)

        row_loop(length, quarter, inner)
        grad_proj[s, :, head_size : 2 * head_size] = key_sum[...].astype(low)
        grad_proj[s, :, 2 * head_size : in_size] = value_sum[...].astype(low)

    block_loop(2, attend)
    turn_blocks("up")
    start_turns("up")
    block_loop(2, lambda s: attend(s + 2))

    size = block + TILE

    def input_part(r, side):
        rows = pl.ds(r * quarter, quarter)
        parts = []
        for core in range(2):
            total = None
            for s in range(zs):
                value = dot_f32(
                    grad_proj[s, rows, :], w_head[s, side, core * size : core * size + block, 0:in_size], ROW_PAIR
                )
                total = value if total is None else total + value
            parts.append(total)
        return jnp.concatenate(parts, axis=1)

    near, far, got, crossed, turned, came = groups["head"]

    def head_far():
        for s in range(zs):
            far[s, 0:half, 0:in_size] = dot_f32(emb[:, half:], grad_proj[s], COL_PAIR).astype(low)
            far[s, 0:half, in_size:] = dot_f32(one[:, half:], ctx[s], COL_PAIR).astype(low)
            sums = jnp.sum(grad_proj[s].astype(f32), axis=0, keepdims=True)
            near[s, half:, :] = jnp.zeros((TILE, near.shape[2]), f32)
            near[s, half : half + 1, 0:head_size] = sums[:, 0:head_size]
            near[s, half : half + 1, 2 * head_size : in_size] = sums[:, 2 * head_size :]
            near[s, half + 1 : half + 2, :] = jnp.sum(
                slope[:, s * block : (s + 1) * block].astype(f32), axis=0, keepdims=True
            )
            far[s, half:, :] = near[s, half:, :].astype(low)
            crossed[s].start()

    add_rows(wires, input_part, keep, acc, bufs, head_far)

    def leave(rows):
        value = (keep[rows, :] + one_full[rows, :]).astype(low)
        for h in range(2):
            out_two[rows, lanes(h)] = value[:, h * half : (h + 1) * half]

    row_loop(quarter, 32, leave)
    outlets[1].start()

    def head_near(s):
        near[s, 0:half, 0:in_size] = dot_f32(emb[:, 0:half], grad_proj[s], COL_PAIR)
        near[s, 0:half, in_size:] = dot_f32(one[:, 0:half], ctx[s], COL_PAIR)

    block_loop(zs, head_near)
    turn_blocks("head")
    edge = at_core * lax.div(at_z, 3) + (1 - at_core) * (1 - lax.div(3 - at_z, 3))
    outlets[1].forward(edge, 0)
    outlets[1].forward(edge, 1)
    start_turns("head")

    acc[0:8, :] = plane_total(feat_sent, slots)
    y_copy = wires.make(acc.at[pl.ds(0, 8)], y_feat, y=1 - at_y)
    y_copy.start()
    y_copy.wait_recv()
    feat_all = acc[0:8, :] + y_feat[...]
    keep[0:8, :] = feat_all
    x_copy = wires.make(keep.at[pl.ds(0, 8), pl.ds(half, half)], x_feat, x=1 - at_x)
    x_copy.start()
    x_copy.wait_recv()
    feature[...] = feat_all[:, 0:half] + x_feat[...]

    settle("down")
    settle("up")
    outlets[1].forward(1 - edge, 0)
    outlets[1].forward(1 - edge, 1)
    settle("head")

    backs = []
    results = (("head", res_head), ("up", res_up), ("down", res_down))
    for at, (name, result) in enumerate(results):
        near = groups[name][0]
        mine = near.at[0, pl.ds(pl.multiple_of(at_core * block, block), block)]
        other = near.at[0, pl.ds(pl.multiple_of((1 - at_core) * block, block), block)]
        place = result.at[at_core]
        if name != "head":
            place = result.at[:, pl.ds(pl.multiple_of(at_core * block, block), block)]
        local = pltpu.make_async_copy(mine, place, local_sem.at[2 + at])
        local.start()
        remote = wires.make(other, place, core=1 - at_core)
        remote.start()
        backs += [local, remote]
    tile = near_head.at[0, pl.ds(half, TILE)]
    local = pltpu.make_async_copy(tile, res_tile.at[at_core], local_sem.at[5])
    remote = wires.make(tile, res_tile.at[at_core], core=1 - at_core)
    local.start()
    remote.start()
    backs += [local, remote]

    acc[8:16, 0:block] = jnp.zeros((8, block), f32)
    for name, _ in results:
        near = groups[name][0]

        def add(rows):
            value = near[0, rows, :]
            acc[8:16, 0:block] += value * value

        row_loop(half, 8, add)
    value = near_head[0, half : half + 8, :]
    acc[8:16, 0:block] += 0.5 * value * value
    shared = feature[...] * feature[...] * (1.0 / 16.0)
    shared = shared[:, 0:block] + shared[:, block:]
    summed_squares = jnp.sum(acc[8:16, 0:block] + shared)
    scalar[...] = jnp.broadcast_to(summed_squares, scalar.shape)
    scalar_sent = plane_sum(wires, scalar, scalar_slots)
    value = plane_total(scalar_sent, scalar_slots)
    norm[...] = value
    y_two = wires.make(norm, y_scalar, y=1 - at_y)
    y_two.start()
    y_two.wait()
    value = value + y_scalar[...]
    send_scalar = scalar_slots.at[8]
    send_scalar[...] = value
    x_two = wires.make(send_scalar, x_scalar, x=1 - at_x)
    x_two.start()
    x_two.wait()
    norm[...] = value + x_scalar[...]

    for member in ended + feat_sent + scalar_sent + [y_copy, x_copy]:
        member.wait_send()
    for member in backs:
        member.wait()
    for outlet in outlets:
        outlet.finish()


def layer_kernel(
    in_full, out_full, up_full, down_full, tiles, tokens, cotangent, times, ids,
    block_out, input_out, res_head, res_up, res_down, res_tile, feature, norm,
    head_piece, up_piece, down_piece, time_row, ids_col, ids_row,
    w_head, w_up, w_down, emb, proj, ctx, w_out, hid, pre, act, normed_one, inverse_one, hidden, vecs, upstream, tok,
    *rest,
):
    mids, gather_sems = rest[:-9], rest[-4:]
    send_sem, recv_sem, out_sem, local_sem, front_sem = rest[-9:-4]
    shared = mids[7:13]
    wires = Wires(send_sem, recv_sem)
    greet(True)
    finish = front_part(
        wires, in_full, out_full, up_full, down_full, tiles, tokens, cotangent, times, ids,
        head_piece, up_piece, down_piece, time_row, ids_col, ids_row,
        w_head, w_up, w_down, emb, proj, ctx, w_out, hid, pre, act, normed_one, inverse_one, hidden, vecs, upstream,
        tok, *shared, front_sem, gather_sems,
    )
    quarter = hidden.shape[0]
    out_one, out_two = tok.at[pl.ds(2 * quarter, quarter)], tok.at[pl.ds(3 * quarter, quarter)]
    back_part_of(
        wires, w_head, w_up, w_down, emb, proj, ctx, w_out, hid, pre, act, normed_one, inverse_one, hidden, vecs,
        upstream, ids_col, ids_row,
        block_out, input_out, res_head, res_up, res_down, res_tile, feature, norm,
        *mids[:25], out_one, out_two, *mids[25:], out_sem, local_sem,
    )
    finish()


def run_layer(weights, tiles, tokens, cotangent, times, ids, head_size):
    low, f32 = jnp.bfloat16, jnp.float32
    length, width = ids.shape[2], tokens.shape[1]
    zs = 4
    quarter, half, block = length // 4, width // 2, width // 4
    units = weights[2].shape[1] // 2
    vmem = pl.BlockSpec(memory_space=pltpu.VMEM)
    anywhere = pl.BlockSpec(memory_space=pl.ANY)
    shape = jax.ShapeDtypeStruct
    kept = [
        ((2, block + TILE, 4 * head_size), low),
        ((2, block, units), low),
        ((2, block, units), low),
        ((1, width), f32),
        ((length, 1), f32),
        ((1, length), f32),
        ((zs, 2, half + 2 * TILE, 4 * head_size), low),
        ((zs, 2, half, units), low),
        ((zs, 2, half, units), low),
        ((length, width), low),
        ((zs, length, 3 * head_size), low),
        ((zs, length, head_size), low),
        ((2, half, zs * head_size), low),
        ((length, width), low),
        ((length, zs * units), f32),
        ((length, zs * units), low),
        ((quarter, width), f32),
        ((quarter, 1), f32),
        ((quarter, width), f32),
        ((8, width), f32),
        ((quarter, width), low),
        ((length, width), low),
    ]

    def group(size):
        return [((n, size, block), d) for n, d in ((zs, f32), (zs, low), (zs, low), (zs - 1, low))]

    worked = [
        ((length, width), low),
        ((length, width), low),
        ((length, width), low),
        ((zs, length, head_size), low),
        ((zs, length, 3 * head_size), low),
        ((quarter, width), f32),
        ((quarter, width), f32),
        ((2, quarter, width), low),
        ((2, quarter, width), low),
        ((quarter, width), low),
        ((quarter, width), low),
        ((quarter, width), f32),
        ((quarter, width), f32),
        *group(half + TILE),
        *group(half),
        *group(half),
        ((8, width), f32),
        ((8, 8, width), f32),
        ((8, 128), f32),
        ((9, 8, 128), f32),
        ((length, head_size), f32),
        ((length, head_size), f32),
        ((8, width), f32),
        ((8, half), f32),
        ((8, 128), f32),
        ((8, 128), f32),
    ]
    return pl.pallas_call(
        layer_kernel,
        out_shape=[
            shape(tokens.shape, low),
            shape(tokens.shape, low),
            shape((2, block, block), f32),
            shape((block, 2 * block), f32),
            shape((block, 2 * block), f32),
            shape((2, TILE, block), f32),
            shape((8, half), f32),
            shape((8, 128), f32),
        ],
        in_specs=[vmem] * 5 + [anywhere] * 4,
        out_specs=[anywhere] * 2 + [vmem] * 6,
        scratch_shapes=[pltpu.VMEM(*member) for member in kept + worked]
        + [
            pltpu.SemaphoreType.DMA((128,)),
            pltpu.SemaphoreType.DMA((128,)),
            pltpu.SemaphoreType.DMA((2, 4, 8)),
            pltpu.SemaphoreType.DMA((6,)),
            pltpu.SemaphoreType.DMA((20,)),
            pltpu.SemaphoreType.DMA((3, 6)),
            pltpu.SemaphoreType.DMA((3, 4)),
            pltpu.SemaphoreType.DMA((3, 4)),
            pltpu.SemaphoreType.DMA((3, 4)),
        ],
        compiler_params=pltpu.CompilerParams(
            collective_id=0, has_side_effects=True, vmem_limit_bytes=67000000
        ),
        name="layer",
    )(*weights, tiles, tokens, cotangent, times, ids)


def on_grid(*arguments):
    tokens, time_embed, segment_ids, cotangent = arguments[:4]
    masters, moments, squares = arguments[4::3], arguments[5::3], arguments[6::3]
    input_weight, output_weight, upward_weight, downward_weight = masters[:4]
    head_bias, hidden_bias, norm_gains, branch_biases = masters[4:]
    at_x, at_core = lax.axis_index("x"), lax.axis_index("core")
    at_z, at_y = lax.axis_index("z"), lax.axis_index("y")
    first_core, first_x = at_core == 0, at_x == 0
    swapped = at_x == 1
    low = jnp.bfloat16
    f32 = jnp.float32
    length = segment_ids.shape[1]
    head_size = head_bias.shape[0] * 4 // 2
    zs = 4
    place = at_core * 2 + at_y
    quarter = length // 4

    rows = input_weight.shape[0]
    wide = upward_weight.shape[1] // 2
    packed = 4 * head_size
    small_rows = head_bias.shape[0]

    position = at_x * 2 + at_core
    vectors = jnp.concatenate([norm_gains, branch_biases], axis=1).T
    vectors = lax.dynamic_update_slice(
        jnp.zeros((TILE, rows), f32), vectors, (2 + 6 * at_core, 0)
    )

    def small_tile(half):
        tile = lax.dynamic_update_slice(
            vectors, head_bias[:, half][None], (0, at_x * 2 * head_size + at_core * small_rows)
        )
        units = lax.dynamic_update_slice(
            jnp.zeros((2, 4 * small_rows), f32),
            hidden_bias[:, 2 * half : 2 * half + 2].T,
            (0, position * small_rows),
        )
        return lax.dynamic_update_slice(tile, units.reshape(1, -1), (1, 0))

    seqs = segment_ids.shape[0]
    times = time_embed.astype(f32).reshape(seqs, 1, -1)
    ids = segment_ids.astype(f32).reshape(seqs, 1, length)
    small = jnp.stack([small_tile(0), small_tile(1)])
    block_output, input_grad, res_head, sent_up, sent_down, tiles, feature, norm = run_layer(
        masters[:4], small, tokens, cotangent, times, ids, head_size
    )
    in_size = 3 * head_size
    sent_in = jnp.concatenate([res_head[0, :, :in_size], res_head[1, :, :in_size]], axis=1)
    sent_out = jnp.concatenate([res_head[0, :, in_size:], res_head[1, :, in_size:]], axis=1)
    sent_head = lax.dynamic_slice(
        tiles[:, 0], (0, at_x * 2 * head_size + at_core * small_rows), (2, small_rows)
    ).T
    units = lax.dynamic_slice(
        tiles[:, 1].reshape(4, 4 * small_rows), (0, position * small_rows), (4, small_rows)
    )
    sent_unit = units.T
    feature = lax.dynamic_slice(feature, (0, at_core * rows), (8, rows))
    sent_gains, sent_shifts = feature[0:2].T, feature[2:6].T
    grad_norm = jnp.sqrt(norm[0, 0])
    gradients = (sent_in, sent_out, sent_up, sent_down, sent_head, sent_unit, sent_gains, sent_shifts)
    factor = CLIP / jnp.maximum(grad_norm, CLIP)
    results = [block_output, input_grad.astype(f32), grad_norm.reshape(1)]
    for position in range(8):
        results += adam_update(
            masters[position],
            moments[position],
            squares[position],
            gradients[position] * factor,
            RATES[position],
            DECAYS[position],
        )
    return tuple(results)


def solution(mesh):
    plain = mesh.shape["rows"] != 4 or mesh.shape["tp"] != 8
    if plain:
        rows, tp = "rows", "tp"
        grid, work = mesh, on_device
    else:
        rows, tp = ("x", "core"), ("z", "y")
        grid = Mesh(mesh.devices.reshape(2, 2, 4, 2), ("x", "core", "z", "y"))
        work = on_grid
    narrow, split = P(rows, None), P(rows, tp)
    return jax.shard_map(
        work,
        mesh=grid,
        in_specs=(narrow,) * 4 + (split,) * 18 + (narrow,) * 6,
        out_specs=(narrow, narrow, P()) + (split,) * 18 + (narrow,) * 6,
        check_vma=False,
    )
```
